32 devices in a mesh: dp: 4 (over y, core), seq: 8 (over z, x).
Axes of the slice: x: 2, y: 2, z: 4, core: 2. Of those that a mesh axis runs over, the one named last changes fastest.
Arguments:
- layer_input: bfloat16 [2, 4, 1024, 768], P(None, 'dp', 'seq'), may hold values from -6 to 6
- cotangent: bfloat16 [2, 4, 1024, 768], P(None, 'dp', 'seq'), may hold values from -6 to 6
- w_joined: bfloat16 [768, 2304], P(('dp', 'seq')), may hold values from -3 to 3
- w_output: bfloat16 [768, 768], P(('dp', 'seq')), may hold values from -2.5 to 2.5
- w_expand: bfloat16 [768, 2304], P(('dp', 'seq')), may hold values from -0.21875 to 0.21875
- w_contract: bfloat16 [1152, 768], P(None, ('dp', 'seq')), may hold values from -0.1875 to 0.1875
- gain_one: bfloat16 [768], P(('dp', 'seq')), may hold values from 0.5 to 1.5
- gain_two: bfloat16 [768], P(('dp', 'seq')), may hold values from 0.5 to 1.5
Outputs:
- layer_output: bfloat16 [2, 4, 1024, 768], P(None, 'dp', 'seq')
- input_grad: bfloat16 [2, 4, 1024, 768], P(None, 'dp', 'seq')
- w_joined_grad: float32 [768, 2304], P(('dp', 'seq'))
- w_output_grad: float32 [768, 768], P(('dp', 'seq'))
- w_expand_grad: float32 [768, 2304], P(('dp', 'seq'))
- w_contract_grad: float32 [1152, 768], P(None, ('dp', 'seq'))
- gain_one_grad: float32 [768], P(('dp', 'seq'))
- gain_two_grad: float32 [768], P(('dp', 'seq'))
The draws below stay inside these ranges and needn't reach their ends.
All inputs are finite; a program needn't handle non-finite values.
Results may differ from the reference program's by a relative error of at most 0.02.
The reference program's roundings to bfloat16 on the way (of `normed_one`, `attended`, `normed_two`, `mixed`, `d_expanded`, `d_attended`, `d_scores` and `d_joined`) count: a program that leaves them out, or rounds other values in their place, can miss the bound.
Values may be sent and summed in bfloat16 or wider, within the bound.
A program may use at most 128 MiB of HBM per device.

```python
import math
import jax
import jax.numpy as jnp
from jax import lax

D = 768
HEADS = 12
HEAD_DIM = 64
FF = 1152
WINDOW = 128
MB = 2
BATCH = 4
LENGTH = 1024


def draw_w_joined(key, part):
    base = jax.random.truncated_normal(jax.random.fold_in(key, 11), -4.0, 4.0, (D, 3 * D), jnp.float32) / math.sqrt(D)
    return base.astype(jnp.bfloat16)


def block_levels(key, dims, pieces, smallest, top_value):
    level = 1.0
    for dim, shards_of in pieces:
        steps = jax.random.uniform(jax.random.fold_in(jax.random.fold_in(key, 6), dim), (shards_of,), jnp.float32, smallest / len(pieces), top_value / len(pieces))
        level = level * jnp.repeat(jnp.exp(steps), dims[dim] // shards_of).reshape((-1,) + (1,) * (len(dims) - 1 - dim))
    return level


def scatter_about(key, dims, deviation, bound, pieces=(), kind=jnp.bfloat16):
    level = block_levels(key, dims, pieces, -0.22, 0.18) if pieces else 1.0
    entries = jax.random.normal(key, dims, jnp.float32) * deviation * level
    return jnp.minimum(jnp.maximum(entries, -bound), bound).astype(kind)


def setup_inputs(seed: int = 0) -> dict:
    splits = jax.random.split(jax.random.key(seed), 9)
    layer_input = scatter_about(splits[0], (MB, BATCH, LENGTH, D), 1.0, 6.0, ((1, 4), (2, 8)))
    cotangent = scatter_about(splits[1], (MB, BATCH, LENGTH, D), 1.0, 6.0, ((1, 4), (2, 8)))
    w_joined = draw_w_joined(jax.random.fold_in(splits[8], 71), 0)
    w_output = scatter_about(splits[3], (D, D), (D // 128) ** -0.5, 2.5, ((0, 32),))
    w_expand = scatter_about(splits[4], (D, 2 * FF), D ** -0.5, 0.21875, ((0, 32),))
    w_contract = scatter_about(splits[5], (FF, D), FF ** -0.5, 0.1875, ((1, 32),))
    gain_one = jnp.clip(1.0 + 0.1 * jax.random.normal(splits[6], (D,), jnp.float32), 0.5, 1.5).astype(jnp.bfloat16)
    gain_two = jnp.clip(1.0 + 0.1 * jax.random.normal(splits[7], (D,), jnp.float32), 0.5, 1.5).astype(jnp.bfloat16)
    return dict(layer_input=layer_input, cotangent=cotangent, w_joined=w_joined, w_output=w_output, w_expand=w_expand, w_contract=w_contract, gain_one=gain_one, gain_two=gain_two)


NORM_EPS = 1e-05
ROPE_BASE = 10000.0
MASK_FILL = -1e+30
SQRT_HALF = 0.7071067811865476
INV_ROOT_TAU = 0.3989422804014327

def norm_apply(values, gain):
    center = lax.optimization_barrier(jnp.mean(values, axis=-1, keepdims=True))
    shifted = values - center
    inv_std = lax.rsqrt(lax.optimization_barrier(jnp.mean(shifted * shifted, axis=-1, keepdims=True)) + NORM_EPS)
    normed = shifted * inv_std
    return (normed * gain.astype(jnp.float32), normed, inv_std)

def norm_back(upstream, normed, inv_std, gain):
    scaled = upstream * gain.astype(jnp.float32)
    inner = scaled - lax.optimization_barrier(jnp.mean(scaled, axis=-1, keepdims=True)) - normed * lax.optimization_barrier(jnp.mean(scaled * normed, axis=-1, keepdims=True))
    return (inv_std * inner, lax.optimization_barrier(jnp.sum(upstream * normed, axis=0)))

def gelu_slope(values):
    cumul = 0.5 * (1.0 + jax.scipy.special.erf(values * SQRT_HALF))
    return cumul + values * jnp.exp(-0.5 * values * values) * INV_ROOT_TAU

def rope_tables(positions, head_dim):
    half_dim = head_dim // 2
    freqs = ROPE_BASE ** (-jnp.arange(half_dim).astype(jnp.float32) * 2.0 / head_dim)
    angles = positions.astype(jnp.float32)[:, None] * freqs[None, :]
    return (jnp.cos(angles)[:, None, :], jnp.sin(angles)[:, None, :])

def rotate(values, cosine, sine):
    half_dim = values.shape[-1] // 2
    first = values[..., :half_dim]
    second = values[..., half_dim:]
    return jnp.concatenate([first * cosine - second * sine, second * cosine + first * sine], axis=-1)

def unrotate(values, cosine, sine):
    half_dim = values.shape[-1] // 2
    first = values[..., :half_dim]
    second = values[..., half_dim:]
    return jnp.concatenate([first * cosine + second * sine, second * cosine - first * sine], axis=-1)

def block_scores(block_index, q_rot, key_pad, qblock, half):
    start = block_index * qblock
    query_blk = lax.dynamic_slice_in_dim(q_rot, start, qblock, 0).astype(jnp.float32)
    key_blk = lax.dynamic_slice_in_dim(key_pad, start, qblock + 2 * half, 0).astype(jnp.float32)
    scores = jnp.einsum('qhd,khd->hqk', query_blk, key_blk) * q_rot.shape[-1] ** (-0.5)
    query_pos = start + jnp.arange(qblock, dtype=jnp.int32)[:, None]
    key_pos = start - half + jnp.arange(qblock + 2 * half, dtype=jnp.int32)[None, :]
    allowed = (jnp.abs(query_pos - key_pos) <= half) & (key_pos >= 0) & (key_pos < LENGTH)
    return (jnp.where(allowed[None], scores, MASK_FILL), query_blk, key_blk)

def spread_keys(blocks, half, qblock):
    count = blocks.shape[0]
    rest = blocks.shape[2:]
    extra = [(0, 0)] * len(rest)
    main_rows = blocks[:, :qblock].reshape((count * qblock,) + rest)
    tails = jnp.pad(blocks[:, qblock:], [(0, 0), (0, qblock - 2 * half)] + extra).reshape((count * qblock,) + rest)
    total = jnp.pad(main_rows, [(0, 2 * half)] + extra) + jnp.pad(tails, [(qblock, 0)] + extra)[:count * qblock + 2 * half]
    return total[half:half + count * qblock]

def one_sequence(source, upstream_half, weights):
    w_joined, w_output, w_expand, w_contract, gain_one, gain_two = weights
    half = WINDOW // 2
    qblock = min(512, LENGTH)
    blocks_count = LENGTH // qblock
    heads, head_dim = (HEADS, HEAD_DIM)
    width = D
    source32 = source.astype(jnp.float32)
    upstream = upstream_half.astype(jnp.float32)
    normed_f, norm_one, inv_one = norm_apply(source32, gain_one)
    normed_one = normed_f.astype(jnp.bfloat16)
    joined = jnp.dot(normed_one, w_joined, preferred_element_type=jnp.float32)
    cosine, sine = rope_tables(jnp.arange(LENGTH, dtype=jnp.int32), head_dim)
    q_rot = rotate(joined[:, :width].reshape(LENGTH, heads, head_dim), cosine, sine).astype(jnp.bfloat16)
    k_rot = rotate(joined[:, width:2 * width].reshape(LENGTH, heads, head_dim), cosine, sine).astype(jnp.bfloat16)
    v_half = joined[:, 2 * width:].reshape(LENGTH, heads, head_dim).astype(jnp.bfloat16)
    key_pad = jnp.pad(k_rot, ((half, half), (0, 0), (0, 0)))
    value_pad = jnp.pad(v_half, ((half, half), (0, 0), (0, 0)))

    def forward_block(block_index):
        scores, query_blk, key_blk = block_scores(block_index, q_rot, key_pad, qblock, half)
        row_max = lax.optimization_barrier(jnp.max(scores, axis=-1, keepdims=True))
        log_total = row_max + jnp.log(lax.optimization_barrier(jnp.sum(jnp.exp(scores - row_max), axis=-1, keepdims=True)))
        probs_half = jnp.exp(scores - log_total).astype(jnp.bfloat16)
        value_blk = lax.dynamic_slice_in_dim(value_pad, block_index * qblock, qblock + 2 * half, 0)
        output_blk = jnp.einsum('hqk,khd->qhd', probs_half.astype(jnp.float32), value_blk.astype(jnp.float32))
        return (output_blk.astype(jnp.bfloat16), log_total)
    block_ids = jnp.arange(blocks_count, dtype=jnp.int32)
    outputs, log_totals = lax.map(forward_block, block_ids)
    attended = outputs.reshape(LENGTH, width)
    resid = source32 + jnp.dot(attended, w_output, preferred_element_type=jnp.float32)
    normed_g, norm_two, inv_two = norm_apply(resid, gain_two)
    normed_two = normed_g.astype(jnp.bfloat16)
    expanded = jnp.dot(normed_two, w_expand, preferred_element_type=jnp.float32)
    pre_act = expanded[:, :FF]
    gate_part = expanded[:, FF:]
    activated = jax.nn.gelu(pre_act, approximate=False)
    mixed = (activated * gate_part).astype(jnp.bfloat16)
    layer_out = (resid + jnp.dot(mixed, w_contract, preferred_element_type=jnp.float32)).astype(jnp.bfloat16)
    contract_grad = jnp.dot(mixed.T, upstream_half, preferred_element_type=jnp.float32)
    d_mixed = jnp.dot(upstream_half, w_contract.T, preferred_element_type=jnp.float32)
    d_expanded = jnp.concatenate([d_mixed * gate_part * gelu_slope(pre_act), d_mixed * activated], axis=-1).astype(jnp.bfloat16)
    expand_grad = jnp.dot(normed_two.T, d_expanded, preferred_element_type=jnp.float32)
    d_normed_two = jnp.dot(d_expanded, w_expand.T, preferred_element_type=jnp.float32)
    d_resid_n, gain_two_grad = norm_back(d_normed_two, norm_two, inv_two, gain_two)
    d_resid = upstream + d_resid_n
    d_resid_half = d_resid.astype(jnp.bfloat16)
    output_grad = jnp.dot(attended.T, d_resid_half, preferred_element_type=jnp.float32)
    d_attended = jnp.dot(d_resid_half, w_output.T, preferred_element_type=jnp.float32).astype(jnp.bfloat16)
    d_attended = d_attended.reshape(LENGTH, heads, head_dim)

    def backward_block(block_index):
        scores, query_blk, key_blk = block_scores(block_index, q_rot, key_pad, qblock, half)
        log_total = log_totals[block_index]
        probs = jnp.exp(scores - log_total)
        probs_half = probs.astype(jnp.bfloat16).astype(jnp.float32)
        value_blk = lax.dynamic_slice_in_dim(value_pad, block_index * qblock, qblock + 2 * half, 0).astype(jnp.float32)
        d_out_blk = lax.dynamic_slice_in_dim(d_attended, block_index * qblock, qblock, 0).astype(jnp.float32)
        d_probs = jnp.einsum('qhd,khd->hqk', d_out_blk, value_blk)
        centred = d_probs - lax.optimization_barrier(jnp.sum(probs * d_probs, axis=-1, keepdims=True))
        d_scores = (probs * centred * head_dim ** (-0.5)).astype(jnp.bfloat16).astype(jnp.float32)
        d_query = jnp.einsum('hqk,khd->qhd', d_scores, key_blk)
        d_key = jnp.einsum('hqk,qhd->khd', d_scores, query_blk)
        d_value = jnp.einsum('hqk,qhd->khd', probs_half, d_out_blk)
        return (d_query, d_key, d_value)
    d_queries, d_key_blocks, d_value_blocks = lax.map(backward_block, block_ids)
    d_query = d_queries.reshape(LENGTH, heads, head_dim)
    d_key = spread_keys(d_key_blocks, half, qblock)
    d_value = spread_keys(d_value_blocks, half, qblock)
    d_joined = jnp.concatenate([unrotate(d_query, cosine, sine).reshape(LENGTH, width), unrotate(d_key, cosine, sine).reshape(LENGTH, width), d_value.reshape(LENGTH, width)], axis=-1).astype(jnp.bfloat16)
    joined_grad = jnp.dot(normed_one.T, d_joined, preferred_element_type=jnp.float32)
    d_normed_one = jnp.dot(d_joined, w_joined.T, preferred_element_type=jnp.float32)
    d_source, gain_one_grad = norm_back(d_normed_one, norm_one, inv_one, gain_one)
    input_grad = (d_resid + d_source).astype(jnp.bfloat16)
    grads = (joined_grad, output_grad, expand_grad, contract_grad, gain_one_grad, gain_two_grad)
    return (layer_out, input_grad, grads)

def reference(layer_input, cotangent, w_joined, w_output, w_expand, w_contract, gain_one, gain_two):
    weights = (w_joined, w_output, w_expand, w_contract, gain_one, gain_two)
    sources = layer_input.reshape(MB * BATCH, LENGTH, D)
    upstreams = cotangent.reshape(MB * BATCH, LENGTH, D)
    start = tuple((jnp.zeros(w.shape, jnp.float32) for w in weights))

    def step(carry, pair):
        layer_out, input_grad, grads = one_sequence(pair[0], pair[1], weights)
        return (tuple((c + g for c, g in zip(carry, grads))), (layer_out, input_grad))
    totals, (outputs, input_grads) = lax.scan(step, start, (sources, upstreams))
    return (outputs.reshape(MB, BATCH, LENGTH, D), input_grads.reshape(MB, BATCH, LENGTH, D), totals[0], totals[1], totals[2], totals[3], totals[4], totals[5])
```

```python
import functools

import jax
import jax.numpy as jnp
from jax import lax
from jax.experimental import pallas as pl
from jax.experimental.pallas import tpu as pltpu
from jax.sharding import PartitionSpec as P

HEADS = 12
HEAD_DIM = 64
WINDOW = 128


NORM_EPS = 1e-05
ROPE_BASE = 10000.0
MASK_FILL = -1e30
SQRT_HALF = 0.7071067811865476
INV_ROOT_TAU = 0.3989422804014327


LANES = 128


def pair_sum(value, outer):
    outer_size = lax.axis_size(outer)
    pairs = outer_size // 2
    core = lax.axis_index(outer) % 2
    blocks = value.reshape(pairs, 2, value.shape[0] // outer_size, value.shape[1])
    other = lax.dynamic_index_in_dim(blocks, 1 - core, axis=1, keepdims=False)
    own = lax.dynamic_index_in_dim(blocks, core, axis=1, keepdims=False)
    swap = [(i, i ^ 1) for i in range(outer_size)]
    return own + lax.ppermute(other, outer, swap)


def line_sum(value, outer):
    outer_size = lax.axis_size(outer)
    if outer_size == 4:
        line = lax.axis_index(outer) // 2
        other = lax.dynamic_index_in_dim(value, 1 - line, axis=0, keepdims=False)
        own = lax.dynamic_index_in_dim(value, line, axis=0, keepdims=False)
        swap = [(i, i ^ 2) for i in range(outer_size)]
        arrived = lax.ppermute(other.astype(jnp.bfloat16), outer, swap)
        value = own + arrived.astype(jnp.float32)
    else:
        groups = [list(range(c, outer_size, 2)) for c in range(2)]
        arrived = lax.all_to_all(
            value.astype(jnp.bfloat16), outer, 0, 0, axis_index_groups=groups
        )
        value = jnp.sum(arrived.astype(jnp.float32), axis=0)
    return value


def ring_sum(value, inner):
    inner_size = lax.axis_size(inner)
    blocks = value.reshape(inner_size, value.shape[0] // inner_size, value.shape[1])
    return jnp.sum(lax.all_to_all(blocks, inner, 0, 0), axis=0)


def norm_apply(values, gain):
    center = jnp.mean(values, axis=-1, keepdims=True)
    shifted = values - center
    inv_std = lax.rsqrt(jnp.mean(shifted * shifted, axis=-1, keepdims=True) + NORM_EPS)
    normed = shifted * inv_std
    return (normed * gain.astype(jnp.float32), normed, inv_std)


def norm_back(upstream, normed, inv_std, gain):
    scaled = upstream * gain.astype(jnp.float32)
    inner = (
        scaled
        - jnp.mean(scaled, axis=-1, keepdims=True)
        - normed * jnp.mean(scaled * normed, axis=-1, keepdims=True)
    )
    return (inv_std * inner, jnp.sum(upstream * normed, axis=(0, 1)))


def gelu_slope(values):
    cumul = 0.5 * (1.0 + jax.scipy.special.erf(values * SQRT_HALF))
    return cumul + values * jnp.exp(-0.5 * values * values) * INV_ROOT_TAU


def rope_tables(positions, head_dim):
    half_dim = head_dim // 2
    freqs = ROPE_BASE ** (-jnp.arange(half_dim).astype(jnp.float32) * 2.0 / head_dim)
    angles = positions.astype(jnp.float32)[:, None] * freqs[None, :]
    return (jnp.cos(angles)[:, None, :], jnp.sin(angles)[:, None, :])


def rotate(values, cosine, sine):
    half_dim = values.shape[-1] // 2
    first = values[..., :half_dim]
    second = values[..., half_dim:]
    return jnp.concatenate(
        [first * cosine - second * sine, second * cosine + first * sine], axis=-1
    )


def unrotate(values, cosine, sine):
    half_dim = values.shape[-1] // 2
    first = values[..., :half_dim]
    second = values[..., half_dim:]
    return jnp.concatenate(
        [first * cosine + second * sine, second * cosine - first * sine], axis=-1
    )


def plain_layer(
    layer_input, cotangent, w_joined, w_output, w_expand, w_contract, gain_one, gain_two
):
    micro, local_batch, group, width = layer_input.shape
    heads = HEADS
    head_dim = HEAD_DIM
    half = WINDOW // 2
    ffn = w_contract.shape[0]
    batch = micro * local_batch
    scale = head_dim ** (-0.5)
    axes = ("dp", "seq")
    seq_count = lax.axis_size("seq")
    up = [(i, i + 1) for i in range(seq_count - 1)]
    down = [(j, i) for i, j in up]
    group_start = lax.axis_index("seq") * group
    cosine, sine = rope_tables(group_start + jnp.arange(group, dtype=jnp.int32), head_dim)
    query_pos = group_start + jnp.arange(group, dtype=jnp.int32)[:, None]
    key_pos = group_start - half + jnp.arange(group + 2 * half, dtype=jnp.int32)[None, :]
    allowed = (
        (jnp.abs(query_pos - key_pos) <= half) & (key_pos >= 0) & (key_pos < group * seq_count)
    )
    gains = jnp.pad(jnp.stack([gain_one, gain_two], axis=1), ((0, 0), (0, LANES - 2)))
    pack_one = jnp.concatenate([w_joined, gains], axis=1)
    pack_two = jnp.concatenate([w_expand, w_contract.T, w_output], axis=1)
    full_one = lax.all_gather(pack_one, axes, axis=0, tiled=True)
    full_two = lax.all_gather(pack_two, axes, axis=0, tiled=True)
    full_joined = full_one[:, : 3 * width]
    full_gain_one = full_one[:, 3 * width]
    full_gain_two = full_one[:, 3 * width + 1]
    full_expand = full_two[:, : 2 * ffn]
    full_contract = full_two[:, 2 * ffn : 3 * ffn]
    full_output = full_two[:, 3 * ffn :]

    source32 = layer_input.reshape(batch, group, width).astype(jnp.float32)
    upstream_half = cotangent.reshape(batch, group, width)
    normed_f, norm_one, inv_one = norm_apply(source32, full_gain_one)
    normed_one = normed_f.astype(jnp.bfloat16)
    joined = jnp.einsum(
        "bcd,de->bce", normed_one, full_joined, preferred_element_type=jnp.float32
    )
    shape_heads = (batch, group, heads, head_dim)
    k_rot = rotate(joined[..., width : 2 * width].reshape(shape_heads), cosine, sine).astype(
        jnp.bfloat16
    )
    v_half = joined[..., 2 * width :].astype(jnp.bfloat16)
    key_value = jnp.stack([k_rot.reshape(batch, group, width), v_half])
    before = lax.ppermute(key_value[:, :, group - half :], "seq", up)
    after = lax.ppermute(key_value[:, :, :half], "seq", down)
    q_rot = rotate(joined[..., :width].reshape(shape_heads), cosine, sine).astype(jnp.bfloat16)
    extended = jnp.concatenate([before, key_value, after], axis=2)
    ext_shape = (batch, group + 2 * half, heads, head_dim)
    key_rows = extended[0].reshape(ext_shape)
    value_rows = extended[1].reshape(ext_shape)
    scores = (
        jnp.einsum("bqhd,bkhd->bhqk", q_rot, key_rows, preferred_element_type=jnp.float32)
        * scale
    )
    scores = jnp.where(allowed[None, None], scores, MASK_FILL)
    row_max = jnp.max(scores, axis=-1, keepdims=True)
    log_total = row_max + jnp.log(jnp.sum(jnp.exp(scores - row_max), axis=-1, keepdims=True))
    probs = jnp.exp(scores - log_total)
    probs_half = probs.astype(jnp.bfloat16)
    attended = jnp.einsum(
        "bhqk,bkhd->bqhd", probs_half, value_rows, preferred_element_type=jnp.float32
    )
    attended = attended.astype(jnp.bfloat16).reshape(batch, group, width)
    resid = source32 + jnp.einsum(
        "bcd,de->bce", attended, full_output, preferred_element_type=jnp.float32
    )
    normed_g, norm_two, inv_two = norm_apply(resid, full_gain_two)
    normed_two = normed_g.astype(jnp.bfloat16)
    expanded = jnp.einsum(
        "bcd,de->bce", normed_two, full_expand, preferred_element_type=jnp.float32
    )
    pre_act = expanded[..., :ffn]
    gate_part = expanded[..., ffn:]
    activated = jax.nn.gelu(pre_act, approximate=False)
    mixed = (activated * gate_part).astype(jnp.bfloat16)
    contract_acc = jnp.einsum(
        "bcd,bcf->df", upstream_half, mixed, preferred_element_type=jnp.float32
    )
    d_mixed = jnp.einsum(
        "bcd,df->bcf", upstream_half, full_contract, preferred_element_type=jnp.float32
    )
    d_expanded = jnp.concatenate(
        [d_mixed * gate_part * gelu_slope(pre_act), d_mixed * activated], axis=-1
    ).astype(jnp.bfloat16)
    expand_acc = jnp.einsum(
        "bcd,bce->de", normed_two, d_expanded, preferred_element_type=jnp.float32
    )
    ffn_grads, d_expanded = lax.optimization_barrier(
        (jnp.concatenate([expand_acc, contract_acc], axis=1), d_expanded)
    )
    ffn_pair = pair_sum(ffn_grads, "dp")
    d_normed_two = jnp.einsum(
        "bce,de->bcd", d_expanded, full_expand, preferred_element_type=jnp.float32
    )
    d_resid_n, gain_two_part = norm_back(d_normed_two, norm_two, inv_two, full_gain_two)
    d_resid = upstream_half.astype(jnp.float32) + d_resid_n
    d_resid_half = d_resid.astype(jnp.bfloat16)
    ffn_pair, d_resid_half = lax.optimization_barrier((ffn_pair, d_resid_half))
    ffn_line = line_sum(ffn_pair, "dp")
    d_attended = jnp.einsum(
        "bce,de->bcd", d_resid_half, full_output, preferred_element_type=jnp.float32
    )
    d_attended = d_attended.astype(jnp.bfloat16).reshape(shape_heads)
    d_probs = jnp.einsum(
        "bqhd,bkhd->bhqk", d_attended, value_rows, preferred_element_type=jnp.float32
    )
    centred = d_probs - jnp.sum(probs * d_probs, axis=-1, keepdims=True)
    d_scores = (probs * centred * scale).astype(jnp.bfloat16)
    d_key_ext = jnp.einsum(
        "bhqk,bqhd->bkhd", d_scores, q_rot, preferred_element_type=jnp.float32
    )
    d_value_ext = jnp.einsum(
        "bhqk,bqhd->bkhd", probs_half, d_attended, preferred_element_type=jnp.float32
    )
    ext_grads = jnp.stack(
        [
            d_key_ext.reshape(batch, group + 2 * half, width),
            d_value_ext.reshape(batch, group + 2 * half, width),
        ]
    )
    rims = ext_grads.astype(jnp.bfloat16)
    ffn_line, rims = lax.optimization_barrier((ffn_line, rims))
    ffn_sum = ring_sum(ffn_line, "seq")
    from_left = lax.ppermute(rims[:, :, group + half :], "seq", up).astype(jnp.float32)
    from_right = lax.ppermute(rims[:, :, :half], "seq", down).astype(jnp.float32)
    d_query = jnp.einsum(
        "bhqk,bkhd->bqhd", d_scores, key_rows, preferred_element_type=jnp.float32
    )
    output_acc = jnp.einsum(
        "bcd,bce->de", attended, d_resid_half, preferred_element_type=jnp.float32
    )
    final = resid + jnp.einsum(
        "bcf,df->bcd", mixed, full_contract, preferred_element_type=jnp.float32
    )
    own_grads = ext_grads[:, :, half : half + group]
    own_grads = own_grads + jnp.pad(
        from_left, ((0, 0), (0, 0), (0, group - half), (0, 0))
    ) + jnp.pad(from_right, ((0, 0), (0, 0), (group - half, 0), (0, 0)))
    d_key = unrotate(own_grads[0].reshape(shape_heads), cosine, sine).reshape(
        batch, group, width
    )
    d_query_flat = unrotate(d_query, cosine, sine).reshape(batch, group, width)
    d_joined = jnp.concatenate([d_query_flat, d_key, own_grads[1]], axis=-1).astype(
        jnp.bfloat16
    )
    d_normed_one = jnp.einsum(
        "bce,de->bcd", d_joined, full_joined, preferred_element_type=jnp.float32
    )
    d_source, gain_one_part = norm_back(d_normed_one, norm_one, inv_one, full_gain_one)
    input_grad = (d_resid + d_source).astype(jnp.bfloat16)
    joined_acc = jnp.einsum(
        "bcd,bce->de", normed_one, d_joined, preferred_element_type=jnp.float32
    )
    gain_parts = jnp.pad(
        jnp.stack([gain_one_part, gain_two_part], axis=1), ((0, 0), (0, LANES - 2))
    )
    last_grads = jnp.concatenate([joined_acc, output_acc, gain_parts], axis=1)
    last_sum = ring_sum(line_sum(pair_sum(last_grads, "dp"), "dp"), "seq")
    return (
        final.astype(jnp.bfloat16).reshape(layer_input.shape),
        input_grad.reshape(layer_input.shape),
        last_sum[:, : 3 * width],
        last_sum[:, 3 * width : 4 * width],
        ffn_sum[:, : 2 * ffn],
        ffn_sum[:, 2 * ffn :].T,
        last_sum[:, 4 * width],
        last_sum[:, 4 * width + 1],
    )


MESH = pl.DeviceIdType.MESH
ROWS = 24
MIB = 2**20


def place():
    dp, seq = lax.axis_index("dp"), lax.axis_index("seq")
    y, core = dp // 2, dp % 2
    z, x = seq // 2, seq % 2
    zh, zl = z // 2, z % 2
    r = x * (1 - core) + y * core
    p = y * (1 - core) + x * core
    flip_r = ((dp + 2 * core * (1 - 2 * y)), (seq + (1 - core) * (1 - 2 * x)))
    flip_p = ((dp + 2 * (1 - core) * (1 - 2 * y)), (seq + core * (1 - 2 * x)))
    peers = dict(
        pair=(dp + 1 - 2 * core, seq),
        r=flip_r,
        p=flip_p,
        zl=(dp, seq + 2 - 4 * zl),
        zh=(dp, seq + 4 - 8 * zh),
    )
    return dict(dp=dp, seq=seq, y=y, core=core, z=z, x=x, zh=zh, zl=zl, r=r, p=p, peers=peers)


def meet(at):
    barrier = pltpu.get_barrier_semaphore()
    for peer in at["peers"].values():
        pl.semaphore_signal(barrier, inc=1, device_id=peer, device_id_type=MESH)
    pl.semaphore_wait(barrier, len(at["peers"]))


def push(src, dst, sems, where, peer):
    send, recv = sems
    copy = pltpu.make_async_remote_copy(
        src_ref=src,
        dst_ref=dst,
        send_sem=send.at[where],
        recv_sem=recv.at[where],
        device_id=peer,
        device_id_type=MESH,
    )
    copy.start()
    return copy


def gather_send(at, buf, sems, group, stage):
    c, r, p, zh, zl = at["core"], at["r"], at["p"], at["zh"], at["zl"]
    name, ref = (
        ("zh", lambda: buf.at[c, r, p, zh, zl]),
        ("zl", lambda: buf.at[c, r, p, :, zl]),
        ("p", lambda: buf.at[c, r, p]),
        ("r", lambda: buf.at[c, r]),
        ("pair", lambda: buf.at[c]),
    )[stage]
    return push(ref(), ref(), sems, (group, stage), at["peers"][name])


def relay(buf, out, offset, width):
    for core in range(2):
        for y in range(2):
            for z in range(4):
                blocks = []
                for x in range(2):
                    r, p = (x, y) if core == 0 else (y, x)
                    blocks.append(buf[core, r, p, z // 2, z % 2].astype(jnp.float32))
                row = y * 384 + core * 192 + z * 48
                out[row : row + 48, offset : offset + width] = jnp.concatenate(
                    blocks, axis=0
                ).astype(jnp.bfloat16)


def gather_kernel(
    wj, wo, we, wc, wj_out, wo_out, we_out, wc_out, b_kv, b_q, b_o, b_e1, b_e2, b_c, send, recv
):
    at = place()
    ff = wc.shape[1]
    width = wo.shape[1]
    groups = (
        (wj, width, 2 * width, b_kv, wj_out),
        (wj, 0, width, b_q, wj_out),
        (wo, 0, width, b_o, wo_out),
        (we, 0, ff, b_e1, we_out),
        (we, ff, ff, b_e2, we_out),
        (wc, 0, ff, b_c, wc_out),
    )
    spot = (at["core"], at["r"], at["p"], at["zh"], at["zl"])
    for ref, offset, size, buf, _ in groups:
        buf[spot] = ref[:, offset : offset + size]
    meet(at)
    sems = (send, recv)
    copies = {}
    for t in range(len(groups) + 5):
        for g, (_, offset, size, buf, out) in enumerate(groups):
            stage = t - g
            if 0 < stage <= 5:
                copies[g, stage - 1].wait()
            if 0 <= stage < 5:
                copies[g, stage] = gather_send(at, buf, sems, g, stage)
            if stage == 5:
                relay(buf, out, offset, size)


def gather_weights(wj, wo, we, wc):
    width, ff = wo.shape[1], wc.shape[1]
    half = jnp.bfloat16
    vmem = pl.BlockSpec(memory_space=pltpu.VMEM)
    lead = (2, 2, 2, 2, 2, ROWS)
    sizes = (2 * width, width, width, ff, ff, ff)
    return pl.pallas_call(
        gather_kernel,
        out_shape=tuple(
            jax.ShapeDtypeStruct((width, n), half) for n in (3 * width, width, 2 * ff, ff)
        ),
        in_specs=[vmem] * 4,
        out_specs=(vmem,) * 4,
        scratch_shapes=[pltpu.VMEM(lead + (n,), half) for n in sizes]
        + [pltpu.SemaphoreType.DMA((6, 5)), pltpu.SemaphoreType.DMA((6, 5))],
        compiler_params=pltpu.CompilerParams(
            collective_id=0, has_side_effects=True, vmem_limit_bytes=40 * MIB
        ),
    )(wj, wo, we, wc)


def block_row(at, p, z, r):
    core = at["core"]
    y = p * (1 - core) + r * core
    x = r * (1 - core) + p * core
    return y, pl.multiple_of(z * 48 + x * ROWS, 8)


def sum_stage(at, stage, grads, cols, bufs, sems, index, width, out, out_cols):
    r0, acc, s1, r1, s2, r2, s3, r3, s4, r4 = bufs
    core, r, p, zh, zl = at["core"], at["r"], at["p"], at["zh"], at["zl"]
    peers = at["peers"]
    f32 = jnp.float32
    w = slice(0, width)
    if stage == 0:
        copies = []
        for y in range(2):
            rows = pl.ds(pl.multiple_of(y * 384 + (1 - core) * 192, 192), 192)
            copies.append(
                push(grads.at[rows, cols], r0.at[y, :, w], sems, (index, y), peers["pair"])
            )
        return copies
    if stage == 1:

        @pl.loop(0, 8)
        def _(i):
            pp, z = i // 4, i % 4
            y, row = block_row(at, pp, z, 1 - r)
            base = pl.multiple_of(y * 384 + core * 192 + row, 8)
            s1[pp, z, :, w] = (
                grads[pl.ds(base, ROWS), cols] + r0[y, pl.ds(row, ROWS), w]
            ).astype(s1.dtype)
            y, row = block_row(at, pp, z, r)
            base = pl.multiple_of(y * 384 + core * 192 + row, 8)
            acc[pp, z, :, w] = grads[pl.ds(base, ROWS), cols] + r0[y, pl.ds(row, ROWS), w]

        return [push(s1.at[:, :, :, w], r1.at[:, :, :, w], sems, (index, 2), peers["r"])]
    if stage == 2:

        @pl.loop(0, 4)
        def _(z):
            s2[z, :, w] = (acc[1 - p, z, :, w] + r1[1 - p, z, :, w].astype(f32)).astype(s2.dtype)
            acc[p, z, :, w] = acc[p, z, :, w] + r1[p, z, :, w].astype(f32)

        return [push(s2.at[:, :, w], r2.at[:, :, w], sems, (index, 3), peers["p"])]
    if stage == 3:
        for h in range(2):
            far, near = 2 * h + 1 - zl, 2 * h + zl
            s3[h, :, w] = acc[p, far, :, w] + r2[far, :, w].astype(f32)
            acc[p, near, :, w] = acc[p, near, :, w] + r2[near, :, w].astype(f32)
        return [push(s3.at[:, :, w], r3.at[:, :, w], sems, (index, 4), peers["zl"])]
    if stage == 4:
        s4[:, w] = acc[p, 2 * (1 - zh) + zl, :, w] + r3[1 - zh, :, w]
        return [push(s4.at[:, w], r4.at[:, w], sems, (index, 5), peers["zh"])]
    out[:, out_cols] = (acc[p, 2 * zh + zl, :, w] + r3[zh, :, w]) + r4[:, w]
    return []


def sum_scratch(width):
    f32, half = jnp.float32, jnp.bfloat16
    return [
        pltpu.VMEM((2, 192, width), f32),
        pltpu.VMEM((2, 4, ROWS, width), f32),
        pltpu.VMEM((2, 4, ROWS, width), half),
        pltpu.VMEM((2, 4, ROWS, width), half),
        pltpu.VMEM((4, ROWS, width), half),
        pltpu.VMEM((4, ROWS, width), half),
        pltpu.VMEM((2, ROWS, width), f32),
        pltpu.VMEM((2, ROWS, width), f32),
        pltpu.VMEM((ROWS, width), f32),
        pltpu.VMEM((ROWS, width), f32),
    ]


GAIN_PATH = ("pair", "r", "p", "zl", "zh")


def sum_kernel(g_e, g_c, g_o, g_j, g_n, o_e, o_c, o_o, o_j, o_n, *scratch):
    at = place()
    ff, width = g_c.shape[1], g_o.shape[1]
    chunks = (
        (g_e, 0, ff, o_e, 0),
        (g_e, ff, ff, o_e, ff),
        (g_c, 0, ff, o_c, 0),
        (g_o, 0, width, o_o, 0),
        (g_j, 0, width, o_j, 0),
        (g_j, width, width, o_j, width),
        (g_j, 2 * width, width, o_j, 2 * width),
    )
    n = len(chunks)
    sets = [scratch[10 * i : 10 * i + 10] for i in range(n)]
    gain_sum, gain_in, send, recv, gain_send, gain_recv = scratch[10 * n :]
    meet(at)
    gain_sum[0] = g_n[...]
    pending = {}
    for t in range(n + 5):
        if t <= 5:
            if t > 0:
                pending["gain"].wait()
                gain_sum[t] = gain_sum[t - 1] + gain_in[t - 1]
            if t < 5:
                pending["gain"] = push(
                    gain_sum.at[t],
                    gain_in.at[t],
                    (gain_send, gain_recv),
                    (t,),
                    at["peers"][GAIN_PATH[t]],
                )
        for i, (grads, offset, size, out, out_offset) in enumerate(chunks):
            stage = t - i
            if 0 <= stage <= 5:
                for copy in pending.get(i, ()):
                    copy.wait()
                pending[i] = sum_stage(
                    at,
                    stage,
                    grads,
                    slice(offset, offset + size),
                    sets[i],
                    (send, recv),
                    i,
                    size,
                    out,
                    slice(out_offset, out_offset + size),
                )
    shift = (32 - (at["dp"] * 8 + at["seq"])) * ROWS
    o_n[...] = pltpu.roll(gain_sum[5], shift % width, axis=1)[:, :128]


def sum_grads(g_e, g_c, g_o, g_j, g_n):
    f32 = jnp.float32
    ff, width = g_c.shape[1], g_o.shape[1]
    vmem = pl.BlockSpec(memory_space=pltpu.VMEM)
    scratch = []
    for size in (ff, ff, ff, width, width, width, width):
        scratch += sum_scratch(size)
    return pl.pallas_call(
        sum_kernel,
        out_shape=(
            jax.ShapeDtypeStruct((ROWS, 2 * ff), f32),
            jax.ShapeDtypeStruct((ROWS, ff), f32),
            jax.ShapeDtypeStruct((ROWS, width), f32),
            jax.ShapeDtypeStruct((ROWS, 3 * width), f32),
            jax.ShapeDtypeStruct((8, 128), f32),
        ),
        in_specs=[vmem] * 5,
        out_specs=(vmem,) * 5,
        scratch_shapes=scratch
        + [pltpu.VMEM((6, 8, width), f32), pltpu.VMEM((5, 8, width), f32)]
        + [pltpu.SemaphoreType.DMA((7, 6)), pltpu.SemaphoreType.DMA((7, 6))]
        + [pltpu.SemaphoreType.DMA((5,)), pltpu.SemaphoreType.DMA((5,))],
        compiler_params=pltpu.CompilerParams(
            collective_id=1, has_side_effects=True, vmem_limit_bytes=58 * MIB
        ),
    )(g_e, g_c, g_o, g_j, g_n)


def fast_layer(
    layer_input, cotangent, w_joined, w_output, w_expand, w_contract, gain_one, gain_two
):
    micro, local_batch, group, width = layer_input.shape
    heads = HEADS
    head_dim = HEAD_DIM
    half = WINDOW // 2
    ffn = w_contract.shape[0]
    batch = micro * local_batch
    scale = head_dim ** (-0.5)
    axes = ("dp", "seq")
    seq_count = lax.axis_size("seq")
    up = [(i, i + 1) for i in range(seq_count - 1)]
    down = [(j, i) for i, j in up]
    group_start = lax.axis_index("seq") * group
    cosine, sine = rope_tables(group_start + jnp.arange(group, dtype=jnp.int32), head_dim)
    query_pos = group_start + jnp.arange(group, dtype=jnp.int32)[:, None]
    key_pos = group_start - half + jnp.arange(group + 2 * half, dtype=jnp.int32)[None, :]
    allowed = (
        (jnp.abs(query_pos - key_pos) <= half) & (key_pos >= 0) & (key_pos < group * seq_count)
    )
    gains = jnp.stack([gain_one, gain_two])
    gains = lax.all_gather(gains, axes, axis=1, tiled=True)
    full_gain_one, full_gain_two = gains[0], gains[1]
    full_joined, full_output, full_expand, full_contract = gather_weights(
        w_joined, w_output, w_expand, w_contract.T
    )

    source32 = layer_input.reshape(batch, group, width).astype(jnp.float32)
    upstream_half = cotangent.reshape(batch, group, width)
    normed_f, norm_one, inv_one = norm_apply(source32, full_gain_one)
    normed_one = normed_f.astype(jnp.bfloat16)
    joined = jnp.einsum(
        "bcd,de->bce", normed_one, full_joined, preferred_element_type=jnp.float32
    )
    shape_heads = (batch, group, heads, head_dim)
    k_rot = rotate(joined[..., width : 2 * width].reshape(shape_heads), cosine, sine).astype(
        jnp.bfloat16
    )
    v_half = joined[..., 2 * width :].astype(jnp.bfloat16)
    key_value = jnp.stack([k_rot.reshape(batch, group, width), v_half])
    before = lax.ppermute(key_value[:, :, group - half :], "seq", up)
    after = lax.ppermute(key_value[:, :, :half], "seq", down)
    q_rot = rotate(joined[..., :width].reshape(shape_heads), cosine, sine).astype(jnp.bfloat16)
    extended = jnp.concatenate([before, key_value, after], axis=2)
    ext_shape = (batch, group + 2 * half, heads, head_dim)
    key_rows = extended[0].reshape(ext_shape)
    value_rows = extended[1].reshape(ext_shape)
    scores = (
        jnp.einsum("bqhd,bkhd->bhqk", q_rot, key_rows, preferred_element_type=jnp.float32)
        * scale
    )
    scores = jnp.where(allowed[None, None], scores, MASK_FILL)
    row_max = jnp.max(scores, axis=-1, keepdims=True)
    log_total = row_max + jnp.log(jnp.sum(jnp.exp(scores - row_max), axis=-1, keepdims=True))
    probs = jnp.exp(scores - log_total)
    probs_half = probs.astype(jnp.bfloat16)
    attended = jnp.einsum(
        "bhqk,bkhd->bqhd", probs_half, value_rows, preferred_element_type=jnp.float32
    )
    attended = attended.astype(jnp.bfloat16).reshape(batch, group, width)
    resid = source32 + jnp.einsum(
        "bcd,de->bce", attended, full_output, preferred_element_type=jnp.float32
    )
    normed_g, norm_two, inv_two = norm_apply(resid, full_gain_two)
    normed_two = normed_g.astype(jnp.bfloat16)
    expanded = jnp.einsum(
        "bcd,de->bce", normed_two, full_expand, preferred_element_type=jnp.float32
    )
    pre_act = expanded[..., :ffn]
    gate_part = expanded[..., ffn:]
    activated = jax.nn.gelu(pre_act, approximate=False)
    mixed = (activated * gate_part).astype(jnp.bfloat16)
    contract_acc = jnp.einsum(
        "bcd,bcf->df", upstream_half, mixed, preferred_element_type=jnp.float32
    )
    d_mixed = jnp.einsum(
        "bcd,df->bcf", upstream_half, full_contract, preferred_element_type=jnp.float32
    )
    d_expanded = jnp.concatenate(
        [d_mixed * gate_part * gelu_slope(pre_act), d_mixed * activated], axis=-1
    ).astype(jnp.bfloat16)
    expand_acc = jnp.einsum(
        "bcd,bce->de", normed_two, d_expanded, preferred_element_type=jnp.float32
    )
    d_normed_two = jnp.einsum(
        "bce,de->bcd", d_expanded, full_expand, preferred_element_type=jnp.float32
    )
    d_resid_n, gain_two_part = norm_back(d_normed_two, norm_two, inv_two, full_gain_two)
    d_resid = upstream_half.astype(jnp.float32) + d_resid_n
    d_resid_half = d_resid.astype(jnp.bfloat16)
    d_attended = jnp.einsum(
        "bce,de->bcd", d_resid_half, full_output, preferred_element_type=jnp.float32
    )
    d_attended = d_attended.astype(jnp.bfloat16).reshape(shape_heads)
    d_probs = jnp.einsum(
        "bqhd,bkhd->bhqk", d_attended, value_rows, preferred_element_type=jnp.float32
    )
    centred = d_probs - jnp.sum(probs * d_probs, axis=-1, keepdims=True)
    d_scores = (probs * centred * scale).astype(jnp.bfloat16)
    d_key_ext = jnp.einsum(
        "bhqk,bqhd->bkhd", d_scores, q_rot, preferred_element_type=jnp.float32
    )
    d_value_ext = jnp.einsum(
        "bhqk,bqhd->bkhd", probs_half, d_attended, preferred_element_type=jnp.float32
    )
    ext_grads = jnp.stack(
        [
            d_key_ext.reshape(batch, group + 2 * half, width),
            d_value_ext.reshape(batch, group + 2 * half, width),
        ]
    )
    rims = ext_grads.astype(jnp.bfloat16)
    from_left = lax.ppermute(rims[:, :, group + half :], "seq", up).astype(jnp.float32)
    from_right = lax.ppermute(rims[:, :, :half], "seq", down).astype(jnp.float32)
    d_query = jnp.einsum(
        "bhqk,bkhd->bqhd", d_scores, key_rows, preferred_element_type=jnp.float32
    )
    output_acc = jnp.einsum(
        "bcd,bce->de", attended, d_resid_half, preferred_element_type=jnp.float32
    )
    final = resid + jnp.einsum(
        "bcf,df->bcd", mixed, full_contract, preferred_element_type=jnp.float32
    )
    own_grads = ext_grads[:, :, half : half + group]
    own_grads = own_grads + jnp.pad(
        from_left, ((0, 0), (0, 0), (0, group - half), (0, 0))
    ) + jnp.pad(from_right, ((0, 0), (0, 0), (group - half, 0), (0, 0)))
    d_key = unrotate(own_grads[0].reshape(shape_heads), cosine, sine).reshape(
        batch, group, width
    )
    d_query_flat = unrotate(d_query, cosine, sine).reshape(batch, group, width)
    d_joined = jnp.concatenate([d_query_flat, d_key, own_grads[1]], axis=-1).astype(
        jnp.bfloat16
    )
    d_normed_one = jnp.einsum(
        "bce,de->bcd", d_joined, full_joined, preferred_element_type=jnp.float32
    )
    d_source, gain_one_part = norm_back(d_normed_one, norm_one, inv_one, full_gain_one)
    input_grad = (d_resid + d_source).astype(jnp.bfloat16)
    joined_acc = jnp.einsum(
        "bcd,bce->de", normed_one, d_joined, preferred_element_type=jnp.float32
    )
    gain_parts = jnp.pad(jnp.stack([gain_one_part, gain_two_part]), ((0, 6), (0, 0)))
    o_e, o_c, o_o, o_j, o_n = sum_grads(
        expand_acc, contract_acc, output_acc, joined_acc, gain_parts
    )
    return (
        final.astype(jnp.bfloat16).reshape(layer_input.shape),
        input_grad.reshape(layer_input.shape),
        o_j,
        o_o,
        o_e,
        o_c.T,
        o_n[0, :24],
        o_n[1, :24],
    )


def solution(mesh):
    fits = mesh.shape["dp"] == 4 and mesh.shape["seq"] == 8
    body = fast_layer if fits else plain_layer
    placed = (
        P(None, "dp", "seq", None),
        P(None, "dp", "seq", None),
        P(("dp", "seq"), None),
        P(("dp", "seq"), None),
        P(("dp", "seq"), None),
        P(None, ("dp", "seq")),
        P(("dp", "seq")),
        P(("dp", "seq")),
    )
    return jax.shard_map(
        body,
        mesh=mesh,
        in_specs=placed,
        out_specs=(
            P(None, "dp", "seq", None),
            P(None, "dp", "seq", None),
            P(("dp", "seq"), None),
            P(("dp", "seq"), None),
            P(("dp", "seq"), None),
            P(None, ("dp", "seq")),
            P(("dp", "seq")),
            P(("dp", "seq")),
        ),
        check_vma=False,
    )
```

```python
import functools

import jax
import jax.numpy as jnp
from jax import lax
from jax.experimental import pallas as pl
from jax.experimental.pallas import tpu as pltpu
from jax.sharding import PartitionSpec as P

HEADS = 12
HEAD_DIM = 64
WINDOW = 128


NORM_EPS = 1e-05
ROPE_BASE = 10000.0
MASK_FILL = -1e30
SQRT_HALF = 0.7071067811865476
INV_ROOT_TAU = 0.3989422804014327


LANES = 128


def pair_sum(value, outer):
    outer_size = lax.axis_size(outer)
    pairs = outer_size // 2
    core = lax.axis_index(outer) % 2
    blocks = value.reshape(pairs, 2, value.shape[0] // outer_size, value.shape[1])
    other = lax.dynamic_index_in_dim(blocks, 1 - core, axis=1, keepdims=False)
    own = lax.dynamic_index_in_dim(blocks, core, axis=1, keepdims=False)
    swap = [(i, i ^ 1) for i in range(outer_size)]
    return own + lax.ppermute(other, outer, swap)


def line_sum(value, outer):
    outer_size = lax.axis_size(outer)
    if outer_size == 4:
        line = lax.axis_index(outer) // 2
        other = lax.dynamic_index_in_dim(value, 1 - line, axis=0, keepdims=False)
        own = lax.dynamic_index_in_dim(value, line, axis=0, keepdims=False)
        swap = [(i, i ^ 2) for i in range(outer_size)]
        arrived = lax.ppermute(other.astype(jnp.bfloat16), outer, swap)
        value = own + arrived.astype(jnp.float32)
    else:
        groups = [list(range(c, outer_size, 2)) for c in range(2)]
        arrived = lax.all_to_all(
            value.astype(jnp.bfloat16), outer, 0, 0, axis_index_groups=groups
        )
        value = jnp.sum(arrived.astype(jnp.float32), axis=0)
    return value


def ring_sum(value, inner):
    inner_size = lax.axis_size(inner)
    blocks = value.reshape(inner_size, value.shape[0] // inner_size, value.shape[1])
    return jnp.sum(lax.all_to_all(blocks, inner, 0, 0), axis=0)


def norm_apply(values, gain):
    center = jnp.mean(values, axis=-1, keepdims=True)
    shifted = values - center
    inv_std = lax.rsqrt(jnp.mean(shifted * shifted, axis=-1, keepdims=True) + NORM_EPS)
    normed = shifted * inv_std
    return (normed * gain.astype(jnp.float32), normed, inv_std)


def norm_back(upstream, normed, inv_std, gain):
    scaled = upstream * gain.astype(jnp.float32)
    inner = (
        scaled
        - jnp.mean(scaled, axis=-1, keepdims=True)
        - normed * jnp.mean(scaled * normed, axis=-1, keepdims=True)
    )
    return (inv_std * inner, jnp.sum(upstream * normed, axis=(0, 1)))


def gelu_slope(values):
    cumul = 0.5 * (1.0 + jax.scipy.special.erf(values * SQRT_HALF))
    return cumul + values * jnp.exp(-0.5 * values * values) * INV_ROOT_TAU


def rope_tables(positions, head_dim):
    half_dim = head_dim // 2
    freqs = ROPE_BASE ** (-jnp.arange(half_dim).astype(jnp.float32) * 2.0 / head_dim)
    angles = positions.astype(jnp.float32)[:, None] * freqs[None, :]
    return (jnp.cos(angles)[:, None, :], jnp.sin(angles)[:, None, :])


def rotate(values, cosine, sine):
    half_dim = values.shape[-1] // 2
    first = values[..., :half_dim]
    second = values[..., half_dim:]
    return jnp.concatenate(
        [first * cosine - second * sine, second * cosine + first * sine], axis=-1
    )


def unrotate(values, cosine, sine):
    half_dim = values.shape[-1] // 2
    first = values[..., :half_dim]
    second = values[..., half_dim:]
    return jnp.concatenate(
        [first * cosine + second * sine, second * cosine - first * sine], axis=-1
    )


def plain_layer(
    layer_input, cotangent, w_joined, w_output, w_expand, w_contract, gain_one, gain_two
):
    micro, local_batch, group, width = layer_input.shape
    heads = HEADS
    head_dim = HEAD_DIM
    half = WINDOW // 2
    ffn = w_contract.shape[0]
    batch = micro * local_batch
    scale = head_dim ** (-0.5)
    axes = ("dp", "seq")
    seq_count = lax.axis_size("seq")
    up = [(i, i + 1) for i in range(seq_count - 1)]
    down = [(j, i) for i, j in up]
    group_start = lax.axis_index("seq") * group
    cosine, sine = rope_tables(group_start + jnp.arange(group, dtype=jnp.int32), head_dim)
    query_pos = group_start + jnp.arange(group, dtype=jnp.int32)[:, None]
    key_pos = group_start - half + jnp.arange(group + 2 * half, dtype=jnp.int32)[None, :]
    allowed = (
        (jnp.abs(query_pos - key_pos) <= half) & (key_pos >= 0) & (key_pos < group * seq_count)
    )
    gains = jnp.pad(jnp.stack([gain_one, gain_two], axis=1), ((0, 0), (0, LANES - 2)))
    pack_one = jnp.concatenate([w_joined, gains], axis=1)
    pack_two = jnp.concatenate([w_expand, w_contract.T, w_output], axis=1)
    full_one = lax.all_gather(pack_one, axes, axis=0, tiled=True)
    full_two = lax.all_gather(pack_two, axes, axis=0, tiled=True)
    full_joined = full_one[:, : 3 * width]
    full_gain_one = full_one[:, 3 * width]
    full_gain_two = full_one[:, 3 * width + 1]
    full_expand = full_two[:, : 2 * ffn]
    full_contract = full_two[:, 2 * ffn : 3 * ffn]
    full_output = full_two[:, 3 * ffn :]

    source32 = layer_input.reshape(batch, group, width).astype(jnp.float32)
    upstream_half = cotangent.reshape(batch, group, width)
    normed_f, norm_one, inv_one = norm_apply(source32, full_gain_one)
    normed_one = normed_f.astype(jnp.bfloat16)
    joined = jnp.einsum(
        "bcd,de->bce", normed_one, full_joined, preferred_element_type=jnp.float32
    )
    shape_heads = (batch, group, heads, head_dim)
    k_rot = rotate(joined[..., width : 2 * width].reshape(shape_heads), cosine, sine).astype(
        jnp.bfloat16
    )
    v_half = joined[..., 2 * width :].astype(jnp.bfloat16)
    key_value = jnp.stack([k_rot.reshape(batch, group, width), v_half])
    before = lax.ppermute(key_value[:, :, group - half :], "seq", up)
    after = lax.ppermute(key_value[:, :, :half], "seq", down)
    q_rot = rotate(joined[..., :width].reshape(shape_heads), cosine, sine).astype(jnp.bfloat16)
    extended = jnp.concatenate([before, key_value, after], axis=2)
    ext_shape = (batch, group + 2 * half, heads, head_dim)
    key_rows = extended[0].reshape(ext_shape)
    value_rows = extended[1].reshape(ext_shape)
    scores = (
        jnp.einsum("bqhd,bkhd->bhqk", q_rot, key_rows, preferred_element_type=jnp.float32)
        * scale
    )
    scores = jnp.where(allowed[None, None], scores, MASK_FILL)
    row_max = jnp.max(scores, axis=-1, keepdims=True)
    log_total = row_max + jnp.log(jnp.sum(jnp.exp(scores - row_max), axis=-1, keepdims=True))
    probs = jnp.exp(scores - log_total)
    probs_half = probs.astype(jnp.bfloat16)
    attended = jnp.einsum(
        "bhqk,bkhd->bqhd", probs_half, value_rows, preferred_element_type=jnp.float32
    )
    attended = attended.astype(jnp.bfloat16).reshape(batch, group, width)
    resid = source32 + jnp.einsum(
        "bcd,de->bce", attended, full_output, preferred_element_type=jnp.float32
    )
    normed_g, norm_two, inv_two = norm_apply(resid, full_gain_two)
    normed_two = normed_g.astype(jnp.bfloat16)
    expanded = jnp.einsum(
        "bcd,de->bce", normed_two, full_expand, preferred_element_type=jnp.float32
    )
    pre_act = expanded[..., :ffn]
    gate_part = expanded[..., ffn:]
    activated = jax.nn.gelu(pre_act, approximate=False)
    mixed = (activated * gate_part).astype(jnp.bfloat16)
    contract_acc = jnp.einsum(
        "bcd,bcf->df", upstream_half, mixed, preferred_element_type=jnp.float32
    )
    d_mixed = jnp.einsum(
        "bcd,df->bcf", upstream_half, full_contract, preferred_element_type=jnp.float32
    )
    d_expanded = jnp.concatenate(
        [d_mixed * gate_part * gelu_slope(pre_act), d_mixed * activated], axis=-1
    ).astype(jnp.bfloat16)
    expand_acc = jnp.einsum(
        "bcd,bce->de", normed_two, d_expanded, preferred_element_type=jnp.float32
    )
    ffn_grads, d_expanded = lax.optimization_barrier(
        (jnp.concatenate([expand_acc, contract_acc], axis=1), d_expanded)
    )
    ffn_pair = pair_sum(ffn_grads, "dp")
    d_normed_two = jnp.einsum(
        "bce,de->bcd", d_expanded, full_expand, preferred_element_type=jnp.float32
    )
    d_resid_n, gain_two_part = norm_back(d_normed_two, norm_two, inv_two, full_gain_two)
    d_resid = upstream_half.astype(jnp.float32) + d_resid_n
    d_resid_half = d_resid.astype(jnp.bfloat16)
    ffn_pair, d_resid_half = lax.optimization_barrier((ffn_pair, d_resid_half))
    ffn_line = line_sum(ffn_pair, "dp")
    d_attended = jnp.einsum(
        "bce,de->bcd", d_resid_half, full_output, preferred_element_type=jnp.float32
    )
    d_attended = d_attended.astype(jnp.bfloat16).reshape(shape_heads)
    d_probs = jnp.einsum(
        "bqhd,bkhd->bhqk", d_attended, value_rows, preferred_element_type=jnp.float32
    )
    centred = d_probs - jnp.sum(probs * d_probs, axis=-1, keepdims=True)
    d_scores = (probs * centred * scale).astype(jnp.bfloat16)
    d_key_ext = jnp.einsum(
        "bhqk,bqhd->bkhd", d_scores, q_rot, preferred_element_type=jnp.float32
    )
    d_value_ext = jnp.einsum(
        "bhqk,bqhd->bkhd", probs_half, d_attended, preferred_element_type=jnp.float32
    )
    ext_grads = jnp.stack(
        [
            d_key_ext.reshape(batch, group + 2 * half, width),
            d_value_ext.reshape(batch, group + 2 * half, width),
        ]
    )
    rims = ext_grads.astype(jnp.bfloat16)
    ffn_line, rims = lax.optimization_barrier((ffn_line, rims))
    ffn_sum = ring_sum(ffn_line, "seq")
    from_left = lax.ppermute(rims[:, :, group + half :], "seq", up).astype(jnp.float32)
    from_right = lax.ppermute(rims[:, :, :half], "seq", down).astype(jnp.float32)
    d_query = jnp.einsum(
        "bhqk,bkhd->bqhd", d_scores, key_rows, preferred_element_type=jnp.float32
    )
    output_acc = jnp.einsum(
        "bcd,bce->de", attended, d_resid_half, preferred_element_type=jnp.float32
    )
    final = resid + jnp.einsum(
        "bcf,df->bcd", mixed, full_contract, preferred_element_type=jnp.float32
    )
    own_grads = ext_grads[:, :, half : half + group]
    own_grads = own_grads + jnp.pad(
        from_left, ((0, 0), (0, 0), (0, group - half), (0, 0))
    ) + jnp.pad(from_right, ((0, 0), (0, 0), (group - half, 0), (0, 0)))
    d_key = unrotate(own_grads[0].reshape(shape_heads), cosine, sine).reshape(
        batch, group, width
    )
    d_query_flat = unrotate(d_query, cosine, sine).reshape(batch, group, width)
    d_joined = jnp.concatenate([d_query_flat, d_key, own_grads[1]], axis=-1).astype(
        jnp.bfloat16
    )
    d_normed_one = jnp.einsum(
        "bce,de->bcd", d_joined, full_joined, preferred_element_type=jnp.float32
    )
    d_source, gain_one_part = norm_back(d_normed_one, norm_one, inv_one, full_gain_one)
    input_grad = (d_resid + d_source).astype(jnp.bfloat16)
    joined_acc = jnp.einsum(
        "bcd,bce->de", normed_one, d_joined, preferred_element_type=jnp.float32
    )
    gain_parts = jnp.pad(
        jnp.stack([gain_one_part, gain_two_part], axis=1), ((0, 0), (0, LANES - 2))
    )
    last_grads = jnp.concatenate([joined_acc, output_acc, gain_parts], axis=1)
    last_sum = ring_sum(line_sum(pair_sum(last_grads, "dp"), "dp"), "seq")
    return (
        final.astype(jnp.bfloat16).reshape(layer_input.shape),
        input_grad.reshape(layer_input.shape),
        last_sum[:, : 3 * width],
        last_sum[:, 3 * width : 4 * width],
        ffn_sum[:, : 2 * ffn],
        ffn_sum[:, 2 * ffn :].T,
        last_sum[:, 4 * width],
        last_sum[:, 4 * width + 1],
    )


MESH = pl.DeviceIdType.MESH
ROWS = 24
MIB = 2**20
F32 = jnp.float32
HALF = jnp.bfloat16
PAIR = 128


def place():
    dp, seq = lax.axis_index("dp"), lax.axis_index("seq")
    y, core = dp // 2, dp % 2
    z, x = seq // 2, seq % 2
    zh, zl = z // 2, z % 2
    r = x * (1 - core) + y * core
    p = y * (1 - core) + x * core
    peers = dict(
        pair=(dp + 1 - 2 * core, seq),
        r=(dp + 2 * core * (1 - 2 * y), seq + (1 - core) * (1 - 2 * x)),
        p=(dp + 2 * (1 - core) * (1 - 2 * y), seq + core * (1 - 2 * x)),
        zl=(dp, seq + 2 - 4 * zl),
        zh=(dp, seq + 4 - 8 * zh),
        left=(dp, (seq + 7) % 8),
        right=(dp, (seq + 1) % 8),
    )
    return dict(dp=dp, seq=seq, core=core, zh=zh, zl=zl, r=r, p=p, peers=peers)


def meet(at):
    barrier = pltpu.get_barrier_semaphore()
    for peer in at["peers"].values():
        pl.semaphore_signal(barrier, inc=1, device_id=peer, device_id_type=MESH)
    pl.semaphore_wait(barrier, len(at["peers"]))


def remote(src, dst, sems, where, peer):
    send, recv = sems
    return pltpu.make_async_remote_copy(
        src_ref=src,
        dst_ref=dst,
        send_sem=send.at[where],
        recv_sem=recv.at[where],
        device_id=peer,
        device_id_type=MESH,
    )


def push(*args):
    copy = remote(*args)
    copy.start()
    return copy


def gather_send(at, buf, sems, group, stage):
    c, r, p, zh, zl = at["core"], at["r"], at["p"], at["zh"], at["zl"]
    name, ref = (
        ("zh", lambda: buf.at[c, r, p, zh, zl]),
        ("zl", lambda: buf.at[c, r, p, :, zl]),
        ("p", lambda: buf.at[c, r, p]),
        ("r", lambda: buf.at[c, r]),
        ("pair", lambda: buf.at[c]),
    )[stage]
    return push(ref(), ref(), sems, (group, stage), at["peers"][name])


def plane_index(core, y, z, x):
    r, p = (x, y) if core == 0 else (y, x)
    return core, r, p, z // 2, z % 2


def relay(buf, store):
    for core in range(2):
        for y in range(2):
            for z in range(4):
                blocks = [buf[plane_index(core, y, z, x)].astype(F32) for x in range(2)]
                store(y * 384 + core * 192 + z * 48, jnp.concatenate(blocks, axis=0).astype(HALF))


def relay_gains(buf, gains):
    width = gains.shape[1]
    total = jnp.zeros((8, width), F32)
    for core in range(2):
        for y in range(2):
            for z in range(4):
                for x in range(2):
                    block = buf[plane_index(core, y, z, x)]
                    wide = jnp.concatenate([block, jnp.zeros((8, width - 128), F32)], axis=1)
                    shift = ROWS * (y * 16 + core * 8 + z * 2 + x)
                    total = total + (pltpu.roll(wide, shift, 1) if shift else wide)
    gains[...] = total


def block_row(at, p, z, r):
    core = at["core"]
    y = p * (1 - core) + r * core
    x = r * (1 - core) + p * core
    return y, pl.multiple_of(z * 48 + x * ROWS, 8)


def sum_stage(at, stage, grads, bufs, sems, index, width, emit):
    r0, r1, r2, r3, r4, s1, s2, s3, s4 = bufs
    core, r, p, zh, zl = at["core"], at["r"], at["p"], at["zh"], at["zl"]
    peers = at["peers"]
    w = slice(0, width)

    def kept(pp, z):
        y, row = block_row(at, pp, z, r)
        return y, pl.ds(row, ROWS)

    if stage == 0:
        copies = []
        for y in range(2):
            rows = pl.ds(pl.multiple_of(y * 384 + (1 - core) * 192, 192), 192)
            copies.append(push(grads.at[rows, w], r0.at[y], sems, (index, y), peers["pair"]))
        return copies
    if stage == 1:

        @pl.loop(0, 8)
        def _(i):
            pp, z = i // 4, i % 4
            y, row = block_row(at, pp, z, 1 - r)
            base = pl.multiple_of(y * 384 + core * 192 + row, 8)
            s1[pp, z // 2, z % 2, :, w] = (grads[pl.ds(base, ROWS), w] + r0[y, pl.ds(row, ROWS)]).astype(HALF)
            y, rows = kept(pp, z)
            base = pl.multiple_of(y * 384 + core * 192 + rows.start, 8)
            r0[y, rows] = grads[pl.ds(base, ROWS), w] + r0[y, rows]

        return [push(s1.at[:, :, :, :, w], r1, sems, (index, 2), peers["r"])]
    if stage == 2:

        @pl.loop(0, 4)
        def _(z):
            zh, zl = z // 2, z % 2
            s2[zh, zl, :, w] = (r0[kept(1 - p, z)] + r1[1 - p, zh, zl].astype(F32)).astype(HALF)
            r0[kept(p, z)] = r0[kept(p, z)] + r1[p, zh, zl].astype(F32)

        return [push(s2.at[:, :, :, w], r2, sems, (index, 3), peers["p"])]
    if stage == 3:
        for h in range(2):
            far, near = 2 * h + 1 - zl, 2 * h + zl
            s3[h, :, w] = r0[kept(p, far)] + r2[h, 1 - zl].astype(F32)
            r0[kept(p, near)] = r0[kept(p, near)] + r2[h, zl].astype(F32)
        return [push(s3.at[:, :, w], r3, sems, (index, 4), peers["zl"])]
    if stage == 4:
        s4[:, w] = r0[kept(p, 2 * (1 - zh) + zl)] + r3[1 - zh]
        return [push(s4.at[:, w], r4, sems, (index, 5), peers["zh"])]
    emit((r0[kept(p, 2 * zh + zl)] + r3[zh]) + r4[...])
    return []


GAIN_PATH = ("pair", "r", "p", "zl", "zh")


class Sums:
    def __init__(self, run):
        self.run, self.queue, self.pending, self.busy = run, [], {}, {}

    def add(self, index):
        self.step(index, 0)
        self.queue += [(index + 1.5 * s, index, s) for s in range(1, 6)]
        self.queue.sort()

    def step(self, index, stage):
        for copy in self.pending.pop(index, ()):
            copy.wait()
        self.busy.pop((index % 2, stage - 1), None)
        assert (index % 2, stage) not in self.busy
        if 0 < stage < 5:
            self.busy[index % 2, stage] = index
        self.pending[index] = self.run(index, stage)

    def pump(self, count=1):
        for _ in range(count):
            if self.queue:
                _, index, stage = self.queue.pop(0)
                self.step(index, stage)

    def reach(self, index, stage):
        while any(i == index and s <= stage for _, i, s in self.queue):
            self.pump()

    def drain(self):
        self.pump(len(self.queue))


def dot(a, b, dims):
    return lax.dot_general(a, b, (dims, ((), ())), preferred_element_type=F32)


NN, NT, TN = ((1,), (0,)), ((1,), (1,)), ((0,), (0,))


def swap_halves(v):
    lane = lax.broadcasted_iota(jnp.int32, v.shape, 1) % HEAD_DIM
    return jnp.where(
        lane < HEAD_DIM // 2,
        pltpu.roll(v, PAIR - HEAD_DIM // 2, 1),
        pltpu.roll(v, HEAD_DIM // 2, 1),
    )


def layer_kernel(names, *refs):
    ns = dict(zip(names, refs))
    g = lambda key: ns[key]
    at = place()
    seq = at["seq"]
    x, cot, gains = g("x"), g("cot"), g("gains")
    tokens, width = x.shape
    third = g("de").shape[2] // 3
    ff = 3 * third
    length = tokens // 2
    half = WINDOW // 2
    scale = HEAD_DIM ** (-0.5)
    cos, sin, low, high = g("cos"), g("sin"), g("low"), g("high")
    n1, n2, q, kx, vx = g("n1"), g("n2"), g("q"), g("kx"), g("vx")
    blocks = tokens // 32

    def rows_of(i, n=32):
        return pl.ds(pl.multiple_of(i * n, n), n)

    spot = (at["core"], at["r"], at["p"], at["zh"], at["zl"])
    wj, wo, we, wc = g("wj"), g("wo"), g("we"), g("wc")
    g("bn")[spot] = g("gn")[...]
    g("bk")[spot] = wj[:, width : 2 * width]
    g("bv")[spot] = wj[:, 2 * width :]
    g("bq")[spot] = wj[:, :width]
    g("bo")[spot] = wo[...]
    for j in range(3):
        buf = g("bf%d" % j)
        buf[spot + (slice(None), slice(0, third))] = we[:, j * third : (j + 1) * third]
        buf[spot + (slice(None), slice(third, 2 * third))] = we[
            :, ff + j * third : ff + (j + 1) * third
        ]
        buf[spot + (slice(None), slice(2 * third, ff))] = wc[:, j * third : (j + 1) * third]

    @pl.when(seq == 0)
    def _():
        kx[:, :half] = jnp.zeros((2, half, width), HALF)
        vx[:, :half] = jnp.zeros((2, half, width), HALF)
        g("rim_in")[1] = jnp.zeros((2, 2, half, width), HALF)

    @pl.when(seq == 7)
    def _():
        kx[:, half + length :] = jnp.zeros((2, half, width), HALF)
        vx[:, half + length :] = jnp.zeros((2, half, width), HALF)
        g("rim_in")[0] = jnp.zeros((2, 2, half, width), HALF)

    meet(at)

    wj_all, wo_all, wf_all = g("wj_all"), g("wo_all"), g("wf_all")

    def into(ref, offset):
        def store(row, value):
            ref[row : row + 48, offset : offset + value.shape[1]] = value

        return store

    groups = [
        ("bn", None),
        ("bk", into(wj_all, width)),
        ("bv", into(wj_all, 2 * width)),
        ("bq", into(wj_all, 0)),
        ("bo", into(wo_all, 0)),
    ] + [("bf%d" % j, into(wf_all.at[j], 0)) for j in range(3)]
    events = sorted((i + 1.5 * s, i, s) for i in range(len(groups)) for s in range(6))
    copies = {}

    def gather_step():
        _, i, stage = events.pop(0)
        name, store = groups[i]
        if stage:
            copies.pop(i).wait()
        if stage < 5:
            copies[i] = gather_send(at, g(name), (g("g_send"), g("g_recv")), i, stage)
        elif store is None:
            relay_gains(g(name), gains)
        else:
            relay(g(name), store)

    def gather_some(count):
        for _ in range(min(count, len(events))):
            gather_step()

    def gather_until(index):
        while any(i == index for _, i, _ in events):
            gather_step()

    gather_some(3)

    lane = lax.broadcasted_iota(jnp.int32, (length, PAIR), 1)
    pos = (lax.broadcasted_iota(jnp.int32, (length, PAIR), 0) + seq * length).astype(F32)
    angle = pos * g("freq")[...]
    cos[...] = jnp.cos(angle)
    sign = jnp.where(lane % HEAD_DIM < HEAD_DIM // 2, -1.0, 1.0)
    sin[...] = jnp.sin(angle) * sign
    low[...] = jnp.where(lane < HEAD_DIM, 1.0, 0.0).astype(HALF)
    high[...] = jnp.where(lane < HEAD_DIM, 0.0, 1.0).astype(HALF)
    span = length + 2 * half
    key = lax.broadcasted_iota(jnp.int32, (span, 2 * length), 0) - half
    query = lax.broadcasted_iota(jnp.int32, (span, 2 * length), 1) % length
    key_pos = key + seq * length
    allowed = (jnp.abs(key - query) <= half) & (key_pos >= 0) & (key_pos < 8 * length)
    g("bias")[...] = jnp.where(allowed, 0.0, MASK_FILL)

    def centre(values):
        mean = jnp.mean(values, axis=-1, keepdims=True)
        shifted = values - mean
        inv = lax.rsqrt(jnp.mean(shifted * shifted, axis=-1, keepdims=True) + NORM_EPS)
        return shifted * inv, inv

    @pl.loop(0, blocks)
    def _(i):
        rows = rows_of(i)
        norm, inv = centre(x[rows].astype(F32))
        g("norm1")[rows] = norm
        g("inv1")[rows] = inv

    for c in range(0, width, 256):
        g("cot_t")[c : c + 256] = jnp.transpose(cot[:, c : c + 256].astype(F32)).astype(HALF)

    gather_until(0)

    for c in range(0, width, 256):
        value = g("norm1")[:, c : c + 256] * gains[0:1, c : c + 256]
        n1[:, c : c + 256] = value.astype(HALF)
        g("n1_t")[c : c + 256] = jnp.transpose(value).astype(HALF)

    halo_sems = (g("h_send"), g("h_recv"))

    def halo(ref, i):
        def left():
            src, dst = ref.at[:, half : 2 * half], ref.at[:, half + length :]
            return remote(src, dst, halo_sems, (i, 0), at["peers"]["left"])

        def right():
            src, dst = ref.at[:, length : length + half], ref.at[:, :half]
            return remote(src, dst, halo_sems, (i, 1), at["peers"]["right"])

        return left, right

    def exchange_start(sides):
        pl.when(seq > 0)(lambda: sides[0]().start())
        pl.when(seq < 7)(lambda: sides[1]().start())

    def exchange_wait(sides):
        left, right = sides

        @pl.when(seq > 0)
        def _():
            left().wait_send()
            right().wait_recv()

        @pl.when(seq < 7)
        def _():
            right().wait_send()
            left().wait_recv()

    def project(offset, store):
        @pl.loop(0, width // 256)
        def _(i):
            base = pl.multiple_of(i * 256, 256)
            value = dot(n1[...], wj_all[:, pl.ds(offset + base, 256)], NN)
            for b in range(2):
                for c in range(2):
                    store(
                        b,
                        pl.ds(base + c * PAIR, PAIR),
                        value[b * length : (b + 1) * length, c * PAIR : (c + 1) * PAIR],
                    )

    def turn(v):
        return v * cos[...] + swap_halves(v) * sin[...]

    def unturn(v):
        return v * cos[...] - swap_halves(v) * sin[...]

    def store_k(b, cols, v):
        kx[b, half : half + length, cols] = turn(v).astype(HALF)

    def store_v(b, cols, v):
        vx[b, half : half + length, cols] = v.astype(HALF)

    def store_q(b, cols, v):
        q[b * length : (b + 1) * length, cols] = turn(v).astype(HALF)

    gather_until(1)
    project(width, store_k)
    exchange_start(halo(kx, 0))
    gather_until(2)
    project(2 * width, store_v)
    exchange_start(halo(vx, 1))
    gather_until(3)
    project(0, store_q)
    gather_some(2)
    exchange_wait(halo(kx, 0))
    exchange_wait(halo(vx, 1))

    def stack_heads(v):
        return jnp.concatenate([v * low[...], v * high[...]], axis=0)

    lower = lax.broadcasted_iota(jnp.int32, (length, PAIR), 1) < HEAD_DIM

    def pick_heads(v):
        return jnp.where(lower, v[:length], v[length:])

    def attend(b, i):
        cols = pl.ds(pl.multiple_of(i * PAIR, PAIR), PAIR)
        rows = slice(b * length, (b + 1) * length)
        qs = stack_heads(q[rows, cols])
        scores = dot(kx[b, :, cols], qs, NT) * scale + g("bias")[...]
        top = jnp.max(scores, axis=0, keepdims=True)
        raised = jnp.exp(scores - top)
        total = jnp.sum(raised, axis=0, keepdims=True)
        probs = raised * (1.0 / total)
        g("stat")[b * pairs + i] = top + jnp.log(total)
        g("att")[rows, cols] = pick_heads(dot(probs.astype(HALF), vx[b, :, cols], TN)).astype(HALF)

    pairs = width // PAIR
    for b in range(2):
        for start in range(0, pairs, 2):
            pl.loop(start, start + 2)(functools.partial(attend, b))
            gather_some(1)

    gather_until(4)

    resid = g("resid")

    @pl.loop(0, width // 256)
    def _(i):
        cols = pl.ds(pl.multiple_of(i * 256, 256), 256)
        resid[:, cols] = x[:, cols].astype(F32) + dot(g("att")[...], wo_all[:, cols], NN)

    @pl.loop(0, blocks)
    def _(i):
        rows = rows_of(i)
        norm, inv = centre(resid[rows])
        g("norm2")[rows] = norm
        g("inv2")[rows] = inv
        n2[rows] = (norm * gains[1:2]).astype(HALF)

    for c in range(0, width, 256):
        g("n2_t")[c : c + 256] = jnp.transpose(n2[:, c : c + 256].astype(F32)).astype(HALF)

    offsets = (("o_o", 0), ("o_j", 0), ("o_j", 2 * width), ("o_j", width))

    def run_sum(index, stage):
        size = ff if index < 3 else width

        def emit(value):
            if index < 3:
                j = index * third
                g("o_e")[:, j : j + third] = value[:, :third]
                g("o_e")[:, ff + j : ff + j + third] = value[:, third : 2 * third]
                g("o_c")[:, j : j + third] = value[:, 2 * third :]
            else:
                name, offset = offsets[index - 3]
                g(name)[:, offset : offset + width] = value

        bufs = [g("r%d_%d" % (k, index)) for k in range(5)]
        bufs += [g("bf0").at[0, index % 2], g("bf1").at[0, index % 2, 0]]
        bufs += [g("s%d" % k).at[index % 2] for k in range(3, 5)]
        return sum_stage(
            at,
            stage,
            g("grads").at[index % 2],
            bufs,
            (g("s_send"), g("s_recv")),
            index,
            size,
            emit,
        )

    sums = Sums(run_sum)

    def weight_grad(index, offset, left, right, columns):
        @pl.loop(0, columns // 384)
        def _(i):
            base = pl.multiple_of(i * 384, 384)
            g("grads")[index % 2, :, pl.ds(offset + base, 384)] = dot(
                left[...], right[:, pl.ds(base, 384)], NN
            )

    e, de, dn = g("e"), g("de"), g("dn")
    for j in range(3):
        gather_until(5 + j)
        w = wf_all.at[j]
        for c in range(0, 2 * third, third):
            e[:, c : c + third] = dot(n2[...], w[:, c : c + third], NN)
        e[:, 2 * third :] = dot(cot[...], w[:, 2 * third :], NN)

        @pl.loop(0, blocks)
        def _(i):
            rows = rows_of(i)
            pre, gate, d_mixed = (e[rows, c * third : (c + 1) * third] for c in range(3))
            cumul = 0.5 * (1.0 + lax.erf(pre * SQRT_HALF))
            active = pre * cumul
            slope = cumul + pre * jnp.exp(-0.5 * pre * pre) * INV_ROOT_TAU
            de[j, rows, :third] = (d_mixed * gate * slope).astype(HALF)
            de[j, rows, third : 2 * third] = (d_mixed * active).astype(HALF)
            de[j, rows, 2 * third :] = (active * gate).astype(HALF)

        if j == 2:
            sums.reach(0, 1)
        weight_grad(j, 0, g("n2_t"), de.at[j], 2 * third)
        weight_grad(j, 2 * third, g("cot_t"), de.at[j, :, 2 * third :], third)
        sums.add(j)
        back = dot(de[j, :, : 2 * third], w[:, : 2 * third], NT)
        dn[...] = back if j == 0 else dn[...] + back
        sums.pump()

    def norm_down(upstream, norm, inv, gain):
        scaled = upstream * gain
        mean = jnp.mean(scaled, axis=-1, keepdims=True)
        along = jnp.mean(scaled * norm, axis=-1, keepdims=True)
        return inv * (scaled - mean - norm * along)

    part = g("part")
    part[...] = jnp.zeros(part.shape, F32)

    def fold(v):
        return sum(v[k : k + 8] for k in range(0, 32, 8))

    @pl.loop(0, blocks)
    def _(i):
        rows = rows_of(i)
        up, norm = dn[rows], g("norm2")[rows]
        part[1] += fold(up * norm)
        d_resid = cot[rows].astype(F32) + norm_down(up, norm, g("inv2")[rows], gains[1:2])
        dn[rows] = d_resid
        n1[rows] = d_resid.astype(HALF)

    sums.pump()

    @pl.loop(0, width // 256)
    def _(i):
        rows = pl.ds(pl.multiple_of(i * 256, 256), 256)
        n2[:, rows] = dot(n1[...], wo_all[rows, :], NT).astype(HALF)

    sums.reach(1, 1)

    @pl.loop(0, width // 256)
    def _(i):
        cols = pl.ds(pl.multiple_of(i * 256, 256), 256)
        g("grads")[1, cols, :width] = dot(g("att")[:, cols], n1[...], TN)

    sums.add(3)

    rim_out, rim_in = g("rim_out"), g("rim_in")
    dj = g("dj")

    def attend_back(b, i):
        cols = pl.ds(pl.multiple_of(i * PAIR, PAIR), PAIR)
        rows = slice(b * length, (b + 1) * length)
        qs = stack_heads(q[rows, cols])
        ups = stack_heads(n2[rows, cols])
        scores = dot(kx[b, :, cols], qs, NT) * scale + g("bias")[...]
        probs = jnp.exp(scores - g("stat")[b * pairs + i])
        d_probs = dot(vx[b, :, cols], ups, NT)
        centred = d_probs - jnp.sum(probs * d_probs, axis=0, keepdims=True)
        d_scores = (probs * centred * scale).astype(HALF)
        d_q = pick_heads(dot(d_scores, kx[b, :, cols], TN))
        dj[rows, cols] = unturn(d_q).astype(HALF)
        for k, (value, own) in enumerate(
            ((dot(d_scores, qs, NN), g("norm2")), (dot(probs.astype(HALF), ups, NN), g("dv")))
        ):
            own[rows, cols] = value[half : half + length]
            rim_out[0, k, b, :, cols] = value[:half].astype(HALF)
            rim_out[1, k, b, :, cols] = value[half + length :].astype(HALF)

    for b in range(2):
        for start in range(0, pairs, 2):
            pl.loop(start, start + 2)(functools.partial(attend_back, b))
            sums.pump(2)

    rim_sems = (g("m_send"), g("m_recv"))

    rims = (
        lambda: remote(rim_out.at[0], rim_in.at[0], rim_sems, (0,), at["peers"]["left"]),
        lambda: remote(rim_out.at[1], rim_in.at[1], rim_sems, (1,), at["peers"]["right"]),
    )

    exchange_start(rims)
    sums.reach(2, 1)
    weight_grad(4, 0, g("n1_t"), dj, width)
    sums.add(4)
    sums.pump()
    back = dot(dj[:, :width], wj_all[:, :width], NT)
    e[:, :width] = back
    exchange_wait(rims)

    def settle(k, own, finish, offset):
        @pl.loop(0, pairs)
        def _(i):
            cols = pl.ds(pl.multiple_of(i * PAIR, PAIR), PAIR)
            out_cols = pl.ds(pl.multiple_of(offset + i * PAIR, PAIR), PAIR)
            for b in range(2):
                rows = slice(b * length, (b + 1) * length)
                edge = jnp.concatenate([rim_in[1, k, b, :, cols], rim_in[0, k, b, :, cols]], axis=0)
                dj[rows, out_cols] = finish(own[rows, cols] + edge.astype(F32)).astype(HALF)

    settle(1, g("dv"), lambda v: v, 2 * width)
    sums.reach(3, 1)
    weight_grad(5, 0, g("n1_t"), dj.at[:, 2 * width :], width)
    sums.add(5)
    settle(0, g("norm2"), unturn, width)
    sums.reach(4, 1)
    weight_grad(6, 0, g("n1_t"), dj.at[:, width : 2 * width], width)
    sums.add(6)
    sums.pump()
    e[:, :width] = e[:, :width] + dot(dj[:, width:], wj_all[:, width:], NT)
    sums.pump()

    @pl.loop(0, blocks)
    def _(i):
        rows = rows_of(i)
        up, norm = e[rows, :width], g("norm1")[rows]
        part[0] += fold(up * norm)
        d_source = norm_down(up, norm, g("inv1")[rows], gains[0:1])
        g("grad")[rows] = (dn[rows] + d_source).astype(HALF)

    gain_sum, gain_in = g("gain_sum"), g("gain_in")
    gain_sum[0] = jnp.zeros(gain_sum.shape[1:], F32)
    for k in range(2):
        gain_sum[0, k : k + 1] = jnp.sum(part[k], axis=0, keepdims=True)
    gain_sems = (g("n_send"), g("n_recv"))

    def gain_push(t):
        peer = at["peers"][GAIN_PATH[t]]
        return push(gain_sum.at[t], gain_in.at[t], gain_sems, (t,), peer)

    moving = gain_push(0)

    @pl.loop(0, width // 256)
    def _(i):
        cols = pl.ds(pl.multiple_of(i * 256, 256), 256)
        value = resid[:, cols]
        for j in range(3):
            value = value + dot(de[j, :, 2 * third :], wf_all[j, cols, 2 * third :], NT)
        g("out")[:, cols] = value.astype(HALF)

    for t in range(5):
        sums.pump(2)
        moving.wait()
        gain_sum[t + 1] = gain_sum[t] + gain_in[t]
        if t < 4:
            moving = gain_push(t + 1)
    shift = ((32 - (at["dp"] * 8 + seq)) * ROWS) % width
    g("o_n")[...] = pltpu.roll(gain_sum[5], shift, 1)[:, :128]
    sums.drain()


def fused_layer(x, cot, wj, wo, we, wc, gn, freq):
    tokens, width = x.shape
    ff = wc.shape[1]
    length = tokens // 2
    half = WINDOW // 2
    span = length + 2 * half
    pairs = width // PAIR
    lead = (2, 2, 2, 2, 2, ROWS)
    ins = dict(x=x, cot=cot, wj=wj, wo=wo, we=we, wc=wc, gn=gn, freq=freq)
    outs = dict(
        out=((tokens, width), HALF),
        grad=((tokens, width), HALF),
        o_e=((ROWS, 2 * ff), F32),
        o_c=((ROWS, ff), F32),
        o_o=((ROWS, width), F32),
        o_j=((ROWS, 3 * width), F32),
        o_n=((8, 128), F32),
    )
    held = dict(bn=((2, 2, 2, 2, 2, 8, 128), F32))
    for name in ("bk", "bv", "bq", "bo"):
        held[name] = (lead + (width,), HALF)
    for j in range(3):
        held["bf%d" % j] = (lead + (ff,), HALF)
    held.update(
        wj_all=((width, 3 * width), HALF),
        wo_all=((width, width), HALF),
        wf_all=((3, width, ff), HALF),
        gains=((8, width), F32),
        cos=((length, PAIR), F32),
        sin=((length, PAIR), F32),
        low=((length, PAIR), HALF),
        high=((length, PAIR), HALF),
        bias=((span, 2 * length), F32),
        norm1=((tokens, width), F32),
        inv1=((tokens, 1), F32),
        n1=((tokens, width), HALF),
        n1_t=((width, tokens), HALF),
        cot_t=((width, tokens), HALF),
        q=((tokens, width), HALF),
        kx=((2, span, width), HALF),
        vx=((2, span, width), HALF),
        stat=((2 * pairs, 1, 2 * length), F32),
        att=((tokens, width), HALF),
        resid=((tokens, width), F32),
        norm2=((tokens, width), F32),
        inv2=((tokens, 1), F32),
        n2=((tokens, width), HALF),
        n2_t=((width, tokens), HALF),
        e=((tokens, ff), F32),
        de=((3, tokens, ff), HALF),
        dn=((tokens, width), F32),
        part=((2, 8, width), F32),
        dv=((tokens, width), F32),
        dj=((tokens, 3 * width), HALF),
        rim_out=((2, 2, 2, half, width), HALF),
        rim_in=((2, 2, 2, half, width), HALF),
        gain_sum=((6, 8, width), F32),
        gain_in=((5, 8, width), F32),
        grads=((2, width, ff), F32),
        s3=((2, 2, ROWS, ff), F32),
        s4=((2, ROWS, ff), F32),
    )
    for i in range(7):
        size = ff if i < 3 else width
        held["r0_%d" % i] = ((2, 8 * ROWS, size), F32)
        held["r1_%d" % i] = ((2, 2, 2, ROWS, size), HALF)
        held["r2_%d" % i] = ((2, 2, ROWS, size), HALF)
        held["r3_%d" % i] = ((2, ROWS, size), F32)
        held["r4_%d" % i] = ((ROWS, size), F32)
    sems = {}
    for side in ("send", "recv"):
        sems["g_" + side] = (8, 5)
        sems["h_" + side] = (2, 2)
        sems["s_" + side] = (7, 6)
        sems["m_" + side] = (2,)
        sems["n_" + side] = (5,)
    vmem = pl.BlockSpec(memory_space=pltpu.VMEM)
    names = tuple(ins) + tuple(outs) + tuple(held) + tuple(sems)
    return pl.pallas_call(
        functools.partial(layer_kernel, names),
        out_shape=tuple(jax.ShapeDtypeStruct(*v) for v in outs.values()),
        in_specs=[vmem] * len(ins),
        out_specs=(vmem,) * len(outs),
        scratch_shapes=[pltpu.VMEM(*v) for v in held.values()]
        + [pltpu.SemaphoreType.DMA(v) for v in sems.values()],
        compiler_params=pltpu.CompilerParams(
            collective_id=0, has_side_effects=True, vmem_limit_bytes=VMEM_LIMIT
        ),
    )(*ins.values())


VMEM_LIMIT = 63 * MIB


def fast_layer(
    layer_input, cotangent, w_joined, w_output, w_expand, w_contract, gain_one, gain_two
):
    width = layer_input.shape[-1]
    tokens = layer_input.shape[0] * layer_input.shape[1] * layer_input.shape[2]
    gains = jnp.pad(
        jnp.stack([gain_one, gain_two]).astype(F32), ((0, 6), (0, 128 - gain_one.shape[0]))
    )
    half_dim = HEAD_DIM // 2
    freqs = ROPE_BASE ** (-jnp.arange(half_dim).astype(F32) * 2.0 / HEAD_DIM)
    freq = jnp.tile(freqs, PAIR // half_dim)[None, :]
    out, grad, o_e, o_c, o_o, o_j, o_n = fused_layer(
        layer_input.reshape(tokens, width),
        cotangent.reshape(tokens, width),
        w_joined,
        w_output,
        w_expand,
        w_contract.T,
        gains,
        freq,
    )
    count = gain_one.shape[0]
    return (
        out.reshape(layer_input.shape),
        grad.reshape(layer_input.shape),
        o_j,
        o_o,
        o_e,
        o_c.T,
        o_n[0, :count],
        o_n[1, :count],
    )


def solution(mesh):
    fits = mesh.shape["dp"] == 4 and mesh.shape["seq"] == 8
    body = fast_layer if fits else plain_layer
    placed = (
        P(None, "dp", "seq", None),
        P(None, "dp", "seq", None),
        P(("dp", "seq"), None),
        P(("dp", "seq"), None),
        P(("dp", "seq"), None),
        P(None, ("dp", "seq")),
        P(("dp", "seq")),
        P(("dp", "seq")),
    )
    return jax.shard_map(
        body,
        mesh=mesh,
        in_specs=placed,
        out_specs=(
            P(None, "dp", "seq", None),
            P(None, "dp", "seq", None),
            P(("dp", "seq"), None),
            P(("dp", "seq"), None),
            P(("dp", "seq"), None),
            P(None, ("dp", "seq")),
            P(("dp", "seq")),
            P(("dp", "seq")),
        ),
        check_vma=False,
    )
```

```python
import functools

import jax
import jax.numpy as jnp
from jax import lax
from jax.experimental import pallas as pl
from jax.experimental.pallas import tpu as pltpu
from jax.sharding import PartitionSpec as P

HEADS = 12
HEAD_DIM = 64
WINDOW = 128


NORM_EPS = 1e-05
ROPE_BASE = 10000.0
MASK_FILL = -1e30
SQRT_HALF = 0.7071067811865476
INV_ROOT_TAU = 0.3989422804014327


LANES = 128


def pair_sum(value, outer):
    outer_size = lax.axis_size(outer)
    pairs = outer_size // 2
    core = lax.axis_index(outer) % 2
    blocks = value.reshape(pairs, 2, value.shape[0] // outer_size, value.shape[1])
    other = lax.dynamic_index_in_dim(blocks, 1 - core, axis=1, keepdims=False)
    own = lax.dynamic_index_in_dim(blocks, core, axis=1, keepdims=False)
    swap = [(i, i ^ 1) for i in range(outer_size)]
    return own + lax.ppermute(other, outer, swap)


def line_sum(value, outer):
    outer_size = lax.axis_size(outer)
    if outer_size == 4:
        line = lax.axis_index(outer) // 2
        other = lax.dynamic_index_in_dim(value, 1 - line, axis=0, keepdims=False)
        own = lax.dynamic_index_in_dim(value, line, axis=0, keepdims=False)
        swap = [(i, i ^ 2) for i in range(outer_size)]
        arrived = lax.ppermute(other.astype(jnp.bfloat16), outer, swap)
        value = own + arrived.astype(jnp.float32)
    else:
        groups = [list(range(c, outer_size, 2)) for c in range(2)]
        arrived = lax.all_to_all(
            value.astype(jnp.bfloat16), outer, 0, 0, axis_index_groups=groups
        )
        value = jnp.sum(arrived.astype(jnp.float32), axis=0)
    return value


def ring_sum(value, inner):
    inner_size = lax.axis_size(inner)
    blocks = value.reshape(inner_size, value.shape[0] // inner_size, value.shape[1])
    return jnp.sum(lax.all_to_all(blocks, inner, 0, 0), axis=0)


def norm_apply(values, gain):
    center = jnp.mean(values, axis=-1, keepdims=True)
    shifted = values - center
    inv_std = lax.rsqrt(jnp.mean(shifted * shifted, axis=-1, keepdims=True) + NORM_EPS)
    normed = shifted * inv_std
    return (normed * gain.astype(jnp.float32), normed, inv_std)


def norm_back(upstream, normed, inv_std, gain):
    scaled = upstream * gain.astype(jnp.float32)
    inner = (
        scaled
        - jnp.mean(scaled, axis=-1, keepdims=True)
        - normed * jnp.mean(scaled * normed, axis=-1, keepdims=True)
    )
    return (inv_std * inner, jnp.sum(upstream * normed, axis=(0, 1)))


def gelu_slope(values):
    cumul = 0.5 * (1.0 + jax.scipy.special.erf(values * SQRT_HALF))
    return cumul + values * jnp.exp(-0.5 * values * values) * INV_ROOT_TAU


def rope_tables(positions, head_dim):
    half_dim = head_dim // 2
    freqs = ROPE_BASE ** (-jnp.arange(half_dim).astype(jnp.float32) * 2.0 / head_dim)
    angles = positions.astype(jnp.float32)[:, None] * freqs[None, :]
    return (jnp.cos(angles)[:, None, :], jnp.sin(angles)[:, None, :])


def rotate(values, cosine, sine):
    half_dim = values.shape[-1] // 2
    first = values[..., :half_dim]
    second = values[..., half_dim:]
    return jnp.concatenate(
        [first * cosine - second * sine, second * cosine + first * sine], axis=-1
    )


def unrotate(values, cosine, sine):
    half_dim = values.shape[-1] // 2
    first = values[..., :half_dim]
    second = values[..., half_dim:]
    return jnp.concatenate(
        [first * cosine + second * sine, second * cosine - first * sine], axis=-1
    )


def plain_layer(
    layer_input, cotangent, w_joined, w_output, w_expand, w_contract, gain_one, gain_two
):
    micro, local_batch, group, width = layer_input.shape
    heads = HEADS
    head_dim = HEAD_DIM
    half = WINDOW // 2
    ffn = w_contract.shape[0]
    batch = micro * local_batch
    scale = head_dim ** (-0.5)
    axes = ("dp", "seq")
    seq_count = lax.axis_size("seq")
    up = [(i, i + 1) for i in range(seq_count - 1)]
    down = [(j, i) for i, j in up]
    group_start = lax.axis_index("seq") * group
    cosine, sine = rope_tables(group_start + jnp.arange(group, dtype=jnp.int32), head_dim)
    query_pos = group_start + jnp.arange(group, dtype=jnp.int32)[:, None]
    key_pos = group_start - half + jnp.arange(group + 2 * half, dtype=jnp.int32)[None, :]
    allowed = (
        (jnp.abs(query_pos - key_pos) <= half) & (key_pos >= 0) & (key_pos < group * seq_count)
    )
    gains = jnp.pad(jnp.stack([gain_one, gain_two], axis=1), ((0, 0), (0, LANES - 2)))
    pack_one = jnp.concatenate([w_joined, gains], axis=1)
    pack_two = jnp.concatenate([w_expand, w_contract.T, w_output], axis=1)
    full_one = lax.all_gather(pack_one, axes, axis=0, tiled=True)
    full_two = lax.all_gather(pack_two, axes, axis=0, tiled=True)
    full_joined = full_one[:, : 3 * width]
    full_gain_one = full_one[:, 3 * width]
    full_gain_two = full_one[:, 3 * width + 1]
    full_expand = full_two[:, : 2 * ffn]
    full_contract = full_two[:, 2 * ffn : 3 * ffn]
    full_output = full_two[:, 3 * ffn :]

    source32 = layer_input.reshape(batch, group, width).astype(jnp.float32)
    upstream_half = cotangent.reshape(batch, group, width)
    normed_f, norm_one, inv_one = norm_apply(source32, full_gain_one)
    normed_one = normed_f.astype(jnp.bfloat16)
    joined = jnp.einsum(
        "bcd,de->bce", normed_one, full_joined, preferred_element_type=jnp.float32
    )
    shape_heads = (batch, group, heads, head_dim)
    k_rot = rotate(joined[..., width : 2 * width].reshape(shape_heads), cosine, sine).astype(
        jnp.bfloat16
    )
    v_half = joined[..., 2 * width :].astype(jnp.bfloat16)
    key_value = jnp.stack([k_rot.reshape(batch, group, width), v_half])
    before = lax.ppermute(key_value[:, :, group - half :], "seq", up)
    after = lax.ppermute(key_value[:, :, :half], "seq", down)
    q_rot = rotate(joined[..., :width].reshape(shape_heads), cosine, sine).astype(jnp.bfloat16)
    extended = jnp.concatenate([before, key_value, after], axis=2)
    ext_shape = (batch, group + 2 * half, heads, head_dim)
    key_rows = extended[0].reshape(ext_shape)
    value_rows = extended[1].reshape(ext_shape)
    scores = (
        jnp.einsum("bqhd,bkhd->bhqk", q_rot, key_rows, preferred_element_type=jnp.float32)
        * scale
    )
    scores = jnp.where(allowed[None, None], scores, MASK_FILL)
    row_max = jnp.max(scores, axis=-1, keepdims=True)
    log_total = row_max + jnp.log(jnp.sum(jnp.exp(scores - row_max), axis=-1, keepdims=True))
    probs = jnp.exp(scores - log_total)
    probs_half = probs.astype(jnp.bfloat16)
    attended = jnp.einsum(
        "bhqk,bkhd->bqhd", probs_half, value_rows, preferred_element_type=jnp.float32
    )
    attended = attended.astype(jnp.bfloat16).reshape(batch, group, width)
    resid = source32 + jnp.einsum(
        "bcd,de->bce", attended, full_output, preferred_element_type=jnp.float32
    )
    normed_g, norm_two, inv_two = norm_apply(resid, full_gain_two)
    normed_two = normed_g.astype(jnp.bfloat16)
    expanded = jnp.einsum(
        "bcd,de->bce", normed_two, full_expand, preferred_element_type=jnp.float32
    )
    pre_act = expanded[..., :ffn]
    gate_part = expanded[..., ffn:]
    activated = jax.nn.gelu(pre_act, approximate=False)
    mixed = (activated * gate_part).astype(jnp.bfloat16)
    contract_acc = jnp.einsum(
        "bcd,bcf->df", upstream_half, mixed, preferred_element_type=jnp.float32
    )
    d_mixed = jnp.einsum(
        "bcd,df->bcf", upstream_half, full_contract, preferred_element_type=jnp.float32
    )
    d_expanded = jnp.concatenate(
        [d_mixed * gate_part * gelu_slope(pre_act), d_mixed * activated], axis=-1
    ).astype(jnp.bfloat16)
    expand_acc = jnp.einsum(
        "bcd,bce->de", normed_two, d_expanded, preferred_element_type=jnp.float32
    )
    ffn_grads, d_expanded = lax.optimization_barrier(
        (jnp.concatenate([expand_acc, contract_acc], axis=1), d_expanded)
    )
    ffn_pair = pair_sum(ffn_grads, "dp")
    d_normed_two = jnp.einsum(
        "bce,de->bcd", d_expanded, full_expand, preferred_element_type=jnp.float32
    )
    d_resid_n, gain_two_part = norm_back(d_normed_two, norm_two, inv_two, full_gain_two)
    d_resid = upstream_half.astype(jnp.float32) + d_resid_n
    d_resid_half = d_resid.astype(jnp.bfloat16)
    ffn_pair, d_resid_half = lax.optimization_barrier((ffn_pair, d_resid_half))
    ffn_line = line_sum(ffn_pair, "dp")
    d_attended = jnp.einsum(
        "bce,de->bcd", d_resid_half, full_output, preferred_element_type=jnp.float32
    )
    d_attended = d_attended.astype(jnp.bfloat16).reshape(shape_heads)
    d_probs = jnp.einsum(
        "bqhd,bkhd->bhqk", d_attended, value_rows, preferred_element_type=jnp.float32
    )
    centred = d_probs - jnp.sum(probs * d_probs, axis=-1, keepdims=True)
    d_scores = (probs * centred * scale).astype(jnp.bfloat16)
    d_key_ext = jnp.einsum(
        "bhqk,bqhd->bkhd", d_scores, q_rot, preferred_element_type=jnp.float32
    )
    d_value_ext = jnp.einsum(
        "bhqk,bqhd->bkhd", probs_half, d_attended, preferred_element_type=jnp.float32
    )
    ext_grads = jnp.stack(
        [
            d_key_ext.reshape(batch, group + 2 * half, width),
            d_value_ext.reshape(batch, group + 2 * half, width),
        ]
    )
    rims = ext_grads.astype(jnp.bfloat16)
    ffn_line, rims = lax.optimization_barrier((ffn_line, rims))
    ffn_sum = ring_sum(ffn_line, "seq")
    from_left = lax.ppermute(rims[:, :, group + half :], "seq", up).astype(jnp.float32)
    from_right = lax.ppermute(rims[:, :, :half], "seq", down).astype(jnp.float32)
    d_query = jnp.einsum(
        "bhqk,bkhd->bqhd", d_scores, key_rows, preferred_element_type=jnp.float32
    )
    output_acc = jnp.einsum(
        "bcd,bce->de", attended, d_resid_half, preferred_element_type=jnp.float32
    )
    final = resid + jnp.einsum(
        "bcf,df->bcd", mixed, full_contract, preferred_element_type=jnp.float32
    )
    own_grads = ext_grads[:, :, half : half + group]
    own_grads = own_grads + jnp.pad(
        from_left, ((0, 0), (0, 0), (0, group - half), (0, 0))
    ) + jnp.pad(from_right, ((0, 0), (0, 0), (group - half, 0), (0, 0)))
    d_key = unrotate(own_grads[0].reshape(shape_heads), cosine, sine).reshape(
        batch, group, width
    )
    d_query_flat = unrotate(d_query, cosine, sine).reshape(batch, group, width)
    d_joined = jnp.concatenate([d_query_flat, d_key, own_grads[1]], axis=-1).astype(
        jnp.bfloat16
    )
    d_normed_one = jnp.einsum(
        "bce,de->bcd", d_joined, full_joined, preferred_element_type=jnp.float32
    )
    d_source, gain_one_part = norm_back(d_normed_one, norm_one, inv_one, full_gain_one)
    input_grad = (d_resid + d_source).astype(jnp.bfloat16)
    joined_acc = jnp.einsum(
        "bcd,bce->de", normed_one, d_joined, preferred_element_type=jnp.float32
    )
    gain_parts = jnp.pad(
        jnp.stack([gain_one_part, gain_two_part], axis=1), ((0, 0), (0, LANES - 2))
    )
    last_grads = jnp.concatenate([joined_acc, output_acc, gain_parts], axis=1)
    last_sum = ring_sum(line_sum(pair_sum(last_grads, "dp"), "dp"), "seq")
    return (
        final.astype(jnp.bfloat16).reshape(layer_input.shape),
        input_grad.reshape(layer_input.shape),
        last_sum[:, : 3 * width],
        last_sum[:, 3 * width : 4 * width],
        ffn_sum[:, : 2 * ffn],
        ffn_sum[:, 2 * ffn :].T,
        last_sum[:, 4 * width],
        last_sum[:, 4 * width + 1],
    )


MESH = pl.DeviceIdType.MESH
ROWS = 24
MIB = 2**20
F32 = jnp.float32
HALF = jnp.bfloat16
PAIR = 128


def place():
    dp, seq = lax.axis_index("dp"), lax.axis_index("seq")
    y, core = dp // 2, dp % 2
    z, x = seq // 2, seq % 2
    zh, zl = z // 2, z % 2
    r = x * (1 - core) + y * core
    p = y * (1 - core) + x * core
    peers = dict(
        pair=(dp + 1 - 2 * core, seq),
        r=(dp + 2 * core * (1 - 2 * y), seq + (1 - core) * (1 - 2 * x)),
        p=(dp + 2 * (1 - core) * (1 - 2 * y), seq + core * (1 - 2 * x)),
        zl=(dp, seq + 2 - 4 * zl),
        zh=(dp, seq + 4 - 8 * zh),
        left=(dp, (seq + 7) % 8),
        right=(dp, (seq + 1) % 8),
    )
    return dict(dp=dp, seq=seq, core=core, zh=zh, zl=zl, r=r, p=p, peers=peers)


def meet(at):
    barrier = pltpu.get_barrier_semaphore()
    for peer in at["peers"].values():
        pl.semaphore_signal(barrier, inc=1, device_id=peer, device_id_type=MESH)
    pl.semaphore_wait(barrier, len(at["peers"]))


def remote(src, dst, sems, where, peer):
    send, recv = sems
    return pltpu.make_async_remote_copy(
        src_ref=src,
        dst_ref=dst,
        send_sem=send.at[where],
        recv_sem=recv.at[where],
        device_id=peer,
        device_id_type=MESH,
    )


def push(*args):
    copy = remote(*args)
    copy.start()
    return copy


def gather_send(at, buf, sems, group, stage):
    c, r, p, zh, zl = at["core"], at["r"], at["p"], at["zh"], at["zl"]
    name, ref = (
        ("zh", lambda: buf.at[c, r, p, zh, zl]),
        ("zl", lambda: buf.at[c, r, p, :, zl]),
        ("p", lambda: buf.at[c, r, p]),
        ("r", lambda: buf.at[c, r]),
        ("pair", lambda: buf.at[c]),
    )[stage]
    return push(ref(), ref(), sems, (group, stage), at["peers"][name])


def plane_index(core, y, z, x):
    r, p = (x, y) if core == 0 else (y, x)
    return core, r, p, z // 2, z % 2


def relay(buf, store):
    for core in range(2):
        for y in range(2):
            for z in range(4):
                blocks = [buf[plane_index(core, y, z, x)].astype(F32) for x in range(2)]
                store(y * 384 + core * 192 + z * 48, jnp.concatenate(blocks, axis=0).astype(HALF))


def relay_gains(buf, gains):
    width = gains.shape[1]
    total = jnp.zeros((8, width), F32)
    for core in range(2):
        for y in range(2):
            for z in range(4):
                for x in range(2):
                    block = buf[plane_index(core, y, z, x)]
                    wide = jnp.concatenate([block, jnp.zeros((8, width - 128), F32)], axis=1)
                    shift = ROWS * (y * 16 + core * 8 + z * 2 + x)
                    total = total + (pltpu.roll(wide, shift, 1) if shift else wide)
    gains[...] = total


def block_row(at, p, z, r):
    core = at["core"]
    y = p * (1 - core) + r * core
    x = r * (1 - core) + p * core
    return y, pl.multiple_of(z * 48 + x * ROWS, 8)


def sum_stage(at, stage, grads, bufs, sems, index, width, emit):
    r0, r1, r2, r3, r4, s1, s2, s3, s4 = bufs
    core, r, p, zh, zl = at["core"], at["r"], at["p"], at["zh"], at["zl"]
    peers = at["peers"]
    w = slice(0, width)

    def kept(pp, z):
        y, row = block_row(at, pp, z, r)
        return y, pl.ds(row, ROWS)

    if stage == 0:
        copies = []
        for y in range(2):
            rows = pl.ds(pl.multiple_of(y * 384 + (1 - core) * 192, 192), 192)
            copies.append(push(grads.at[rows, w], r0.at[y], sems, (index, y), peers["pair"]))
        return copies
    if stage == 1:

        @pl.loop(0, 8)
        def _(i):
            pp, z = i // 4, i % 4
            y, row = block_row(at, pp, z, 1 - r)
            base = pl.multiple_of(y * 384 + core * 192 + row, 8)
            s1[pp, z // 2, z % 2, :, w] = (grads[pl.ds(base, ROWS), w] + r0[y, pl.ds(row, ROWS)]).astype(HALF)
            y, rows = kept(pp, z)
            base = pl.multiple_of(y * 384 + core * 192 + rows.start, 8)
            r0[y, rows] = grads[pl.ds(base, ROWS), w] + r0[y, rows]

        return [push(s1.at[:, :, :, :, w], r1, sems, (index, 2), peers["r"])]
    if stage == 2:

        @pl.loop(0, 4)
        def _(z):
            zh, zl = z // 2, z % 2
            s2[zh, zl, :, w] = (r0[kept(1 - p, z)] + r1[1 - p, zh, zl].astype(F32)).astype(HALF)
            r0[kept(p, z)] = r0[kept(p, z)] + r1[p, zh, zl].astype(F32)

        return [push(s2.at[:, :, :, w], r2, sems, (index, 3), peers["p"])]
    if stage == 3:
        for h in range(2):
            far, near = 2 * h + 1 - zl, 2 * h + zl
            s3[h, :, w] = r0[kept(p, far)] + r2[h, 1 - zl].astype(F32)
            r0[kept(p, near)] = r0[kept(p, near)] + r2[h, zl].astype(F32)
        return [push(s3.at[:, :, w], r3, sems, (index, 4), peers["zl"])]
    if stage == 4:
        s4[:, w] = r0[kept(p, 2 * (1 - zh) + zl)] + r3[1 - zh]
        return [push(s4.at[:, w], r4, sems, (index, 5), peers["zh"])]
    emit((r0[kept(p, 2 * zh + zl)] + r3[zh]) + r4[...])
    return []


GAIN_PATH = ("pair", "r", "p", "zl", "zh")


def dot(a, b, dims):
    return lax.dot_general(a, b, (dims, ((), ())), preferred_element_type=F32)


NN, NT, TN = ((1,), (0,)), ((1,), (1,)), ((0,), (0,))


def swap_halves(v):
    lane = lax.broadcasted_iota(jnp.int32, v.shape, 1) % HEAD_DIM
    return jnp.where(
        lane < HEAD_DIM // 2,
        pltpu.roll(v, PAIR - HEAD_DIM // 2, 1),
        pltpu.roll(v, HEAD_DIM // 2, 1),
    )


ORDER = (
    ('halo',), ('g', 0, 0), ('g', 1, 0), ('pre',), ('g', 0, 1), ('g', 2, 0), ('g', 1, 1),
    ('g', 3, 0), ('g', 0, 2), ('g', 2, 1), ('g', 4, 0), ('g', 1, 2), ('g', 3, 1), ('g', 5, 0),
    ('halow',), ('g', 2, 2), ('g', 0, 3), ('g', 4, 1), ('g', 6, 0), ('g', 1, 3), ('g', 3, 2),
    ('g', 2, 3), ('g', 0, 4), ('g', 5, 1), ('g', 7, 0), ('g', 0, 5), ('n1',), ('g', 4, 2),
    ('n1h',), ('g', 1, 4), ('g', 6, 1), ('g', 3, 3), ('g', 5, 2), ('g', 1, 5), ('proj', 'k'),
    ('g', 7, 1), ('g', 2, 4), ('g', 4, 3), ('g', 6, 2), ('g', 2, 5), ('proj', 'v'), ('g', 3, 4),
    ('g', 7, 2), ('g', 5, 3), ('g', 3, 5), ('proj', 'q'), ('att', 0), ('att', 1), ('att', 2),
    ('g', 4, 4), ('att', 3), ('att', 4), ('g', 6, 3), ('att', 5), ('g', 4, 5), ('oproj',),
    ('g', 7, 3), ('norm2',), ('g', 5, 4), ('g', 5, 5), ('fwd', 0), ('grad', 0), ('g', 6, 4),
    ('back', 0), ('g', 7, 4), ('s', 0, 1), ('g', 6, 5), ('fwd', 1), ('grad', 1), ('g', 7, 5),
    ('fwd', 2), ('grad', 2), ('back', 1), ('back', 2), ('s', 0, 2), ('norm2b',), ('s', 1, 1),
    ('grad', 3), ('datt',), ('attb', 0), ('s', 2, 1), ('attb', 1), ('s', 0, 3), ('attb', 2),
    ('attb', 3), ('attb', 4), ('attb', 5), ('s', 1, 2), ('s', 3, 1), ('grad', 4), ('grad', 5),
    ('backh',), ('s', 0, 4), ('backq',), ('s', 2, 2), ('backkv',), ('s', 4, 1), ('grad', 6),
    ('s', 1, 3), ('n', 0), ('final',), ('s', 3, 2), ('s', 5, 1), ('n', 1), ('s', 0, 5),
    ('s', 2, 3), ('n', 2), ('s', 4, 2), ('s', 6, 1), ('rim',), ('s', 1, 4), ('n', 3), ('s', 3, 3),
    ('n', 4), ('s', 5, 2), ('s', 2, 4), ('n', 5), ('s', 4, 3), ('s', 1, 5), ('s', 6, 2),
    ('s', 3, 4), ('s', 2, 5), ('rimw',), ('norm1b',), ('s', 4, 4), ('s', 5, 3), ('s', 3, 5),
    ('s', 6, 3), ('s', 4, 5), ('s', 5, 4), ('s', 6, 4), ('s', 5, 5), ('s', 6, 5),
)


def layer_kernel(names, *refs):
    ns = dict(zip(names, refs))
    g = lambda key: ns[key]
    at = place()
    seq = at["seq"]
    x, cot, gains = g("x"), g("cot"), g("gains")
    tokens, width = x.shape
    third = g("de").shape[2] // 3
    ff = 3 * third
    length = tokens // 2
    half = WINDOW // 2
    scale = HEAD_DIM ** (-0.5)
    cos, sin, low, high = g("cos"), g("sin"), g("low"), g("high")
    n1, n2, q, kx, vx = g("n1"), g("n2"), g("q"), g("kx"), g("vx")
    blocks = tokens // 32
    span = length + 2 * half
    pairs = width // PAIR

    def rows_of(i, n=32):
        return pl.ds(pl.multiple_of(i * n, n), n)

    spot = (at["core"], at["r"], at["p"], at["zh"], at["zl"])
    wj, wo, we, wc = g("wj"), g("wo"), g("we"), g("wc")
    g("bn")[spot] = g("gn")[...]
    g("bk")[spot] = wj[:, width : 2 * width]
    g("bv")[spot] = wj[:, 2 * width :]
    g("bq")[spot] = wj[:, :width]
    g("bo")[spot] = wo[...]
    for j in range(3):
        buf = g("bf%d" % j)
        buf[spot + (slice(None), slice(0, third))] = we[:, j * third : (j + 1) * third]
        buf[spot + (slice(None), slice(third, 2 * third))] = we[
            :, ff + j * third : ff + (j + 1) * third
        ]
        buf[spot + (slice(None), slice(2 * third, ff))] = wc[:, j * third : (j + 1) * third]

    xh, rim_in = g("xh"), g("rim_in")

    @pl.when(seq == 0)
    def _():
        xh[0] = jnp.zeros(xh.shape[1:], HALF)
        rim_in[0] = jnp.zeros(rim_in.shape[1:], HALF)

    @pl.when(seq == 7)
    def _():
        xh[1] = jnp.zeros(xh.shape[1:], HALF)
        rim_in[1] = jnp.zeros(rim_in.shape[1:], HALF)

    meet(at)

    wj_all, wo_all, wf_all = g("wj_all"), g("wo_all"), g("wf_all")

    def into(ref, offset):
        def store(row, value):
            ref[row : row + 48, offset : offset + value.shape[1]] = value

        return store

    groups = [
        ("bn", None),
        ("bk", into(wj_all, width)),
        ("bv", into(wj_all, 2 * width)),
        ("bq", into(wj_all, 0)),
        ("bo", into(wo_all, 0)),
    ] + [("bf%d" % j, into(wf_all.at[j], 0)) for j in range(3)]
    copies = {}
    tasks = {}

    def task(*name):
        def note(f):
            tasks[name] = f

        return note

    def gather_task(i, stage):
        def run():
            name, store = groups[i]
            if stage:
                copies.pop(i).wait()
            if stage < 5:
                copies[i] = gather_send(at, g(name), (g("g_send"), g("g_recv")), i, stage)
            elif store is None:
                relay_gains(g(name), gains)
            else:
                relay(g(name), store)

        return run

    for i in range(len(groups)):
        for stage in range(6):
            tasks["g", i, stage] = gather_task(i, stage)

    def centre(values):
        mean = jnp.mean(values, axis=-1, keepdims=True)
        shifted = values - mean
        inv = lax.rsqrt(jnp.mean(shifted * shifted, axis=-1, keepdims=True) + NORM_EPS)
        return shifted * inv, inv

    @task("pre")
    def _():
        lane = lax.broadcasted_iota(jnp.int32, (length, PAIR), 1)
        row = lax.broadcasted_iota(jnp.int32, (length, PAIR), 0)
        sign = jnp.where(lane % HEAD_DIM < HEAD_DIM // 2, -1.0, 1.0)
        beside = jnp.where(row < half, row - half, row + half)
        for k, offset in enumerate((row, beside)):
            angle = (offset + seq * length).astype(F32) * g("freq")[...]
            cos[k] = jnp.cos(angle)
            sin[k] = jnp.sin(angle) * sign
        low[...] = jnp.where(lane < HEAD_DIM, 1.0, 0.0).astype(HALF)
        high[...] = jnp.where(lane < HEAD_DIM, 0.0, 1.0).astype(HALF)
        key = lax.broadcasted_iota(jnp.int32, (span, 2 * length), 0)
        key = jnp.where(key < length, key, jnp.where(key < length + half, key - span + half, key - half))
        query = lax.broadcasted_iota(jnp.int32, (span, 2 * length), 1) % length
        key_pos = key + seq * length
        allowed = (jnp.abs(key - query) <= half) & (key_pos >= 0) & (key_pos < 8 * length)
        g("bias")[...] = jnp.where(allowed, 0.0, MASK_FILL)

        @pl.loop(0, blocks)
        def _(i):
            rows = rows_of(i)
            norm, inv = centre(x[rows].astype(F32))
            g("norm1")[rows] = norm
            g("inv1")[rows] = inv

        for c in range(0, width, 256):
            g("cot_t")[c : c + 256] = jnp.transpose(cot[:, c : c + 256].astype(F32)).astype(HALF)

    @task("n1")
    def _():
        for c in range(0, width, 256):
            value = g("norm1")[:, c : c + 256] * gains[0:1, c : c + 256]
            n1[:tokens, c : c + 256] = value.astype(HALF)
            g("n1_t")[c : c + 256, :tokens] = jnp.transpose(value).astype(HALF)

    @task("n1h")
    def _():
        for b in range(2):
            for side in range(2):
                rows = slice(tokens + b * length + side * half, tokens + b * length + (side + 1) * half)
                n1[rows] = (centre(xh[side, b].astype(F32))[0] * gains[0:1]).astype(HALF)
        for c in range(0, width, 256):
            value = n1[tokens:, c : c + 256].astype(F32)
            g("n1_t")[c : c + 256, tokens:] = jnp.transpose(value).astype(HALF)

    halo_sems = (g("h_send"), g("h_recv"))

    def halo(i, from_left, to_left, from_right, to_right):
        def left():
            return remote(to_left, from_right, halo_sems, (i, 0), at["peers"]["left"])

        def right():
            return remote(to_right, from_left, halo_sems, (i, 1), at["peers"]["right"])

        return left, right

    x_rows = x.reshape(2, length, width)
    x_halo = halo(0, xh.at[0], x_rows.at[:, :half], xh.at[1], x_rows.at[:, half:])

    def exchange_start(sides):
        pl.when(seq > 0)(lambda: sides[0]().start())
        pl.when(seq < 7)(lambda: sides[1]().start())

    def exchange_wait(sides):
        left, right = sides

        @pl.when(seq > 0)
        def _():
            left().wait_send()
            right().wait_recv()

        @pl.when(seq < 7)
        def _():
            right().wait_send()
            left().wait_recv()

    def project(offset, rows, store):
        @pl.loop(0, width // 256)
        def _(i):
            base = pl.multiple_of(i * 256, 256)
            value = dot(n1[:rows], wj_all[:, pl.ds(offset + base, 256)], NN)
            for b in range(rows // length):
                for c in range(2):
                    store(
                        b,
                        pl.ds(base + c * PAIR, PAIR),
                        value[b * length : (b + 1) * length, c * PAIR : (c + 1) * PAIR],
                    )

    def turn(v, k=0):
        return v * cos[k] + swap_halves(v) * sin[k]

    def unturn(v, k=0):
        return v * cos[k] - swap_halves(v) * sin[k]

    def store_k(b, cols, v):
        k = b // 2
        kx[b % 2, k * length : (k + 1) * length, cols] = turn(v, k).astype(HALF)

    def store_v(b, cols, v):
        k = b // 2
        vx[b % 2, k * length : (k + 1) * length, cols] = v.astype(HALF)

    def store_q(b, cols, v):
        q[b * length : (b + 1) * length, cols] = turn(v).astype(HALF)

    @task("halo")
    def _():
        exchange_start(x_halo)

    @task("halow")
    def _():
        exchange_wait(x_halo)

    @task("proj", "k")
    def _():
        project(width, 2 * tokens, store_k)

    @task("proj", "v")
    def _():
        project(2 * width, 2 * tokens, store_v)

    @task("proj", "q")
    def _():
        project(0, tokens, store_q)

    def stack_heads(v):
        return jnp.concatenate([v * low[...], v * high[...]], axis=0)

    lower = lax.broadcasted_iota(jnp.int32, (length, PAIR), 1) < HEAD_DIM

    def pick_heads(v):
        return jnp.where(lower, v[:length], v[length:])

    def attend(b, i):
        cols = pl.ds(pl.multiple_of(i * PAIR, PAIR), PAIR)
        rows = slice(b * length, (b + 1) * length)
        qs = stack_heads(q[rows, cols])
        scores = dot(kx[b, :, cols], qs, NT) * scale + g("bias")[...]
        top = jnp.max(scores, axis=0, keepdims=True)
        raised = jnp.exp(scores - top)
        total = jnp.sum(raised, axis=0, keepdims=True)
        probs = raised * (1.0 / total)
        g("stat")[b * pairs + i] = top + jnp.log(total)
        g("att")[rows, cols] = pick_heads(dot(probs.astype(HALF), vx[b, :, cols], TN)).astype(HALF)

    def some_pairs(f, j):
        per = pairs // 3
        return lambda: pl.loop(j % 3 * per, (j % 3 + 1) * per)(functools.partial(f, j // 3))

    for j in range(6):
        tasks["att", j] = some_pairs(attend, j)

    resid = g("resid")

    @task("oproj")
    def _():
        @pl.loop(0, width // 256)
        def _(i):
            cols = pl.ds(pl.multiple_of(i * 256, 256), 256)
            resid[:, cols] = x[:, cols].astype(F32) + dot(g("att")[...], wo_all[:, cols], NN)

    @task("norm2")
    def _():
        @pl.loop(0, blocks)
        def _(i):
            rows = rows_of(i)
            norm, inv = centre(resid[rows])
            g("norm2")[rows] = norm
            g("inv2")[rows] = inv
            n2[rows] = (norm * gains[1:2]).astype(HALF)

        for c in range(0, width, 256):
            g("n2_t")[c : c + 256] = jnp.transpose(n2[:, c : c + 256].astype(F32)).astype(HALF)

    offsets = (("o_o", 0), ("o_j", 0), ("o_j", 2 * width), ("o_j", width))

    def run_sum(index, stage):
        size = ff if index < 3 else width

        def emit(value):
            if index < 3:
                j = index * third
                g("o_e")[:, j : j + third] = value[:, :third]
                g("o_e")[:, ff + j : ff + j + third] = value[:, third : 2 * third]
                g("o_c")[:, j : j + third] = value[:, 2 * third :]
            else:
                name, offset = offsets[index - 3]
                g(name)[:, offset : offset + width] = value

        bufs = [g("r%d_%d" % (k, index)) for k in range(5)]
        bufs += [g("bf0").at[0, index % 2], g("bf1").at[0, index % 2, 0]]
        bufs += [g("s%d" % k).at[index % 2] for k in range(3, 5)]
        return sum_stage(
            at,
            stage,
            g("grads").at[index % 2],
            bufs,
            (g("s_send"), g("s_recv")),
            index,
            size,
            emit,
        )

    def sum_task(i, stage):
        def run():
            for copy in copies.pop(("s", i), ()):
                copy.wait()
            copies["s", i] = run_sum(i, stage)

        return run

    for i in range(7):
        for stage in range(1, 6):
            tasks["s", i, stage] = sum_task(i, stage)

    def weight_grad(index, offset, left, right, columns):
        @pl.loop(0, columns // 384)
        def _(i):
            base = pl.multiple_of(i * 384, 384)
            g("grads")[index % 2, :, pl.ds(offset + base, 384)] = dot(
                left[...], right[:, pl.ds(base, 384)], NN
            )

    e, de, dn = g("e"), g("de"), g("dn")

    def forward_third(j):
        w = wf_all.at[j]
        for c in range(0, 2 * third, third):
            e[:, c : c + third] = dot(n2[...], w[:, c : c + third], NN)
        e[:, 2 * third :] = dot(cot[...], w[:, 2 * third :], NN)

        @pl.loop(0, blocks)
        def _(i):
            rows = rows_of(i)
            pre, gate, d_mixed = (e[rows, c * third : (c + 1) * third] for c in range(3))
            cumul = 0.5 * (1.0 + lax.erf(pre * SQRT_HALF))
            active = pre * cumul
            slope = cumul + pre * jnp.exp(-0.5 * pre * pre) * INV_ROOT_TAU
            de[j, rows, :third] = (d_mixed * gate * slope).astype(HALF)
            de[j, rows, third : 2 * third] = (d_mixed * active).astype(HALF)
            de[j, rows, 2 * third :] = (active * gate).astype(HALF)

    def grad_third(j):
        weight_grad(j, 0, g("n2_t"), de.at[j], 2 * third)
        weight_grad(j, 2 * third, g("cot_t"), de.at[j, :, 2 * third :], third)
        sum_task(j, 0)()

    def back_third(j):
        back = dot(de[j, :, : 2 * third], wf_all[j, :, : 2 * third], NT)
        dn[...] = back if j == 0 else dn[...] + back

    for j in range(3):
        tasks["fwd", j] = functools.partial(forward_third, j)
        tasks["grad", j] = functools.partial(grad_third, j)
        tasks["back", j] = functools.partial(back_third, j)

    def norm_down(upstream, norm, inv, gain):
        scaled = upstream * gain
        mean = jnp.mean(scaled, axis=-1, keepdims=True)
        along = jnp.mean(scaled * norm, axis=-1, keepdims=True)
        return inv * (scaled - mean - norm * along)

    part = g("part")
    def fold(v):
        return sum(v[k : k + 8] for k in range(0, 32, 8))

    @task("norm2b")
    def _():
        part[...] = jnp.zeros(part.shape, F32)

        @pl.loop(0, blocks)
        def _(i):
            rows = rows_of(i)
            up, norm = dn[rows], g("norm2")[rows]
            part[1] += fold(up * norm)
            d_resid = cot[rows].astype(F32) + norm_down(up, norm, g("inv2")[rows], gains[1:2])
            dn[rows] = d_resid
            n1[rows] = d_resid.astype(HALF)

    @task("datt")
    def _():
        @pl.loop(0, width // 256)
        def _(i):
            rows = pl.ds(pl.multiple_of(i * 256, 256), 256)
            n2[:, rows] = dot(n1[:tokens], wo_all[rows, :], NT).astype(HALF)

    @task("grad", 3)
    def _():
        @pl.loop(0, width // 256)
        def _(i):
            cols = pl.ds(pl.multiple_of(i * 256, 256), 256)
            g("grads")[1, cols, :width] = dot(g("att")[:, cols], n1[:tokens], TN)

        sum_task(3, 0)()

    n1_own, n1_all = g("n1_t").at[:, :tokens], g("n1_t")

    def grad_joined(index, left, right):
        weight_grad(index, 0, left, right, width)
        sum_task(index, 0)()

    rim_out = g("rim_out")
    dq, dkv = g("dq"), g("dkv")

    def attend_back(b, i):
        cols = pl.ds(pl.multiple_of(i * PAIR, PAIR), PAIR)
        rows = slice(b * length, (b + 1) * length)
        qs = stack_heads(q[rows, cols])
        ups = stack_heads(n2[rows, cols])
        scores = dot(kx[b, :, cols], qs, NT) * scale + g("bias")[...]
        probs = jnp.exp(scores - g("stat")[b * pairs + i])
        d_probs = dot(vx[b, :, cols], ups, NT)
        centred = d_probs - jnp.sum(probs * d_probs, axis=0, keepdims=True)
        d_scores = (probs * centred * scale).astype(HALF)
        d_q = pick_heads(dot(d_scores, kx[b, :, cols], TN))
        dq[rows, cols] = unturn(d_q).astype(HALF)
        d_k = dot(d_scores, qs, NN)
        d_v = dot(probs.astype(HALF), ups, NN)
        v_cols = pl.ds(pl.multiple_of(width + i * PAIR, PAIR), PAIR)
        for k in range(2):
            part_rows = slice(k * tokens + b * length, k * tokens + (b + 1) * length)
            piece = slice(k * length, (k + 1) * length)
            dkv[part_rows, cols] = unturn(d_k[piece], k).astype(HALF)
            dkv[part_rows, v_cols] = d_v[piece].astype(HALF)

    for j in range(6):
        tasks["attb", j] = some_pairs(attend_back, j)

    for i, (left, right) in enumerate(((n1_own, dq), (n1_all, dkv.at[:, width:]), (n1_all, dkv))):
        tasks["grad", 4 + i] = functools.partial(grad_joined, 4 + i, left, right)

    @task("backq")
    def _():
        e[:, :width] = dot(dq[...], wj_all[:, :width], NT)

    @task("backkv")
    def _():
        e[:, :width] = e[:, :width] + dot(dkv[:tokens], wj_all[:, width:], NT)

    rims = halo(1, rim_in.at[0], rim_out.at[0], rim_in.at[1], rim_out.at[1])

    @task("backh")
    def _():
        total = jnp.zeros((1, width), F32)
        for b in range(2):
            first = tokens + b * length
            back = dot(dkv[first : first + length], wj_all[:, width:], NT)
            for side in range(2):
                piece = back[side * half : (side + 1) * half]
                rim_out[side, b] = piece.astype(HALF)
                norm = centre(xh[side, b].astype(F32))[0]
                total = total + jnp.sum(piece * norm, axis=0, keepdims=True)
        part[0, 0:1] = part[0, 0:1] + total

    @task("rim")
    def _():
        exchange_start(rims)

    @task("rimw")
    def _():
        exchange_wait(rims)

    gain_sum, gain_in = g("gain_sum"), g("gain_in")
    gain_sems = (g("n_send"), g("n_recv"))

    def gain_push(t):
        peer = at["peers"][GAIN_PATH[t]]
        copies["n"] = push(gain_sum.at[t], gain_in.at[t], gain_sems, (t,), peer)

    @task("n", 0)
    def _():
        @pl.loop(0, blocks)
        def _(i):
            rows = rows_of(i)
            part[0] += fold(e[rows, :width] * g("norm1")[rows])

        gain_sum[0] = jnp.zeros(gain_sum.shape[1:], F32)
        for k in range(2):
            gain_sum[0, k : k + 1] = jnp.sum(part[k], axis=0, keepdims=True)
        gain_push(0)

    @task("norm1b")
    def _():
        for b in range(2):
            for side in range(2):
                first = b * length + side * half
                for k in range(0, half, 32):
                    rows = slice(first + k, first + k + 32)
                    up = e[rows, :width] + rim_in[side, b, k : k + 32].astype(F32)
                    d_source = norm_down(up, g("norm1")[rows], g("inv1")[rows], gains[0:1])
                    g("grad")[rows] = (dn[rows] + d_source).astype(HALF)

    def gain_task(t):
        def run():
            copies.pop("n").wait()
            gain_sum[t] = gain_sum[t - 1] + gain_in[t - 1]
            if t < 5:
                gain_push(t)
                return
            shift = ((32 - (at["dp"] * 8 + seq)) * ROWS) % width
            g("o_n")[...] = pltpu.roll(gain_sum[5], shift, 1)[:, :128]

        return run

    for t in range(1, 6):
        tasks["n", t] = gain_task(t)

    @task("final")
    def _():
        @pl.loop(0, width // 256)
        def _(i):
            cols = pl.ds(pl.multiple_of(i * 256, 256), 256)
            value = resid[:, cols]
            for j in range(3):
                value = value + dot(de[j, :, 2 * third :], wf_all[j, cols, 2 * third :], NT)
            g("out")[:, cols] = value.astype(HALF)

    for name in ORDER:
        tasks.pop(name)()
    assert not tasks


def fused_layer(x, cot, wj, wo, we, wc, gn, freq):
    tokens, width = x.shape
    ff = wc.shape[1]
    length = tokens // 2
    half = WINDOW // 2
    span = length + 2 * half
    pairs = width // PAIR
    lead = (2, 2, 2, 2, 2, ROWS)
    ins = dict(x=x, cot=cot, wj=wj, wo=wo, we=we, wc=wc, gn=gn, freq=freq)
    outs = dict(
        out=((tokens, width), HALF),
        grad=((tokens, width), HALF),
        o_e=((ROWS, 2 * ff), F32),
        o_c=((ROWS, ff), F32),
        o_o=((ROWS, width), F32),
        o_j=((ROWS, 3 * width), F32),
        o_n=((8, 128), F32),
    )
    held = dict(bn=((2, 2, 2, 2, 2, 8, 128), F32))
    for name in ("bk", "bv", "bq", "bo"):
        held[name] = (lead + (width,), HALF)
    for j in range(3):
        held["bf%d" % j] = (lead + (ff,), HALF)
    held.update(
        wj_all=((width, 3 * width), HALF),
        wo_all=((width, width), HALF),
        wf_all=((3, width, ff), HALF),
        gains=((8, width), F32),
        cos=((2, length, PAIR), F32),
        sin=((2, length, PAIR), F32),
        xh=((2, 2, half, width), HALF),
        low=((length, PAIR), HALF),
        high=((length, PAIR), HALF),
        bias=((span, 2 * length), F32),
        norm1=((tokens, width), F32),
        inv1=((tokens, 1), F32),
        n1=((2 * tokens, width), HALF),
        n1_t=((width, 2 * tokens), HALF),
        cot_t=((width, tokens), HALF),
        q=((tokens, width), HALF),
        kx=((2, span, width), HALF),
        vx=((2, span, width), HALF),
        stat=((2 * pairs, 1, 2 * length), F32),
        att=((tokens, width), HALF),
        resid=((tokens, width), F32),
        norm2=((tokens, width), F32),
        inv2=((tokens, 1), F32),
        n2=((tokens, width), HALF),
        n2_t=((width, tokens), HALF),
        e=((tokens, ff), F32),
        de=((3, tokens, ff), HALF),
        dn=((tokens, width), F32),
        part=((2, 8, width), F32),
        dq=((tokens, width), HALF),
        dkv=((2 * tokens, 2 * width), HALF),
        rim_out=((2, 2, half, width), HALF),
        rim_in=((2, 2, half, width), HALF),
        gain_sum=((6, 8, width), F32),
        gain_in=((5, 8, width), F32),
        grads=((2, width, ff), F32),
        s3=((2, 2, ROWS, ff), F32),
        s4=((2, ROWS, ff), F32),
    )
    for i in range(7):
        size = ff if i < 3 else width
        held["r0_%d" % i] = ((2, 8 * ROWS, size), F32)
        held["r1_%d" % i] = ((2, 2, 2, ROWS, size), HALF)
        held["r2_%d" % i] = ((2, 2, ROWS, size), HALF)
        held["r3_%d" % i] = ((2, ROWS, size), F32)
        held["r4_%d" % i] = ((ROWS, size), F32)
    sems = {}
    for side in ("send", "recv"):
        sems["g_" + side] = (8, 5)
        sems["h_" + side] = (2, 2)
        sems["s_" + side] = (7, 6)
        sems["n_" + side] = (5,)
    vmem = pl.BlockSpec(memory_space=pltpu.VMEM)
    names = tuple(ins) + tuple(outs) + tuple(held) + tuple(sems)
    return pl.pallas_call(
        functools.partial(layer_kernel, names),
        out_shape=tuple(jax.ShapeDtypeStruct(*v) for v in outs.values()),
        in_specs=[vmem] * len(ins),
        out_specs=(vmem,) * len(outs),
        scratch_shapes=[pltpu.VMEM(*v) for v in held.values()]
        + [pltpu.SemaphoreType.DMA(v) for v in sems.values()],
        compiler_params=pltpu.CompilerParams(
            collective_id=0, has_side_effects=True, vmem_limit_bytes=VMEM_LIMIT
        ),
    )(*ins.values())


VMEM_LIMIT = 63 * MIB


def fast_layer(
    layer_input, cotangent, w_joined, w_output, w_expand, w_contract, gain_one, gain_two
):
    width = layer_input.shape[-1]
    tokens = layer_input.shape[0] * layer_input.shape[1] * layer_input.shape[2]
    gains = jnp.pad(
        jnp.stack([gain_one, gain_two]).astype(F32), ((0, 6), (0, 128 - gain_one.shape[0]))
    )
    half_dim = HEAD_DIM // 2
    freqs = ROPE_BASE ** (-jnp.arange(half_dim).astype(F32) * 2.0 / HEAD_DIM)
    freq = jnp.tile(freqs, PAIR // half_dim)[None, :]
    out, grad, o_e, o_c, o_o, o_j, o_n = fused_layer(
        layer_input.reshape(tokens, width),
        cotangent.reshape(tokens, width),
        w_joined,
        w_output,
        w_expand,
        w_contract.T,
        gains,
        freq,
    )
    count = gain_one.shape[0]
    return (
        out.reshape(layer_input.shape),
        grad.reshape(layer_input.shape),
        o_j,
        o_o,
        o_e,
        o_c.T,
        o_n[0, :count],
        o_n[1, :count],
    )


def solution(mesh):
    fits = mesh.shape["dp"] == 4 and mesh.shape["seq"] == 8
    body = fast_layer if fits else plain_layer
    placed = (
        P(None, "dp", "seq", None),
        P(None, "dp", "seq", None),
        P(("dp", "seq"), None),
        P(("dp", "seq"), None),
        P(("dp", "seq"), None),
        P(None, ("dp", "seq")),
        P(("dp", "seq")),
        P(("dp", "seq")),
    )
    return jax.shard_map(
        body,
        mesh=mesh,
        in_specs=placed,
        out_specs=(
            P(None, "dp", "seq", None),
            P(None, "dp", "seq", None),
            P(("dp", "seq"), None),
            P(("dp", "seq"), None),
            P(("dp", "seq"), None),
            P(None, ("dp", "seq")),
            P(("dp", "seq")),
            P(("dp", "seq")),
        ),
        check_vma=False,
    )
```

```python
import functools

import jax
import jax.numpy as jnp
from jax import lax
import numpy as np
from jax.experimental import pallas as pl
from jax.experimental.pallas import tpu as pltpu
from jax.sharding import PartitionSpec as P

HEADS = 12
HEAD_DIM = 64
WINDOW = 128


NORM_EPS = 1e-05
ROPE_BASE = 10000.0
MASK_FILL = -1e30
SQRT_HALF = 0.7071067811865476
INV_ROOT_TAU = 0.3989422804014327


LANES = 128


def pair_sum(value, outer):
    outer_size = lax.axis_size(outer)
    pairs = outer_size // 2
    core = lax.axis_index(outer) % 2
    blocks = value.reshape(pairs, 2, value.shape[0] // outer_size, value.shape[1])
    other = lax.dynamic_index_in_dim(blocks, 1 - core, axis=1, keepdims=False)
    own = lax.dynamic_index_in_dim(blocks, core, axis=1, keepdims=False)
    swap = [(i, i ^ 1) for i in range(outer_size)]
    return own + lax.ppermute(other, outer, swap)


def line_sum(value, outer):
    outer_size = lax.axis_size(outer)
    if outer_size == 4:
        line = lax.axis_index(outer) // 2
        other = lax.dynamic_index_in_dim(value, 1 - line, axis=0, keepdims=False)
        own = lax.dynamic_index_in_dim(value, line, axis=0, keepdims=False)
        swap = [(i, i ^ 2) for i in range(outer_size)]
        arrived = lax.ppermute(other.astype(jnp.bfloat16), outer, swap)
        value = own + arrived.astype(jnp.float32)
    else:
        groups = [list(range(c, outer_size, 2)) for c in range(2)]
        arrived = lax.all_to_all(
            value.astype(jnp.bfloat16), outer, 0, 0, axis_index_groups=groups
        )
        value = jnp.sum(arrived.astype(jnp.float32), axis=0)
    return value


def ring_sum(value, inner):
    inner_size = lax.axis_size(inner)
    blocks = value.reshape(inner_size, value.shape[0] // inner_size, value.shape[1])
    return jnp.sum(lax.all_to_all(blocks, inner, 0, 0), axis=0)


def norm_apply(values, gain):
    center = jnp.mean(values, axis=-1, keepdims=True)
    shifted = values - center
    inv_std = lax.rsqrt(jnp.mean(shifted * shifted, axis=-1, keepdims=True) + NORM_EPS)
    normed = shifted * inv_std
    return (normed * gain.astype(jnp.float32), normed, inv_std)


def norm_back(upstream, normed, inv_std, gain):
    scaled = upstream * gain.astype(jnp.float32)
    inner = (
        scaled
        - jnp.mean(scaled, axis=-1, keepdims=True)
        - normed * jnp.mean(scaled * normed, axis=-1, keepdims=True)
    )
    return (inv_std * inner, jnp.sum(upstream * normed, axis=(0, 1)))


def gelu_slope(values):
    cumul = 0.5 * (1.0 + jax.scipy.special.erf(values * SQRT_HALF))
    return cumul + values * jnp.exp(-0.5 * values * values) * INV_ROOT_TAU


def rope_tables(positions, head_dim):
    half_dim = head_dim // 2
    freqs = ROPE_BASE ** (-jnp.arange(half_dim).astype(jnp.float32) * 2.0 / head_dim)
    angles = positions.astype(jnp.float32)[:, None] * freqs[None, :]
    return (jnp.cos(angles)[:, None, :], jnp.sin(angles)[:, None, :])


def rotate(values, cosine, sine):
    half_dim = values.shape[-1] // 2
    first = values[..., :half_dim]
    second = values[..., half_dim:]
    return jnp.concatenate(
        [first * cosine - second * sine, second * cosine + first * sine], axis=-1
    )


def unrotate(values, cosine, sine):
    half_dim = values.shape[-1] // 2
    first = values[..., :half_dim]
    second = values[..., half_dim:]
    return jnp.concatenate(
        [first * cosine + second * sine, second * cosine - first * sine], axis=-1
    )


def plain_layer(
    layer_input, cotangent, w_joined, w_output, w_expand, w_contract, gain_one, gain_two
):
    micro, local_batch, group, width = layer_input.shape
    heads = HEADS
    head_dim = HEAD_DIM
    half = WINDOW // 2
    ffn = w_contract.shape[0]
    batch = micro * local_batch
    scale = head_dim ** (-0.5)
    axes = ("dp", "seq")
    seq_count = lax.axis_size("seq")
    up = [(i, i + 1) for i in range(seq_count - 1)]
    down = [(j, i) for i, j in up]
    group_start = lax.axis_index("seq") * group
    cosine, sine = rope_tables(group_start + jnp.arange(group, dtype=jnp.int32), head_dim)
    query_pos = group_start + jnp.arange(group, dtype=jnp.int32)[:, None]
    key_pos = group_start - half + jnp.arange(group + 2 * half, dtype=jnp.int32)[None, :]
    allowed = (
        (jnp.abs(query_pos - key_pos) <= half) & (key_pos >= 0) & (key_pos < group * seq_count)
    )
    gains = jnp.pad(jnp.stack([gain_one, gain_two], axis=1), ((0, 0), (0, LANES - 2)))
    pack_one = jnp.concatenate([w_joined, gains], axis=1)
    pack_two = jnp.concatenate([w_expand, w_contract.T, w_output], axis=1)
    full_one = lax.all_gather(pack_one, axes, axis=0, tiled=True)
    full_two = lax.all_gather(pack_two, axes, axis=0, tiled=True)
    full_joined = full_one[:, : 3 * width]
    full_gain_one = full_one[:, 3 * width]
    full_gain_two = full_one[:, 3 * width + 1]
    full_expand = full_two[:, : 2 * ffn]
    full_contract = full_two[:, 2 * ffn : 3 * ffn]
    full_output = full_two[:, 3 * ffn :]

    source32 = layer_input.reshape(batch, group, width).astype(jnp.float32)
    upstream_half = cotangent.reshape(batch, group, width)
    normed_f, norm_one, inv_one = norm_apply(source32, full_gain_one)
    normed_one = normed_f.astype(jnp.bfloat16)
    joined = jnp.einsum(
        "bcd,de->bce", normed_one, full_joined, preferred_element_type=jnp.float32
    )
    shape_heads = (batch, group, heads, head_dim)
    k_rot = rotate(joined[..., width : 2 * width].reshape(shape_heads), cosine, sine).astype(
        jnp.bfloat16
    )
    v_half = joined[..., 2 * width :].astype(jnp.bfloat16)
    key_value = jnp.stack([k_rot.reshape(batch, group, width), v_half])
    before = lax.ppermute(key_value[:, :, group - half :], "seq", up)
    after = lax.ppermute(key_value[:, :, :half], "seq", down)
    q_rot = rotate(joined[..., :width].reshape(shape_heads), cosine, sine).astype(jnp.bfloat16)
    extended = jnp.concatenate([before, key_value, after], axis=2)
    ext_shape = (batch, group + 2 * half, heads, head_dim)
    key_rows = extended[0].reshape(ext_shape)
    value_rows = extended[1].reshape(ext_shape)
    scores = (
        jnp.einsum("bqhd,bkhd->bhqk", q_rot, key_rows, preferred_element_type=jnp.float32)
        * scale
    )
    scores = jnp.where(allowed[None, None], scores, MASK_FILL)
    row_max = jnp.max(scores, axis=-1, keepdims=True)
    log_total = row_max + jnp.log(jnp.sum(jnp.exp(scores - row_max), axis=-1, keepdims=True))
    probs = jnp.exp(scores - log_total)
    probs_half = probs.astype(jnp.bfloat16)
    attended = jnp.einsum(
        "bhqk,bkhd->bqhd", probs_half, value_rows, preferred_element_type=jnp.float32
    )
    attended = attended.astype(jnp.bfloat16).reshape(batch, group, width)
    resid = source32 + jnp.einsum(
        "bcd,de->bce", attended, full_output, preferred_element_type=jnp.float32
    )
    normed_g, norm_two, inv_two = norm_apply(resid, full_gain_two)
    normed_two = normed_g.astype(jnp.bfloat16)
    expanded = jnp.einsum(
        "bcd,de->bce", normed_two, full_expand, preferred_element_type=jnp.float32
    )
    pre_act = expanded[..., :ffn]
    gate_part = expanded[..., ffn:]
    activated = jax.nn.gelu(pre_act, approximate=False)
    mixed = (activated * gate_part).astype(jnp.bfloat16)
    contract_acc = jnp.einsum(
        "bcd,bcf->df", upstream_half, mixed, preferred_element_type=jnp.float32
    )
    d_mixed = jnp.einsum(
        "bcd,df->bcf", upstream_half, full_contract, preferred_element_type=jnp.float32
    )
    d_expanded = jnp.concatenate(
        [d_mixed * gate_part * gelu_slope(pre_act), d_mixed * activated], axis=-1
    ).astype(jnp.bfloat16)
    expand_acc = jnp.einsum(
        "bcd,bce->de", normed_two, d_expanded, preferred_element_type=jnp.float32
    )
    ffn_grads, d_expanded = lax.optimization_barrier(
        (jnp.concatenate([expand_acc, contract_acc], axis=1), d_expanded)
    )
    ffn_pair = pair_sum(ffn_grads, "dp")
    d_normed_two = jnp.einsum(
        "bce,de->bcd", d_expanded, full_expand, preferred_element_type=jnp.float32
    )
    d_resid_n, gain_two_part = norm_back(d_normed_two, norm_two, inv_two, full_gain_two)
    d_resid = upstream_half.astype(jnp.float32) + d_resid_n
    d_resid_half = d_resid.astype(jnp.bfloat16)
    ffn_pair, d_resid_half = lax.optimization_barrier((ffn_pair, d_resid_half))
    ffn_line = line_sum(ffn_pair, "dp")
    d_attended = jnp.einsum(
        "bce,de->bcd", d_resid_half, full_output, preferred_element_type=jnp.float32
    )
    d_attended = d_attended.astype(jnp.bfloat16).reshape(shape_heads)
    d_probs = jnp.einsum(
        "bqhd,bkhd->bhqk", d_attended, value_rows, preferred_element_type=jnp.float32
    )
    centred = d_probs - jnp.sum(probs * d_probs, axis=-1, keepdims=True)
    d_scores = (probs * centred * scale).astype(jnp.bfloat16)
    d_key_ext = jnp.einsum(
        "bhqk,bqhd->bkhd", d_scores, q_rot, preferred_element_type=jnp.float32
    )
    d_value_ext = jnp.einsum(
        "bhqk,bqhd->bkhd", probs_half, d_attended, preferred_element_type=jnp.float32
    )
    ext_grads = jnp.stack(
        [
            d_key_ext.reshape(batch, group + 2 * half, width),
            d_value_ext.reshape(batch, group + 2 * half, width),
        ]
    )
    rims = ext_grads.astype(jnp.bfloat16)
    ffn_line, rims = lax.optimization_barrier((ffn_line, rims))
    ffn_sum = ring_sum(ffn_line, "seq")
    from_left = lax.ppermute(rims[:, :, group + half :], "seq", up).astype(jnp.float32)
    from_right = lax.ppermute(rims[:, :, :half], "seq", down).astype(jnp.float32)
    d_query = jnp.einsum(
        "bhqk,bkhd->bqhd", d_scores, key_rows, preferred_element_type=jnp.float32
    )
    output_acc = jnp.einsum(
        "bcd,bce->de", attended, d_resid_half, preferred_element_type=jnp.float32
    )
    final = resid + jnp.einsum(
        "bcf,df->bcd", mixed, full_contract, preferred_element_type=jnp.float32
    )
    own_grads = ext_grads[:, :, half : half + group]
    own_grads = own_grads + jnp.pad(
        from_left, ((0, 0), (0, 0), (0, group - half), (0, 0))
    ) + jnp.pad(from_right, ((0, 0), (0, 0), (group - half, 0), (0, 0)))
    d_key = unrotate(own_grads[0].reshape(shape_heads), cosine, sine).reshape(
        batch, group, width
    )
    d_query_flat = unrotate(d_query, cosine, sine).reshape(batch, group, width)
    d_joined = jnp.concatenate([d_query_flat, d_key, own_grads[1]], axis=-1).astype(
        jnp.bfloat16
    )
    d_normed_one = jnp.einsum(
        "bce,de->bcd", d_joined, full_joined, preferred_element_type=jnp.float32
    )
    d_source, gain_one_part = norm_back(d_normed_one, norm_one, inv_one, full_gain_one)
    input_grad = (d_resid + d_source).astype(jnp.bfloat16)
    joined_acc = jnp.einsum(
        "bcd,bce->de", normed_one, d_joined, preferred_element_type=jnp.float32
    )
    gain_parts = jnp.pad(
        jnp.stack([gain_one_part, gain_two_part], axis=1), ((0, 0), (0, LANES - 2))
    )
    last_grads = jnp.concatenate([joined_acc, output_acc, gain_parts], axis=1)
    last_sum = ring_sum(line_sum(pair_sum(last_grads, "dp"), "dp"), "seq")
    return (
        final.astype(jnp.bfloat16).reshape(layer_input.shape),
        input_grad.reshape(layer_input.shape),
        last_sum[:, : 3 * width],
        last_sum[:, 3 * width : 4 * width],
        ffn_sum[:, : 2 * ffn],
        ffn_sum[:, 2 * ffn :].T,
        last_sum[:, 4 * width],
        last_sum[:, 4 * width + 1],
    )


MESH = pl.DeviceIdType.MESH
ROWS = 24
MIB = 2**20
F32 = jnp.float32
HALF = jnp.bfloat16
PAIR = 128


def place(steep=False):
    dp, seq = lax.axis_index("dp"), lax.axis_index("seq")
    y, core = dp // 2, dp % 2
    z, x = seq // 2, seq % 2
    zh, zl = z // 2, z % 2
    turn = 1 if steep else core
    peers = dict(
        pair=(dp + 1 - 2 * core, seq),
        r=(dp + 2 * turn * (1 - 2 * y), seq + (1 - turn) * (1 - 2 * x)),
        p=(dp + 2 * (1 - turn) * (1 - 2 * y), seq + turn * (1 - 2 * x)),
        zl=(dp, seq + 2 - 4 * zl),
        zh=(dp, seq + 4 - 8 * zh),
        left=(dp, (seq + 7) % 8),
        right=(dp, (seq + 1) % 8),
    )
    r = x * (1 - turn) + y * turn
    p = y * (1 - turn) + x * turn
    return dict(dp=dp, seq=seq, core=core, turn=turn, zh=zh, zl=zl, r=r, p=p, peers=peers)


def meet(at):
    barrier = pltpu.get_barrier_semaphore()
    for peer in at["peers"].values():
        pl.semaphore_signal(barrier, inc=1, device_id=peer, device_id_type=MESH)
    pl.semaphore_wait(barrier, len(at["peers"]))


def remote(src, dst, sems, where, peer):
    send, recv = sems
    return pltpu.make_async_remote_copy(
        src_ref=src,
        dst_ref=dst,
        send_sem=send.at[where],
        recv_sem=recv.at[where],
        device_id=peer,
        device_id_type=MESH,
    )


def push(*args):
    copy = remote(*args)
    copy.start()
    return copy


def gather_spot(at, path, stage=0):
    return (at["core"],) + tuple(at[name] for name in reversed(path[stage:]))


def gather_send(at, path, buf, sems, group, stage):
    part = buf.at[gather_spot(at, path, stage)]
    name = path[stage] if stage < 4 else "pair"
    return push(part, part, sems, (group, stage), at["peers"][name])


def plane_index(path, steep, core, y, z, x):
    r, p = (y, x) if steep or core else (x, y)
    place = dict(r=r, p=p, zh=z // 2, zl=z % 2)
    return (core,) + tuple(place[name] for name in reversed(path))


def relay(path, steep, buf, store):
    for core in range(2):
        for y in range(2):
            for z in range(4):
                blocks = [buf[plane_index(path, steep, core, y, z, x)].astype(F32) for x in range(2)]
                store(y * 384 + core * 192 + z * 48, jnp.concatenate(blocks, axis=0).astype(HALF))


def relay_gains(path, steep, buf, gains):
    width = gains.shape[1]
    total = jnp.zeros((8, width), F32)
    row, lane = (lax.broadcasted_iota(jnp.int32, (8, 128), k) for k in range(2))
    valid = (row < 2) & (lane < ROWS)
    for core in range(2):
        for y in range(2):
            for z in range(4):
                for x in range(2):
                    block = jnp.where(valid, buf[plane_index(path, steep, core, y, z, x)], 0.0)
                    wide = jnp.concatenate([block, jnp.zeros((8, width - 128), F32)], axis=1)
                    shift = ROWS * (y * 16 + core * 8 + z * 2 + x)
                    total = total + (pltpu.roll(wide, shift, 1) if shift else wide)
    gains[...] = total


def block_row(at, p, z, r):
    y = p * (1 - at["turn"]) + r * at["turn"]
    x = r * (1 - at["turn"]) + p * at["turn"]
    return y, pl.multiple_of(z * 48 + x * ROWS, 8)


def sum_stage(at, stage, grads, bufs, sems, index, width, emit):
    r0, r1, r2, r3, r4, s1, s2, s3, s4 = bufs
    core, r, p, zh, zl = at["core"], at["r"], at["p"], at["zh"], at["zl"]
    peers = at["peers"]
    w = slice(0, width)

    def kept(pp, z):
        y, row = block_row(at, pp, z, r)
        return y, pl.ds(row, ROWS)

    if stage == 0:
        copies = []
        for y in range(2):
            rows = pl.ds(pl.multiple_of(y * 384 + (1 - core) * 192, 192), 192)
            copies.append(push(grads.at[rows, w], r0.at[y], sems, (index, y), peers["pair"]))
        return copies
    if stage == 1:

        @pl.loop(0, 8)
        def _(i):
            pp, z = i // 4, i % 4
            y, row = block_row(at, pp, z, 1 - r)
            base = pl.multiple_of(y * 384 + core * 192 + row, 8)
            s1[pp, z // 2, z % 2, :, w] = (grads[pl.ds(base, ROWS), w] + r0[y, pl.ds(row, ROWS)]).astype(HALF)
            y, rows = kept(pp, z)
            base = pl.multiple_of(y * 384 + core * 192 + rows.start, 8)
            r0[y, rows] = grads[pl.ds(base, ROWS), w] + r0[y, rows]

        return [push(s1.at[:, :, :, :, w], r1, sems, (index, 2), peers["r"])]
    if stage == 2:

        @pl.loop(0, 4)
        def _(z):
            zh, zl = z // 2, z % 2
            s2[zh, zl, :, w] = (r0[kept(1 - p, z)] + r1[1 - p, zh, zl].astype(F32)).astype(HALF)
            r0[kept(p, z)] = r0[kept(p, z)] + r1[p, zh, zl].astype(F32)

        return [push(s2.at[:, :, :, w], r2, sems, (index, 3), peers["p"])]
    if stage == 3:
        for h in range(2):
            far, near = 2 * h + 1 - zl, 2 * h + zl
            s3[h, :, w] = r0[kept(p, far)] + r2[h, 1 - zl].astype(F32)
            r0[kept(p, near)] = r0[kept(p, near)] + r2[h, zl].astype(F32)
        return [push(s3.at[:, :, w], r3, sems, (index, 4), peers["zl"])]
    if stage == 4:
        s4[:, w] = r0[kept(p, 2 * (1 - zh) + zl)] + r3[1 - zh]
        return [push(s4.at[:, w], r4, sems, (index, 5), peers["zh"])]
    emit((r0[kept(p, 2 * zh + zl)] + r3[zh]) + r4[...])
    return []


GAIN_PATH = ("pair", "r", "p", "zl", "zh")


def dot(a, b, dims):
    return lax.dot_general(a, b, (dims, ((), ())), preferred_element_type=F32)


NN, NT, TN = ((1,), (0,)), ((1,), (1,)), ((0,), (0,))


def swap_halves(v):
    lane = lax.broadcasted_iota(jnp.int32, v.shape, 1) % HEAD_DIM
    return jnp.where(
        lane < HEAD_DIM // 2,
        pltpu.roll(v, PAIR - HEAD_DIM // 2, 1),
        pltpu.roll(v, HEAD_DIM // 2, 1),
    )


PATHS = (("zh", "zl", "p", "r"), ("p", "r", "zh", "zl"))
GATHER = ((0, 0), (0, 0), (0, 0), (0, 0), (0, 1), (0, 0), (0, 0), (0, 0))
SUM_STEEP = (0, 0, 0, 0, 0, 0, 0)
KINDS = (
    "g",
    "s",
    "pre",
    "n1",
    "n1h",
    "halo",
    "halow",
    "proj",
    "att",
    "oproj",
    "norm2",
    "fwd",
    "grad",
    "back",
    "norm2b",
    "datt",
    "attb",
    "backq",
    "backkv",
    "backh",
    "rim",
    "rimw",
    "n",
    "norm1b",
    "final",
)
ORDER = (
    86, 0, 6, 83, 1, 12, 7, 18, 2, 87, 13, 24, 3, 8, 19, 30, 25, 36, 4, 14, 5, 84, 9, 20,
    26, 85, 31, 42, 15, 37, 10, 21, 11, 88, 27, 32, 16, 43, 38, 17, 90, 22, 33, 23, 89, 91,
    28, 39, 92, 93, 44, 94, 29, 95, 34, 96, 97, 98, 35, 99, 40, 102, 45, 109, 41, 100, 103,
    110, 48, 46, 53, 47, 101, 104, 49, 111, 112, 105, 113, 114, 115, 54, 58, 106, 50, 63,
    116, 117, 107, 55, 118, 119, 122, 51, 59, 68, 108, 120, 121, 125, 64, 73, 56, 132, 60,
    126, 52, 69, 78, 123, 127, 65, 128, 57, 74, 61, 129, 70, 130, 79, 66, 62, 124, 131, 71,
    75, 67, 80, 72, 76, 81, 77, 82,
)


def layer_kernel(names, *refs):
    ns = dict(zip(names, refs))
    g = lambda key: ns[key]
    at = place()
    seq = at["seq"]
    x, cot, gains = g("x"), g("cot"), g("gains")
    tokens, width = x.shape
    third = g("de").shape[2] // 3
    ff = 3 * third
    length = tokens // 2
    half = WINDOW // 2
    scale = HEAD_DIM ** (-0.5)
    cos, sin, low, high = g("cos"), g("sin"), g("low"), g("high")
    n1, n2, q, kx, vx = g("n1"), g("n2"), g("q"), g("kx"), g("vx")
    blocks = tokens // 32
    span = length + 2 * half
    pairs = width // PAIR

    def rows_of(i, n=32):
        return pl.ds(pl.multiple_of(i * n, n), n)

    wj, wo, we, wc = g("wj"), g("wo"), g("we"), g("wc")
    views = (at, place(True))
    group_at = [views[steep] for steep, _ in GATHER]
    paths = [PATHS[way] for _, way in GATHER]
    spots = [gather_spot(*pair) for pair in zip(group_at, paths)]
    bn = g("bn")
    for k, ref in enumerate((g("g1"), g("g2"))):
        bn[spots[0] + (slice(k, k + 1), slice(0, ROWS))] = ref[...].astype(F32)
    g("bk")[spots[1]] = wj[:, width : 2 * width]
    g("bv")[spots[2]] = wj[:, 2 * width :]
    g("bq")[spots[3]] = wj[:, :width]
    g("bo")[spots[4]] = wo[...]
    for j in range(3):
        buf, spot = g("bf%d" % j), spots[5 + j]
        buf[spot + (slice(None), slice(0, third))] = we[:, j * third : (j + 1) * third]
        buf[spot + (slice(None), slice(third, 2 * third))] = we[
            :, ff + j * third : ff + (j + 1) * third
        ]
        buf[spot + (slice(None), slice(2 * third, ff))] = wc[:, j * third : (j + 1) * third]

    xh, rim_in = g("xh"), g("rim_in")

    @pl.when(seq == 0)
    def _():
        xh[0] = jnp.zeros(xh.shape[1:], HALF)
        rim_in[0] = jnp.zeros(rim_in.shape[1:], HALF)

    @pl.when(seq == 7)
    def _():
        xh[1] = jnp.zeros(xh.shape[1:], HALF)
        rim_in[1] = jnp.zeros(rim_in.shape[1:], HALF)

    meet(at)

    wj_all, wo_all, wf_all = g("wj_all"), g("wo_all"), g("wf_all")

    def into(ref, offset):
        def store(row, value):
            ref[row : row + 48, offset : offset + value.shape[1]] = value

        return store

    groups = [
        ("bn", None),
        ("bk", into(wj_all, width)),
        ("bv", into(wj_all, 2 * width)),
        ("bq", into(wj_all, 0)),
        ("bo", into(wo_all, 0)),
    ] + [("bf%d" % j, into(wf_all.at[j], 0)) for j in range(3)]
    copies = {}
    tasks = {}

    def task(*name):
        def note(f):
            tasks[name] = f

        return note

    def gather_task(i, stage):
        def run():
            name, store = groups[i]
            if stage:
                copies.pop(i).wait()
            if stage < 5:
                sems = (g("g_send"), g("g_recv"))
                copies[i] = gather_send(group_at[i], paths[i], g(name), sems, i, stage)
            elif store is None:
                relay_gains(paths[i], GATHER[i][0], g(name), gains)
            else:
                relay(paths[i], GATHER[i][0], g(name), store)

        return run

    for i in range(len(groups)):
        for stage in range(6):
            tasks["g", i, stage] = gather_task(i, stage)

    def centre(values):
        mean = jnp.mean(values, axis=-1, keepdims=True)
        shifted = values - mean
        inv = lax.rsqrt(jnp.mean(shifted * shifted, axis=-1, keepdims=True) + NORM_EPS)
        return shifted * inv, inv

    @task("pre")
    def _():
        lane = lax.broadcasted_iota(jnp.int32, (length, PAIR), 1)
        row = lax.broadcasted_iota(jnp.int32, (length, PAIR), 0)
        sign = jnp.where(lane % HEAD_DIM < HEAD_DIM // 2, -1.0, 1.0)
        beside = jnp.where(row < half, row - half, row + half)
        for k, offset in enumerate((row, beside)):
            angle = (offset + seq * length).astype(F32) * g("freq")[...]
            cos[k] = jnp.cos(angle)
            sin[k] = jnp.sin(angle) * sign
        low[...] = jnp.where(lane < HEAD_DIM, 1.0, 0.0).astype(HALF)
        high[...] = jnp.where(lane < HEAD_DIM, 0.0, 1.0).astype(HALF)
        key = lax.broadcasted_iota(jnp.int32, (span, 2 * length), 0)
        key = jnp.where(key < length, key, jnp.where(key < length + half, key - span + half, key - half))
        query = lax.broadcasted_iota(jnp.int32, (span, 2 * length), 1) % length
        key_pos = key + seq * length
        allowed = (jnp.abs(key - query) <= half) & (key_pos >= 0) & (key_pos < 8 * length)
        g("bias")[...] = jnp.where(allowed, 0.0, MASK_FILL)

        @pl.loop(0, blocks)
        def _(i):
            rows = rows_of(i)
            norm, inv = centre(x[rows].astype(F32))
            g("norm1")[rows] = norm
            g("inv1")[rows] = inv

        for c in range(0, width, 256):
            g("cot_t")[c : c + 256] = jnp.transpose(cot[:, c : c + 256].astype(F32)).astype(HALF)

    @task("n1")
    def _():
        for c in range(0, width, 256):
            value = g("norm1")[:, c : c + 256] * gains[0:1, c : c + 256]
            n1[:tokens, c : c + 256] = value.astype(HALF)
            g("n1_t")[c : c + 256, :tokens] = jnp.transpose(value).astype(HALF)

    @task("n1h")
    def _():
        for b in range(2):
            for side in range(2):
                rows = slice(tokens + b * length + side * half, tokens + b * length + (side + 1) * half)
                n1[rows] = (centre(xh[side, b].astype(F32))[0] * gains[0:1]).astype(HALF)
        for c in range(0, width, 256):
            value = n1[tokens:, c : c + 256].astype(F32)
            g("n1_t")[c : c + 256, tokens:] = jnp.transpose(value).astype(HALF)

    halo_sems = (g("h_send"), g("h_recv"))

    def halo(i, from_left, to_left, from_right, to_right):
        def left():
            return remote(to_left, from_right, halo_sems, (i, 0), at["peers"]["left"])

        def right():
            return remote(to_right, from_left, halo_sems, (i, 1), at["peers"]["right"])

        return left, right

    x_rows = x.reshape(2, length, width)
    x_halo = halo(0, xh.at[0], x_rows.at[:, :half], xh.at[1], x_rows.at[:, half:])

    def exchange_start(sides):
        pl.when(seq > 0)(lambda: sides[0]().start())
        pl.when(seq < 7)(lambda: sides[1]().start())

    def exchange_wait(sides):
        left, right = sides

        @pl.when(seq > 0)
        def _():
            left().wait_send()
            right().wait_recv()

        @pl.when(seq < 7)
        def _():
            right().wait_send()
            left().wait_recv()

    def project(offset, rows, store):
        @pl.loop(0, width // 256)
        def _(i):
            base = pl.multiple_of(i * 256, 256)
            value = dot(n1[:rows], wj_all[:, pl.ds(offset + base, 256)], NN)
            for b in range(rows // length):
                for c in range(2):
                    store(
                        b,
                        pl.ds(base + c * PAIR, PAIR),
                        value[b * length : (b + 1) * length, c * PAIR : (c + 1) * PAIR],
                    )

    def turn(v, k=0):
        return v * cos[k] + swap_halves(v) * sin[k]

    def unturn(v, k=0):
        return v * cos[k] - swap_halves(v) * sin[k]

    def store_k(b, cols, v):
        k = b // 2
        kx[b % 2, k * length : (k + 1) * length, cols] = turn(v, k).astype(HALF)

    def store_v(b, cols, v):
        k = b // 2
        vx[b % 2, k * length : (k + 1) * length, cols] = v.astype(HALF)

    def store_q(b, cols, v):
        q[b * length : (b + 1) * length, cols] = turn(v).astype(HALF)

    @task("halo")
    def _():
        exchange_start(x_halo)

    @task("halow")
    def _():
        exchange_wait(x_halo)

    @task("proj", "k")
    def _():
        project(width, 2 * tokens, store_k)

    @task("proj", "v")
    def _():
        project(2 * width, 2 * tokens, store_v)

    @task("proj", "q")
    def _():
        project(0, tokens, store_q)

    def stack_heads(v):
        return jnp.concatenate([v * low[...], v * high[...]], axis=0)

    lower = lax.broadcasted_iota(jnp.int32, (length, PAIR), 1) < HEAD_DIM

    def pick_heads(v):
        return jnp.where(lower, v[:length], v[length:])

    def attend(b, i):
        cols = pl.ds(pl.multiple_of(i * PAIR, PAIR), PAIR)
        rows = slice(b * length, (b + 1) * length)
        qs = stack_heads(q[rows, cols])
        scores = dot(kx[b, :, cols], qs, NT) * scale + g("bias")[...]
        top = jnp.max(scores, axis=0, keepdims=True)
        raised = jnp.exp(scores - top)
        total = jnp.sum(raised, axis=0, keepdims=True)
        probs = raised * (1.0 / total)
        g("stat")[b * pairs + i] = top + jnp.log(total)
        g("att")[rows, cols] = pick_heads(dot(probs.astype(HALF), vx[b, :, cols], TN)).astype(HALF)

    def some_pairs(f, j):
        few = pairs // 3
        return lambda: pl.loop(j % 3 * few, (j % 3 + 1) * few)(functools.partial(f, j // 3))

    for j in range(6):
        tasks["att", j] = some_pairs(attend, j)

    resid = g("resid")

    @task("oproj")
    def _():
        @pl.loop(0, width // 256)
        def _(i):
            cols = pl.ds(pl.multiple_of(i * 256, 256), 256)
            resid[:, cols] = x[:, cols].astype(F32) + dot(g("att")[...], wo_all[:, cols], NN)

    @task("norm2")
    def _():
        @pl.loop(0, blocks)
        def _(i):
            rows = rows_of(i)
            norm, inv = centre(resid[rows])
            g("norm2")[rows] = norm
            g("inv2")[rows] = inv
            n2[rows] = (norm * gains[1:2]).astype(HALF)

        for c in range(0, width, 256):
            g("n2_t")[c : c + 256] = jnp.transpose(n2[:, c : c + 256].astype(F32)).astype(HALF)

    per = width // 3

    def run_sum(index, stage):
        size = ff if index < 3 else width

        def emit(value):
            if index < 3:
                j = index * third
                g("o_e")[:, j : j + third] = value[:, :third]
                g("o_e")[:, ff + j : ff + j + third] = value[:, third : 2 * third]
                g("o_c")[:, j : j + third] = value[:, 2 * third :]
            elif index == 3:
                g("o_o")[...] = value
            else:
                for k in range(3):
                    j = k * width + (index - 4) * per
                    g("o_j")[:, j : j + per] = value[:, k * per : (k + 1) * per]

        bufs = [g("r%d_%d" % (k, index)) for k in range(5)]
        bufs += [g("bf0").at[0, index % 2], g("bf1").at[0, index % 2, 0]]
        bufs += [g("s%d" % k).at[index % 2] for k in range(3, 5)]
        return sum_stage(
            views[SUM_STEEP[index]],
            stage,
            g("grads").at[index % 2],
            bufs,
            (g("s_send"), g("s_recv")),
            index,
            size,
            emit,
        )

    def sum_task(i, stage):
        def run():
            for copy in copies.pop(("s", i), ()):
                copy.wait()
            copies["s", i] = run_sum(i, stage)

        return run

    for i in range(7):
        for stage in range(1, 6):
            tasks["s", i, stage] = sum_task(i, stage)

    def weight_grad(index, offset, left, right, columns):
        step = min(columns, 384)

        @pl.loop(0, columns // step)
        def _(i):
            base = pl.multiple_of(i * step, step)
            g("grads")[index % 2, :, pl.ds(offset + base, step)] = dot(
                left[...], right[:, pl.ds(base, step)], NN
            )

    e, de, dn = g("e"), g("de"), g("dn")

    def forward_third(j):
        w = wf_all.at[j]
        for c in range(0, 2 * third, third):
            e[:, c : c + third] = dot(n2[...], w[:, c : c + third], NN)
        e[:, 2 * third :] = dot(cot[...], w[:, 2 * third :], NN)

        @pl.loop(0, blocks)
        def _(i):
            rows = rows_of(i)
            pre, gate, d_mixed = (e[rows, c * third : (c + 1) * third] for c in range(3))
            cumul = 0.5 * (1.0 + lax.erf(pre * SQRT_HALF))
            active = pre * cumul
            slope = cumul + pre * jnp.exp(-0.5 * pre * pre) * INV_ROOT_TAU
            de[j, rows, :third] = (d_mixed * gate * slope).astype(HALF)
            de[j, rows, third : 2 * third] = (d_mixed * active).astype(HALF)
            de[j, rows, 2 * third :] = (active * gate).astype(HALF)

    def grad_third(j):
        weight_grad(j, 0, g("n2_t"), de.at[j], 2 * third)
        weight_grad(j, 2 * third, g("cot_t"), de.at[j, :, 2 * third :], third)
        sum_task(j, 0)()

    def back_third(j):
        back = dot(de[j, :, : 2 * third], wf_all[j, :, : 2 * third], NT)
        dn[...] = back if j == 0 else dn[...] + back

    for j in range(3):
        tasks["fwd", j] = functools.partial(forward_third, j)
        tasks["grad", j] = functools.partial(grad_third, j)
        tasks["back", j] = functools.partial(back_third, j)

    def norm_down(upstream, norm, inv, gain):
        scaled = upstream * gain
        mean = jnp.mean(scaled, axis=-1, keepdims=True)
        along = jnp.mean(scaled * norm, axis=-1, keepdims=True)
        return inv * (scaled - mean - norm * along)

    part = g("part")
    def fold(v):
        return sum(v[k : k + 8] for k in range(0, 32, 8))

    @task("norm2b")
    def _():
        part[...] = jnp.zeros(part.shape, F32)

        @pl.loop(0, blocks)
        def _(i):
            rows = rows_of(i)
            up, norm = dn[rows], g("norm2")[rows]
            part[1] += fold(up * norm)
            d_resid = cot[rows].astype(F32) + norm_down(up, norm, g("inv2")[rows], gains[1:2])
            dn[rows] = d_resid
            n1[rows] = d_resid.astype(HALF)

    @task("datt")
    def _():
        @pl.loop(0, width // 256)
        def _(i):
            rows = pl.ds(pl.multiple_of(i * 256, 256), 256)
            n2[:, rows] = dot(n1[:tokens], wo_all[rows, :], NT).astype(HALF)

    @task("grad", 3)
    def _():
        @pl.loop(0, width // 256)
        def _(i):
            cols = pl.ds(pl.multiple_of(i * 256, 256), 256)
            g("grads")[1, cols, :width] = dot(g("att")[:, cols], n1[:tokens], TN)

        sum_task(3, 0)()

    n1_own, n1_all = g("n1_t").at[:, :tokens], g("n1_t")

    def grad_joined(h):
        cols = slice(h * per, (h + 1) * per)
        v_cols = slice(width + h * per, width + (h + 1) * per)
        weight_grad(4 + h, 0, n1_own, dq.at[:, cols], per)
        weight_grad(4 + h, per, n1_all, dkv.at[:, cols], per)
        weight_grad(4 + h, 2 * per, n1_all, dkv.at[:, v_cols], per)
        sum_task(4 + h, 0)()

    rim_out = g("rim_out")
    dq, dkv = g("dq"), g("dkv")

    def attend_back(b, i):
        cols = pl.ds(pl.multiple_of(i * PAIR, PAIR), PAIR)
        rows = slice(b * length, (b + 1) * length)
        qs = stack_heads(q[rows, cols])
        ups = stack_heads(n2[rows, cols])
        scores = dot(kx[b, :, cols], qs, NT) * scale + g("bias")[...]
        probs = jnp.exp(scores - g("stat")[b * pairs + i])
        d_probs = dot(vx[b, :, cols], ups, NT)
        centred = d_probs - jnp.sum(probs * d_probs, axis=0, keepdims=True)
        d_scores = (probs * centred * scale).astype(HALF)
        d_q = pick_heads(dot(d_scores, kx[b, :, cols], TN))
        dq[rows, cols] = unturn(d_q).astype(HALF)
        d_k = dot(d_scores, qs, NN)
        d_v = dot(probs.astype(HALF), ups, NN)
        v_cols = pl.ds(pl.multiple_of(width + i * PAIR, PAIR), PAIR)
        for k in range(2):
            part_rows = slice(k * tokens + b * length, k * tokens + (b + 1) * length)
            piece = slice(k * length, (k + 1) * length)
            dkv[part_rows, cols] = unturn(d_k[piece], k).astype(HALF)
            dkv[part_rows, v_cols] = d_v[piece].astype(HALF)

    for j in range(6):
        tasks["attb", j] = some_pairs(attend_back, j % 2 * 3 + j // 2)

    for h in range(3):
        tasks["grad", 4 + h] = functools.partial(grad_joined, h)

    @task("backq")
    def _():
        e[:, :width] = dot(dq[...], wj_all[:, :width], NT)

    @task("backkv")
    def _():
        e[:, :width] = e[:, :width] + dot(dkv[:tokens], wj_all[:, width:], NT)

    rims = halo(1, rim_in.at[0], rim_out.at[0], rim_in.at[1], rim_out.at[1])

    @task("backh")
    def _():
        total = jnp.zeros((1, width), F32)
        for b in range(2):
            first = tokens + b * length
            back = dot(dkv[first : first + length], wj_all[:, width:], NT)
            for side in range(2):
                piece = back[side * half : (side + 1) * half]
                rim_out[side, b] = piece.astype(HALF)
                norm = centre(xh[side, b].astype(F32))[0]
                total = total + jnp.sum(piece * norm, axis=0, keepdims=True)
        part[0, 0:1] = part[0, 0:1] + total

    @task("rim")
    def _():
        exchange_start(rims)

    @task("rimw")
    def _():
        exchange_wait(rims)

    gain_sum, gain_in = g("gain_sum"), g("gain_in")
    gain_sems = (g("n_send"), g("n_recv"))

    def gain_push(t):
        peer = at["peers"][GAIN_PATH[t]]
        copies["n"] = push(gain_sum.at[t], gain_in.at[t], gain_sems, (t,), peer)

    @task("n", 0)
    def _():
        @pl.loop(0, blocks)
        def _(i):
            rows = rows_of(i)
            part[0] += fold(e[rows, :width] * g("norm1")[rows])

        gain_sum[0] = jnp.zeros(gain_sum.shape[1:], F32)
        for k in range(2):
            gain_sum[0, k : k + 1] = jnp.sum(part[k], axis=0, keepdims=True)
        gain_push(0)

    @task("norm1b")
    def _():
        for b in range(2):
            for side in range(2):
                first = b * length + side * half
                for k in range(0, half, 32):
                    rows = slice(first + k, first + k + 32)
                    up = e[rows, :width] + rim_in[side, b, k : k + 32].astype(F32)
                    d_source = norm_down(up, g("norm1")[rows], g("inv1")[rows], gains[0:1])
                    g("grad")[rows] = (dn[rows] + d_source).astype(HALF)

    def gain_task(t):
        def run():
            copies.pop("n").wait()
            gain_sum[t] = gain_sum[t - 1] + gain_in[t - 1]
            if t < 5:
                gain_push(t)
                return
            shift = ((32 - (at["dp"] * 8 + seq)) * ROWS) % width
            own = pltpu.roll(gain_sum[5], shift, 1)
            g("o_g1")[...] = own[0:1, :ROWS]
            g("o_g2")[...] = own[1:2, :ROWS]

        return run

    for t in range(1, 6):
        tasks["n", t] = gain_task(t)

    @task("final")
    def _():
        @pl.loop(0, width // 256)
        def _(i):
            cols = pl.ds(pl.multiple_of(i * 256, 256), 256)
            value = resid[:, cols]
            for j in range(3):
                value = value + dot(de[j, :, 2 * third :], wf_all[j, cols, 2 * third :], NT)
            g("out")[:, cols] = value.astype(HALF)

    kinds = {}
    for name, run in tasks.items():
        kinds.setdefault(name[0], {})[name[1:]] = run
    steps = [run for kind in KINDS for _, run in sorted(kinds.pop(kind).items())]
    assert not kinds and sorted(ORDER) == list(range(len(steps)))
    for number in ORDER:
        steps[number]()


def fused_layer(x, cot, wj, wo, we, wc, g1, g2, freq):
    tokens, width = x.shape
    ff = wc.shape[1]
    length = tokens // 2
    half = WINDOW // 2
    span = length + 2 * half
    pairs = width // PAIR
    lead = (2, 2, 2, 2, 2, ROWS)
    ins = dict(x=x, cot=cot, wj=wj, wo=wo, we=we, wc=wc, g1=g1, g2=g2, freq=freq)
    outs = dict(
        out=((tokens, width), HALF),
        grad=((tokens, width), HALF),
        o_e=((ROWS, 2 * ff), F32),
        o_c=((ROWS, ff), F32),
        o_o=((ROWS, width), F32),
        o_j=((ROWS, 3 * width), F32),
        o_g1=((1, ROWS), F32),
        o_g2=((1, ROWS), F32),
    )
    held = dict(bn=((2, 2, 2, 2, 2, 8, 128), F32))
    for name in ("bk", "bv", "bq", "bo"):
        held[name] = (lead + (width,), HALF)
    for j in range(3):
        held["bf%d" % j] = (lead + (ff,), HALF)
    held.update(
        wj_all=((width, 3 * width), HALF),
        wo_all=((width, width), HALF),
        wf_all=((3, width, ff), HALF),
        gains=((8, width), F32),
        cos=((2, length, PAIR), F32),
        sin=((2, length, PAIR), F32),
        xh=((2, 2, half, width), HALF),
        low=((length, PAIR), HALF),
        high=((length, PAIR), HALF),
        bias=((span, 2 * length), F32),
        norm1=((tokens, width), F32),
        inv1=((tokens, 1), F32),
        n1=((2 * tokens, width), HALF),
        n1_t=((width, 2 * tokens), HALF),
        cot_t=((width, tokens), HALF),
        q=((tokens, width), HALF),
        kx=((2, span, width), HALF),
        vx=((2, span, width), HALF),
        stat=((2 * pairs, 1, 2 * length), F32),
        att=((tokens, width), HALF),
        resid=((tokens, width), F32),
        norm2=((tokens, width), F32),
        inv2=((tokens, 1), F32),
        n2=((tokens, width), HALF),
        n2_t=((width, tokens), HALF),
        e=((tokens, ff), F32),
        de=((3, tokens, ff), HALF),
        dn=((tokens, width), F32),
        part=((2, 8, width), F32),
        dq=((tokens, width), HALF),
        dkv=((2 * tokens, 2 * width), HALF),
        rim_out=((2, 2, half, width), HALF),
        rim_in=((2, 2, half, width), HALF),
        gain_sum=((6, 8, width), F32),
        gain_in=((5, 8, width), F32),
        grads=((2, width, ff), F32),
        s3=((2, 2, ROWS, ff), F32),
        s4=((2, ROWS, ff), F32),
    )
    for i in range(7):
        size = ff if i < 3 else width
        held["r0_%d" % i] = ((2, 8 * ROWS, size), F32)
        held["r1_%d" % i] = ((2, 2, 2, ROWS, size), HALF)
        held["r2_%d" % i] = ((2, 2, ROWS, size), HALF)
        held["r3_%d" % i] = ((2, ROWS, size), F32)
        held["r4_%d" % i] = ((ROWS, size), F32)
    sems = {}
    for side in ("send", "recv"):
        sems["g_" + side] = (8, 5)
        sems["h_" + side] = (2, 2)
        sems["s_" + side] = (7, 6)
        sems["n_" + side] = (5,)
    vmem = pl.BlockSpec(memory_space=pltpu.VMEM)
    names = tuple(ins) + tuple(outs) + tuple(held) + tuple(sems)
    return pl.pallas_call(
        functools.partial(layer_kernel, names),
        out_shape=tuple(jax.ShapeDtypeStruct(*v) for v in outs.values()),
        in_specs=[vmem] * len(ins),
        out_specs=(vmem,) * len(outs),
        scratch_shapes=[pltpu.VMEM(*v) for v in held.values()]
        + [pltpu.SemaphoreType.DMA(v) for v in sems.values()],
        compiler_params=pltpu.CompilerParams(
            collective_id=0, has_side_effects=True, vmem_limit_bytes=VMEM_LIMIT
        ),
    )(*ins.values())


VMEM_LIMIT = 63 * MIB


def hand_on(arrays):
    vmem = pl.BlockSpec(memory_space=pltpu.VMEM)
    count = len(arrays)

    def kernel(*refs):
        for source, target in zip(refs[:count], refs[count:]):
            target[...] = source[...]

    return pl.pallas_call(
        kernel,
        out_shape=tuple(jax.ShapeDtypeStruct(a.shape, a.dtype) for a in arrays),
        in_specs=[vmem] * count,
        out_specs=(vmem,) * count,
    )(*arrays)


def fast_layer(
    layer_input, cotangent, w_joined, w_output, w_expand, w_contract, gain_one, gain_two
):
    width = layer_input.shape[-1]
    tokens = layer_input.shape[0] * layer_input.shape[1] * layer_input.shape[2]
    half_dim = HEAD_DIM // 2
    freqs = np.float32(ROPE_BASE) ** (-np.arange(half_dim, dtype=np.float32) * 2.0 / HEAD_DIM)
    freq = np.tile(freqs.astype(np.float32), PAIR // half_dim)[None, :]
    outs = fused_layer(
        layer_input.reshape(tokens, width),
        cotangent.reshape(tokens, width),
        w_joined,
        w_output,
        w_expand,
        w_contract.T,
        gain_one[None, :],
        gain_two[None, :],
        freq,
    )
    out, grad, o_e, o_c, o_o, o_j, o_g1, o_g2 = hand_on(outs)
    return (
        out.reshape(layer_input.shape),
        grad.reshape(layer_input.shape),
        o_j,
        o_o,
        o_e,
        o_c.T,
        o_g1[0],
        o_g2[0],
    )


def solution(mesh):
    fits = mesh.shape["dp"] == 4 and mesh.shape["seq"] == 8
    body = fast_layer if fits else plain_layer
    placed = (
        P(None, "dp", "seq", None),
        P(None, "dp", "seq", None),
        P(("dp", "seq"), None),
        P(("dp", "seq"), None),
        P(("dp", "seq"), None),
        P(None, ("dp", "seq")),
        P(("dp", "seq")),
        P(("dp", "seq")),
    )
    return jax.shard_map(
        body,
        mesh=mesh,
        in_specs=placed,
        out_specs=(
            P(None, "dp", "seq", None),
            P(None, "dp", "seq", None),
            P(("dp", "seq"), None),
            P(("dp", "seq"), None),
            P(("dp", "seq"), None),
            P(None, ("dp", "seq")),
            P(("dp", "seq")),
            P(("dp", "seq")),
        ),
        check_vma=False,
    )
```

```python
import enum
import functools
import types

import jax
import jax.numpy as jnp
from jax import lax
import numpy as np
from jax.experimental import pallas as pl
from jax.experimental.pallas import tpu as pltpu
from jax.sharding import PartitionSpec as P

HEADS = 12
HEAD_DIM = 64
WINDOW = 128


NORM_EPS = 1e-05
ROPE_BASE = 10000.0
MASK_FILL = -1e30
SQRT_HALF = 0.7071067811865476
INV_ROOT_TAU = 0.3989422804014327


LANES = 128


def pair_sum(value, outer):
    outer_size = lax.axis_size(outer)
    pairs = outer_size // 2
    core = lax.axis_index(outer) % 2
    blocks = value.reshape(pairs, 2, value.shape[0] // outer_size, value.shape[1])
    other = lax.dynamic_index_in_dim(blocks, 1 - core, axis=1, keepdims=False)
    own = lax.dynamic_index_in_dim(blocks, core, axis=1, keepdims=False)
    swap = [(i, i ^ 1) for i in range(outer_size)]
    return own + lax.ppermute(other, outer, swap)


def line_sum(value, outer):
    outer_size = lax.axis_size(outer)
    if outer_size == 4:
        line = lax.axis_index(outer) // 2
        other = lax.dynamic_index_in_dim(value, 1 - line, axis=0, keepdims=False)
        own = lax.dynamic_index_in_dim(value, line, axis=0, keepdims=False)
        swap = [(i, i ^ 2) for i in range(outer_size)]
        arrived = lax.ppermute(other.astype(jnp.bfloat16), outer, swap)
        value = own + arrived.astype(jnp.float32)
    else:
        groups = [list(range(c, outer_size, 2)) for c in range(2)]
        arrived = lax.all_to_all(
            value.astype(jnp.bfloat16), outer, 0, 0, axis_index_groups=groups
        )
        value = jnp.sum(arrived.astype(jnp.float32), axis=0)
    return value


def ring_sum(value, inner):
    inner_size = lax.axis_size(inner)
    blocks = value.reshape(inner_size, value.shape[0] // inner_size, value.shape[1])
    return jnp.sum(lax.all_to_all(blocks, inner, 0, 0), axis=0)


def norm_apply(values, gain):
    center = jnp.mean(values, axis=-1, keepdims=True)
    shifted = values - center
    inv_std = lax.rsqrt(jnp.mean(shifted * shifted, axis=-1, keepdims=True) + NORM_EPS)
    normed = shifted * inv_std
    return (normed * gain.astype(jnp.float32), normed, inv_std)


def norm_back(upstream, normed, inv_std, gain):
    scaled = upstream * gain.astype(jnp.float32)
    inner = (
        scaled
        - jnp.mean(scaled, axis=-1, keepdims=True)
        - normed * jnp.mean(scaled * normed, axis=-1, keepdims=True)
    )
    return (inv_std * inner, jnp.sum(upstream * normed, axis=(0, 1)))


def gelu_slope(values):
    cumul = 0.5 * (1.0 + jax.scipy.special.erf(values * SQRT_HALF))
    return cumul + values * jnp.exp(-0.5 * values * values) * INV_ROOT_TAU


def rope_tables(positions, head_dim):
    half_dim = head_dim // 2
    freqs = ROPE_BASE ** (-jnp.arange(half_dim).astype(jnp.float32) * 2.0 / head_dim)
    angles = positions.astype(jnp.float32)[:, None] * freqs[None, :]
    return (jnp.cos(angles)[:, None, :], jnp.sin(angles)[:, None, :])


def rotate(values, cosine, sine):
    half_dim = values.shape[-1] // 2
    first = values[..., :half_dim]
    second = values[..., half_dim:]
    return jnp.concatenate(
        [first * cosine - second * sine, second * cosine + first * sine], axis=-1
    )


def unrotate(values, cosine, sine):
    half_dim = values.shape[-1] // 2
    first = values[..., :half_dim]
    second = values[..., half_dim:]
    return jnp.concatenate(
        [first * cosine + second * sine, second * cosine - first * sine], axis=-1
    )


def plain_layer(
    layer_input, cotangent, w_joined, w_output, w_expand, w_contract, gain_one, gain_two
):
    micro, local_batch, group, width = layer_input.shape
    heads = HEADS
    head_dim = HEAD_DIM
    half = WINDOW // 2
    ffn = w_contract.shape[0]
    batch = micro * local_batch
    scale = head_dim ** (-0.5)
    axes = ("dp", "seq")
    seq_count = lax.axis_size("seq")
    up = [(i, i + 1) for i in range(seq_count - 1)]
    down = [(j, i) for i, j in up]
    group_start = lax.axis_index("seq") * group
    cosine, sine = rope_tables(group_start + jnp.arange(group, dtype=jnp.int32), head_dim)
    query_pos = group_start + jnp.arange(group, dtype=jnp.int32)[:, None]
    key_pos = group_start - half + jnp.arange(group + 2 * half, dtype=jnp.int32)[None, :]
    allowed = (
        (jnp.abs(query_pos - key_pos) <= half) & (key_pos >= 0) & (key_pos < group * seq_count)
    )
    gains = jnp.pad(jnp.stack([gain_one, gain_two], axis=1), ((0, 0), (0, LANES - 2)))
    pack_one = jnp.concatenate([w_joined, gains], axis=1)
    pack_two = jnp.concatenate([w_expand, w_contract.T, w_output], axis=1)
    full_one = lax.all_gather(pack_one, axes, axis=0, tiled=True)
    full_two = lax.all_gather(pack_two, axes, axis=0, tiled=True)
    full_joined = full_one[:, : 3 * width]
    full_gain_one = full_one[:, 3 * width]
    full_gain_two = full_one[:, 3 * width + 1]
    full_expand = full_two[:, : 2 * ffn]
    full_contract = full_two[:, 2 * ffn : 3 * ffn]
    full_output = full_two[:, 3 * ffn :]

    source32 = layer_input.reshape(batch, group, width).astype(jnp.float32)
    upstream_half = cotangent.reshape(batch, group, width)
    normed_f, norm_one, inv_one = norm_apply(source32, full_gain_one)
    normed_one = normed_f.astype(jnp.bfloat16)
    joined = jnp.einsum(
        "bcd,de->bce", normed_one, full_joined, preferred_element_type=jnp.float32
    )
    shape_heads = (batch, group, heads, head_dim)
    k_rot = rotate(joined[..., width : 2 * width].reshape(shape_heads), cosine, sine).astype(
        jnp.bfloat16
    )
    v_half = joined[..., 2 * width :].astype(jnp.bfloat16)
    key_value = jnp.stack([k_rot.reshape(batch, group, width), v_half])
    before = lax.ppermute(key_value[:, :, group - half :], "seq", up)
    after = lax.ppermute(key_value[:, :, :half], "seq", down)
    q_rot = rotate(joined[..., :width].reshape(shape_heads), cosine, sine).astype(jnp.bfloat16)
    extended = jnp.concatenate([before, key_value, after], axis=2)
    ext_shape = (batch, group + 2 * half, heads, head_dim)
    key_rows = extended[0].reshape(ext_shape)
    value_rows = extended[1].reshape(ext_shape)
    scores = (
        jnp.einsum("bqhd,bkhd->bhqk", q_rot, key_rows, preferred_element_type=jnp.float32)
        * scale
    )
    scores = jnp.where(allowed[None, None], scores, MASK_FILL)
    row_max = jnp.max(scores, axis=-1, keepdims=True)
    log_total = row_max + jnp.log(jnp.sum(jnp.exp(scores - row_max), axis=-1, keepdims=True))
    probs = jnp.exp(scores - log_total)
    probs_half = probs.astype(jnp.bfloat16)
    attended = jnp.einsum(
        "bhqk,bkhd->bqhd", probs_half, value_rows, preferred_element_type=jnp.float32
    )
    attended = attended.astype(jnp.bfloat16).reshape(batch, group, width)
    resid = source32 + jnp.einsum(
        "bcd,de->bce", attended, full_output, preferred_element_type=jnp.float32
    )
    normed_g, norm_two, inv_two = norm_apply(resid, full_gain_two)
    normed_two = normed_g.astype(jnp.bfloat16)
    expanded = jnp.einsum(
        "bcd,de->bce", normed_two, full_expand, preferred_element_type=jnp.float32
    )
    pre_act = expanded[..., :ffn]
    gate_part = expanded[..., ffn:]
    activated = jax.nn.gelu(pre_act, approximate=False)
    mixed = (activated * gate_part).astype(jnp.bfloat16)
    contract_acc = jnp.einsum(
        "bcd,bcf->df", upstream_half, mixed, preferred_element_type=jnp.float32
    )
    d_mixed = jnp.einsum(
        "bcd,df->bcf", upstream_half, full_contract, preferred_element_type=jnp.float32
    )
    d_expanded = jnp.concatenate(
        [d_mixed * gate_part * gelu_slope(pre_act), d_mixed * activated], axis=-1
    ).astype(jnp.bfloat16)
    expand_acc = jnp.einsum(
        "bcd,bce->de", normed_two, d_expanded, preferred_element_type=jnp.float32
    )
    ffn_grads, d_expanded = lax.optimization_barrier(
        (jnp.concatenate([expand_acc, contract_acc], axis=1), d_expanded)
    )
    ffn_pair = pair_sum(ffn_grads, "dp")
    d_normed_two = jnp.einsum(
        "bce,de->bcd", d_expanded, full_expand, preferred_element_type=jnp.float32
    )
    d_resid_n, gain_two_part = norm_back(d_normed_two, norm_two, inv_two, full_gain_two)
    d_resid = upstream_half.astype(jnp.float32) + d_resid_n
    d_resid_half = d_resid.astype(jnp.bfloat16)
    ffn_pair, d_resid_half = lax.optimization_barrier((ffn_pair, d_resid_half))
    ffn_line = line_sum(ffn_pair, "dp")
    d_attended = jnp.einsum(
        "bce,de->bcd", d_resid_half, full_output, preferred_element_type=jnp.float32
    )
    d_attended = d_attended.astype(jnp.bfloat16).reshape(shape_heads)
    d_probs = jnp.einsum(
        "bqhd,bkhd->bhqk", d_attended, value_rows, preferred_element_type=jnp.float32
    )
    centred = d_probs - jnp.sum(probs * d_probs, axis=-1, keepdims=True)
    d_scores = (probs * centred * scale).astype(jnp.bfloat16)
    d_key_ext = jnp.einsum(
        "bhqk,bqhd->bkhd", d_scores, q_rot, preferred_element_type=jnp.float32
    )
    d_value_ext = jnp.einsum(
        "bhqk,bqhd->bkhd", probs_half, d_attended, preferred_element_type=jnp.float32
    )
    ext_grads = jnp.stack(
        [
            d_key_ext.reshape(batch, group + 2 * half, width),
            d_value_ext.reshape(batch, group + 2 * half, width),
        ]
    )
    rims = ext_grads.astype(jnp.bfloat16)
    ffn_line, rims = lax.optimization_barrier((ffn_line, rims))
    ffn_sum = ring_sum(ffn_line, "seq")
    from_left = lax.ppermute(rims[:, :, group + half :], "seq", up).astype(jnp.float32)
    from_right = lax.ppermute(rims[:, :, :half], "seq", down).astype(jnp.float32)
    d_query = jnp.einsum(
        "bhqk,bkhd->bqhd", d_scores, key_rows, preferred_element_type=jnp.float32
    )
    output_acc = jnp.einsum(
        "bcd,bce->de", attended, d_resid_half, preferred_element_type=jnp.float32
    )
    final = resid + jnp.einsum(
        "bcf,df->bcd", mixed, full_contract, preferred_element_type=jnp.float32
    )
    own_grads = ext_grads[:, :, half : half + group]
    own_grads = own_grads + jnp.pad(
        from_left, ((0, 0), (0, 0), (0, group - half), (0, 0))
    ) + jnp.pad(from_right, ((0, 0), (0, 0), (group - half, 0), (0, 0)))
    d_key = unrotate(own_grads[0].reshape(shape_heads), cosine, sine).reshape(
        batch, group, width
    )
    d_query_flat = unrotate(d_query, cosine, sine).reshape(batch, group, width)
    d_joined = jnp.concatenate([d_query_flat, d_key, own_grads[1]], axis=-1).astype(
        jnp.bfloat16
    )
    d_normed_one = jnp.einsum(
        "bce,de->bcd", d_joined, full_joined, preferred_element_type=jnp.float32
    )
    d_source, gain_one_part = norm_back(d_normed_one, norm_one, inv_one, full_gain_one)
    input_grad = (d_resid + d_source).astype(jnp.bfloat16)
    joined_acc = jnp.einsum(
        "bcd,bce->de", normed_one, d_joined, preferred_element_type=jnp.float32
    )
    gain_parts = jnp.pad(
        jnp.stack([gain_one_part, gain_two_part], axis=1), ((0, 0), (0, LANES - 2))
    )
    last_grads = jnp.concatenate([joined_acc, output_acc, gain_parts], axis=1)
    last_sum = ring_sum(line_sum(pair_sum(last_grads, "dp"), "dp"), "seq")
    return (
        final.astype(jnp.bfloat16).reshape(layer_input.shape),
        input_grad.reshape(layer_input.shape),
        last_sum[:, : 3 * width],
        last_sum[:, 3 * width : 4 * width],
        ffn_sum[:, : 2 * ffn],
        ffn_sum[:, 2 * ffn :].T,
        last_sum[:, 4 * width],
        last_sum[:, 4 * width + 1],
    )


MESH = pl.DeviceIdType.MESH
ROWS = 24
MIB = 2**20
F32 = jnp.float32
HALF = jnp.bfloat16
PAIR = 128


def place(steep=False):
    dp, seq = lax.axis_index("dp"), lax.axis_index("seq")
    y, core = dp // 2, dp % 2
    z, x = seq // 2, seq % 2
    zh, zl = z // 2, z % 2
    turn = 1 if steep else core
    peers = dict(
        pair=(dp + 1 - 2 * core, seq),
        r=(dp + 2 * turn * (1 - 2 * y), seq + (1 - turn) * (1 - 2 * x)),
        p=(dp + 2 * (1 - turn) * (1 - 2 * y), seq + turn * (1 - 2 * x)),
        zl=(dp, seq + 2 - 4 * zl),
        zh=(dp, seq + 4 - 8 * zh),
        left=(dp, (seq + 7) % 8),
        right=(dp, (seq + 1) % 8),
    )
    r = x * (1 - turn) + y * turn
    p = y * (1 - turn) + x * turn
    return types.SimpleNamespace(dp=dp, seq=seq, core=core, turn=turn, zh=zh, zl=zl, r=r, p=p, peers=peers)


def meet(at):
    barrier = pltpu.get_barrier_semaphore()
    for peer in at.peers.values():
        pl.semaphore_signal(barrier, inc=1, device_id=peer, device_id_type=MESH)
    pl.semaphore_wait(barrier, len(at.peers))


def remote(src, dst, sems, where, peer):
    send, recv = sems
    return pltpu.make_async_remote_copy(
        src_ref=src,
        dst_ref=dst,
        send_sem=send.at[where],
        recv_sem=recv.at[where],
        device_id=peer,
        device_id_type=MESH,
    )


def push(*args):
    copy = remote(*args)
    copy.start()
    return copy


def gather_spot(at, path, stage=0):
    return (at.core,) + tuple(getattr(at, name) for name in reversed(path[stage:]))


def gather_send(at, path, buf, sems, group, stage):
    part = buf.at[gather_spot(at, path, stage)]
    name = path[stage] if stage < 4 else "pair"
    return push(part, part, sems, (group, stage), at.peers[name])


def plane_index(path, steep, core, y, z, x):
    r, p = (y, x) if steep or core else (x, y)
    place = dict(r=r, p=p, zh=z // 2, zl=z % 2)
    return (core,) + tuple(place[name] for name in reversed(path))


def relay(path, steep, buf, store):
    for core in range(2):
        for y in range(2):
            for z in range(4):
                blocks = [buf[plane_index(path, steep, core, y, z, x)].astype(F32) for x in range(2)]
                store(y * 384 + core * 192 + z * 48, jnp.concatenate(blocks, axis=0).astype(HALF))


def relay_gains(path, steep, buf, gains):
    width = gains.shape[1]
    total = jnp.zeros((8, width), F32)
    row, lane = (lax.broadcasted_iota(jnp.int32, (8, 128), k) for k in range(2))
    valid = (row < 2) & (lane < ROWS)
    for core in range(2):
        for y in range(2):
            for z in range(4):
                for x in range(2):
                    block = jnp.where(valid, buf[plane_index(path, steep, core, y, z, x)], 0.0)
                    wide = jnp.concatenate([block, jnp.zeros((8, width - 128), F32)], axis=1)
                    shift = ROWS * (y * 16 + core * 8 + z * 2 + x)
                    total = total + (pltpu.roll(wide, shift, 1) if shift else wide)
    gains[...] = total


def block_row(at, p, z, r):
    y = p * (1 - at.turn) + r * at.turn
    x = r * (1 - at.turn) + p * at.turn
    return y, pl.multiple_of(z * 48 + x * ROWS, 8)


def sum_stage(at, stage, grads, bufs, sems, index, width, emit):
    r0, r1, r2, r3, r4, s1, s2, s3, s4 = bufs
    core, r, p, zh, zl = at.core, at.r, at.p, at.zh, at.zl
    peers = at.peers
    w = slice(0, width)

    def kept(pp, z):
        y, row = block_row(at, pp, z, r)
        return y, pl.ds(row, ROWS)

    if stage == 0:
        copies = []
        for y in range(2):
            rows = pl.ds(pl.multiple_of(y * 384 + (1 - core) * 192, 192), 192)
            copies.append(push(grads.at[rows, w], r0.at[y], sems, (index, y), peers["pair"]))
        return copies
    if stage == 1:

        @pl.loop(0, 8)
        def _(i):
            pp, z = i // 4, i % 4
            y, row = block_row(at, pp, z, 1 - r)
            base = pl.multiple_of(y * 384 + core * 192 + row, 8)
            s1[pp, z // 2, z % 2, :, w] = (grads[pl.ds(base, ROWS), w] + r0[y, pl.ds(row, ROWS)]).astype(HALF)
            y, rows = kept(pp, z)
            base = pl.multiple_of(y * 384 + core * 192 + rows.start, 8)
            r0[y, rows] = grads[pl.ds(base, ROWS), w] + r0[y, rows]

        return [push(s1.at[:, :, :, :, w], r1, sems, (index, 2), peers["r"])]
    if stage == 2:

        @pl.loop(0, 4)
        def _(z):
            zh, zl = z // 2, z % 2
            s2[zh, zl, :, w] = (r0[kept(1 - p, z)] + r1[1 - p, zh, zl].astype(F32)).astype(HALF)
            r0[kept(p, z)] = r0[kept(p, z)] + r1[p, zh, zl].astype(F32)

        return [push(s2.at[:, :, :, w], r2, sems, (index, 3), peers["p"])]
    if stage == 3:
        for h in range(2):
            far, near = 2 * h + 1 - zl, 2 * h + zl
            s3[h, :, w] = r0[kept(p, far)] + r2[h, 1 - zl].astype(F32)
            r0[kept(p, near)] = r0[kept(p, near)] + r2[h, zl].astype(F32)
        return [push(s3.at[:, :, w], r3, sems, (index, 4), peers["zl"])]
    if stage == 4:
        s4[:, w] = r0[kept(p, 2 * (1 - zh) + zl)] + r3[1 - zh]
        return [push(s4.at[:, w], r4, sems, (index, 5), peers["zh"])]
    emit((r0[kept(p, 2 * zh + zl)] + r3[zh]) + r4[...])
    return []


GAIN_PATH = ("pair", "r", "p", "zl", "zh")


def dot(a, b, dims):
    return lax.dot_general(a, b, (dims, ((), ())), preferred_element_type=F32)


NN, NT, TN = ((1,), (0,)), ((1,), (1,)), ((0,), (0,))


def swap_halves(v):
    lane = lax.broadcasted_iota(jnp.int32, v.shape, 1) % HEAD_DIM
    return jnp.where(
        lane < HEAD_DIM // 2,
        pltpu.roll(v, PAIR - HEAD_DIM // 2, 1),
        pltpu.roll(v, HEAD_DIM // 2, 1),
    )


class Kind(enum.IntEnum):
    g = 0
    s = 1
    pre = 2
    n1 = 3
    n1h = 4
    halo = 5
    halow = 6
    proj = 7
    att = 8
    oproj = 9
    norm2 = 10
    fwd = 11
    grad = 12
    back = 13
    norm2b = 14
    datt = 15
    attb = 16
    backq = 17
    backkv = 18
    backh = 19
    rim = 20
    rimw = 21
    n = 22
    norm1b = 23
    final = 24


PATHS = (("zh", "zl", "p", "r"), ("p", "r", "zh", "zl"))
GATHER = ((0, 0), (0, 0), (0, 0), (0, 0), (0, 1), (0, 0), (0, 0), (0, 0))
SUM_STEEP = (0, 0, 0, 0, 0, 0, 0)
ORDER = (
    0, 6, 83, 1, 12, 7, 86, 18, 2, 13, 24, 8, 19, 30, 14, 87, 3, 25, 36, 20, 9, 31, 42, 15,
    4, 26, 37, 5, 84, 21, 85, 32, 43, 10, 11, 88, 16, 27, 38, 22, 17, 90, 44, 33, 23, 89,
    91, 92, 39, 93, 94, 28, 45, 95, 96, 29, 97, 98, 34, 35, 40, 99, 102, 109, 41, 100, 46,
    103, 110, 48, 47, 101, 104, 53, 111, 112, 105, 113, 49, 114, 58, 115, 106, 116, 54, 63,
    117, 50, 107, 118, 119, 122, 59, 68, 108, 55, 120, 51, 121, 125, 132, 64, 73, 60, 126,
    56, 127, 69, 78, 65, 52, 128, 74, 129, 61, 70, 130, 57, 79, 123, 66, 75, 62, 71, 80,
    124, 131, 67, 76, 72, 81, 77, 82,
)


def layer_kernel(names, *refs):
    ns = types.SimpleNamespace(**dict(zip(names, refs)))
    at = place()
    seq = at.seq
    x, cot, gains = ns.x, ns.cot, ns.gains
    tokens, width = x.shape
    third = ns.de.shape[2] // 3
    ff = 3 * third
    length = tokens // 2
    half = WINDOW // 2
    scale = HEAD_DIM ** (-0.5)
    cos, sin, low, high = ns.cos, ns.sin, ns.low, ns.high
    n1, n2, q, kx, vx = ns.n1, ns.n2, ns.q, ns.kx, ns.vx
    blocks = tokens // 32
    span = length + 2 * half
    pairs = width // PAIR

    def rows_of(i, n=32):
        return pl.ds(pl.multiple_of(i * n, n), n)

    wj, wo, we, wc = ns.wj, ns.wo, ns.we, ns.wc
    views = (at, place(True))
    group_at = [views[steep] for steep, _ in GATHER]
    paths = [PATHS[way] for _, way in GATHER]
    spots = [gather_spot(*pair) for pair in zip(group_at, paths)]
    bn = ns.bn
    for k, ref in enumerate((ns.g1, ns.g2)):
        bn[spots[0] + (slice(k, k + 1), slice(0, ROWS))] = ref[...].astype(F32)
    ns.bk[spots[1]] = wj[:, width : 2 * width]
    ns.bv[spots[2]] = wj[:, 2 * width :]
    ns.bq[spots[3]] = wj[:, :width]
    ns.bo[spots[4]] = wo[...]
    for j in range(3):
        buf, spot = getattr(ns, "bf%d" % j), spots[5 + j]
        buf[spot + (slice(None), slice(0, third))] = we[:, j * third : (j + 1) * third]
        buf[spot + (slice(None), slice(third, 2 * third))] = we[
            :, ff + j * third : ff + (j + 1) * third
        ]
        buf[spot + (slice(None), slice(2 * third, ff))] = wc[:, j * third : (j + 1) * third]

    xh, rim_in = ns.xh, ns.rim_in

    @pl.when(seq == 0)
    def _():
        xh[0] = jnp.zeros(xh.shape[1:], HALF)
        rim_in[0] = jnp.zeros(rim_in.shape[1:], HALF)

    @pl.when(seq == 7)
    def _():
        xh[1] = jnp.zeros(xh.shape[1:], HALF)
        rim_in[1] = jnp.zeros(rim_in.shape[1:], HALF)

    meet(at)

    wj_all, wo_all, wf_all = ns.wj_all, ns.wo_all, ns.wf_all

    def into(ref, offset):
        def store(row, value):
            ref[row : row + 48, offset : offset + value.shape[1]] = value

        return store

    groups = [
        (bn, None),
        (ns.bk, into(wj_all, width)),
        (ns.bv, into(wj_all, 2 * width)),
        (ns.bq, into(wj_all, 0)),
        (ns.bo, into(wo_all, 0)),
    ] + [(buf, into(wf_all.at[j], 0)) for j, buf in enumerate((ns.bf0, ns.bf1, ns.bf2))]
    copies = {}
    tasks = {}

    def task(*name):
        def note(f):
            tasks[name] = f

        return note

    def gather_task(i, stage):
        def run():
            buf, store = groups[i]
            if stage:
                copies.pop(i).wait()
            if stage < 5:
                sems = (ns.g_send, ns.g_recv)
                copies[i] = gather_send(group_at[i], paths[i], buf, sems, i, stage)
            elif store is None:
                relay_gains(paths[i], GATHER[i][0], buf, gains)
            else:
                relay(paths[i], GATHER[i][0], buf, store)

        return run

    for i in range(len(groups)):
        for stage in range(6):
            tasks[Kind.g, i, stage] = gather_task(i, stage)

    def centre(values):
        mean = jnp.mean(values, axis=-1, keepdims=True)
        shifted = values - mean
        inv = lax.rsqrt(jnp.mean(shifted * shifted, axis=-1, keepdims=True) + NORM_EPS)
        return shifted * inv, inv

    @task(Kind.pre)
    def _():
        lane = lax.broadcasted_iota(jnp.int32, (length, PAIR), 1)
        row = lax.broadcasted_iota(jnp.int32, (length, PAIR), 0)
        sign = jnp.where(lane % HEAD_DIM < HEAD_DIM // 2, -1.0, 1.0)
        beside = jnp.where(row < half, row - half, row + half)
        for k, offset in enumerate((row, beside)):
            angle = (offset + seq * length).astype(F32) * ns.freq[...]
            cos[k] = jnp.cos(angle)
            sin[k] = jnp.sin(angle) * sign
        low[...] = jnp.where(lane < HEAD_DIM, 1.0, 0.0).astype(HALF)
        high[...] = jnp.where(lane < HEAD_DIM, 0.0, 1.0).astype(HALF)
        key = lax.broadcasted_iota(jnp.int32, (span, 2 * length), 0)
        key = jnp.where(key < length, key, jnp.where(key < length + half, key - span + half, key - half))
        query = lax.broadcasted_iota(jnp.int32, (span, 2 * length), 1) % length
        key_pos = key + seq * length
        allowed = (jnp.abs(key - query) <= half) & (key_pos >= 0) & (key_pos < 8 * length)
        ns.bias[...] = jnp.where(allowed, 0.0, MASK_FILL)

        @pl.loop(0, blocks)
        def _(i):
            rows = rows_of(i)
            norm, inv = centre(x[rows].astype(F32))
            ns.norm1[rows] = norm
            ns.inv1[rows] = inv

        for c in range(0, width, 256):
            ns.cot_t[c : c + 256] = jnp.transpose(cot[:, c : c + 256].astype(F32)).astype(HALF)

    @task(Kind.n1)
    def _():
        for c in range(0, width, 256):
            value = ns.norm1[:, c : c + 256] * gains[0:1, c : c + 256]
            n1[:tokens, c : c + 256] = value.astype(HALF)
            ns.n1_t[c : c + 256, :tokens] = jnp.transpose(value).astype(HALF)

    @task(Kind.n1h)
    def _():
        for b in range(2):
            for side in range(2):
                rows = slice(tokens + b * length + side * half, tokens + b * length + (side + 1) * half)
                n1[rows] = (centre(xh[side, b].astype(F32))[0] * gains[0:1]).astype(HALF)
        for c in range(0, width, 256):
            value = n1[tokens:, c : c + 256].astype(F32)
            ns.n1_t[c : c + 256, tokens:] = jnp.transpose(value).astype(HALF)

    halo_sems = (ns.h_send, ns.h_recv)

    def halo(i, from_left, to_left, from_right, to_right):
        def left():
            return remote(to_left, from_right, halo_sems, (i, 0), at.peers["left"])

        def right():
            return remote(to_right, from_left, halo_sems, (i, 1), at.peers["right"])

        return left, right

    x_rows = x.reshape(2, length, width)
    x_halo = halo(0, xh.at[0], x_rows.at[:, :half], xh.at[1], x_rows.at[:, half:])

    def exchange_start(sides):
        pl.when(seq > 0)(lambda: sides[0]().start())
        pl.when(seq < 7)(lambda: sides[1]().start())

    def exchange_wait(sides):
        left, right = sides

        @pl.when(seq > 0)
        def _():
            left().wait_send()
            right().wait_recv()

        @pl.when(seq < 7)
        def _():
            right().wait_send()
            left().wait_recv()

    def project(offset, rows, store):
        @pl.loop(0, width // 256)
        def _(i):
            base = pl.multiple_of(i * 256, 256)
            value = dot(n1[:rows], wj_all[:, pl.ds(offset + base, 256)], NN)
            for b in range(rows // length):
                for c in range(2):
                    store(
                        b,
                        pl.ds(base + c * PAIR, PAIR),
                        value[b * length : (b + 1) * length, c * PAIR : (c + 1) * PAIR],
                    )

    def turn(v, k=0):
        return v * cos[k] + swap_halves(v) * sin[k]

    def unturn(v, k=0):
        return v * cos[k] - swap_halves(v) * sin[k]

    def store_k(b, cols, v):
        k = b // 2
        kx[b % 2, k * length : (k + 1) * length, cols] = turn(v, k).astype(HALF)

    def store_v(b, cols, v):
        k = b // 2
        vx[b % 2, k * length : (k + 1) * length, cols] = v.astype(HALF)

    def store_q(b, cols, v):
        q[b * length : (b + 1) * length, cols] = turn(v).astype(HALF)

    @task(Kind.halo)
    def _():
        exchange_start(x_halo)

    @task(Kind.halow)
    def _():
        exchange_wait(x_halo)

    @task(Kind.proj, 0)
    def _():
        project(width, 2 * tokens, store_k)

    @task(Kind.proj, 2)
    def _():
        project(2 * width, 2 * tokens, store_v)

    @task(Kind.proj, 1)
    def _():
        project(0, tokens, store_q)

    def stack_heads(v):
        return jnp.concatenate([v * low[...], v * high[...]], axis=0)

    lower = lax.broadcasted_iota(jnp.int32, (length, PAIR), 1) < HEAD_DIM

    def pick_heads(v):
        return jnp.where(lower, v[:length], v[length:])

    def attend(b, i):
        cols = pl.ds(pl.multiple_of(i * PAIR, PAIR), PAIR)
        rows = slice(b * length, (b + 1) * length)
        qs = stack_heads(q[rows, cols])
        scores = dot(kx[b, :, cols], qs, NT) * scale + ns.bias[...]
        top = jnp.max(scores, axis=0, keepdims=True)
        raised = jnp.exp(scores - top)
        total = jnp.sum(raised, axis=0, keepdims=True)
        probs = raised * (1.0 / total)
        ns.stat[b * pairs + i] = top + jnp.log(total)
        ns.att[rows, cols] = pick_heads(dot(probs.astype(HALF), vx[b, :, cols], TN)).astype(HALF)

    def some_pairs(f, j):
        few = pairs // 3
        return lambda: pl.loop(j % 3 * few, (j % 3 + 1) * few)(functools.partial(f, j // 3))

    for j in range(6):
        tasks[Kind.att, j] = some_pairs(attend, j)

    resid = ns.resid

    @task(Kind.oproj)
    def _():
        @pl.loop(0, width // 256)
        def _(i):
            cols = pl.ds(pl.multiple_of(i * 256, 256), 256)
            resid[:, cols] = x[:, cols].astype(F32) + dot(ns.att[...], wo_all[:, cols], NN)

    @task(Kind.norm2)
    def _():
        @pl.loop(0, blocks)
        def _(i):
            rows = rows_of(i)
            norm, inv = centre(resid[rows])
            ns.norm2[rows] = norm
            ns.inv2[rows] = inv
            n2[rows] = (norm * gains[1:2]).astype(HALF)

        for c in range(0, width, 256):
            ns.n2_t[c : c + 256] = jnp.transpose(n2[:, c : c + 256].astype(F32)).astype(HALF)

    per = width // 3

    def run_sum(index, stage):
        size = ff if index < 3 else width

        def emit(value):
            if index < 3:
                j = index * third
                ns.o_e[:, j : j + third] = value[:, :third]
                ns.o_e[:, ff + j : ff + j + third] = value[:, third : 2 * third]
                ns.o_c[:, j : j + third] = value[:, 2 * third :]
            elif index == 3:
                ns.o_o[...] = value
            else:
                for k in range(3):
                    j = k * width + (index - 4) * per
                    ns.o_j[:, j : j + per] = value[:, k * per : (k + 1) * per]

        bufs = [getattr(ns, "r%d_%d" % (k, index)) for k in range(5)]
        bufs += [ns.bf0.at[0, index % 2], ns.bf1.at[0, index % 2, 0]]
        bufs += [getattr(ns, "s%d" % k).at[index % 2] for k in range(3, 5)]
        return sum_stage(
            views[SUM_STEEP[index]],
            stage,
            ns.grads.at[index % 2],
            bufs,
            (ns.s_send, ns.s_recv),
            index,
            size,
            emit,
        )

    def sum_task(i, stage):
        def run():
            for copy in copies.pop((Kind.s, i), ()):
                copy.wait()
            copies[Kind.s, i] = run_sum(i, stage)

        return run

    for i in range(7):
        for stage in range(1, 6):
            tasks[Kind.s, i, stage] = sum_task(i, stage)

    def weight_grad(index, offset, left, right, columns):
        step = min(columns, 384)

        @pl.loop(0, columns // step)
        def _(i):
            base = pl.multiple_of(i * step, step)
            ns.grads[index % 2, :, pl.ds(offset + base, step)] = dot(
                left[...], right[:, pl.ds(base, step)], NN
            )

    e, de, dn = ns.e, ns.de, ns.dn

    def forward_third(j):
        w = wf_all.at[j]
        for c in range(0, 2 * third, third):
            e[:, c : c + third] = dot(n2[...], w[:, c : c + third], NN)
        e[:, 2 * third :] = dot(cot[...], w[:, 2 * third :], NN)

        @pl.loop(0, blocks)
        def _(i):
            rows = rows_of(i)
            pre, gate, d_mixed = (e[rows, c * third : (c + 1) * third] for c in range(3))
            cumul = 0.5 * (1.0 + lax.erf(pre * SQRT_HALF))
            active = pre * cumul
            slope = cumul + pre * jnp.exp(-0.5 * pre * pre) * INV_ROOT_TAU
            de[j, rows, :third] = (d_mixed * gate * slope).astype(HALF)
            de[j, rows, third : 2 * third] = (d_mixed * active).astype(HALF)
            de[j, rows, 2 * third :] = (active * gate).astype(HALF)

    def grad_third(j):
        weight_grad(j, 0, ns.n2_t, de.at[j], 2 * third)
        weight_grad(j, 2 * third, ns.cot_t, de.at[j, :, 2 * third :], third)
        sum_task(j, 0)()

    def back_third(j):
        back = dot(de[j, :, : 2 * third], wf_all[j, :, : 2 * third], NT)
        dn[...] = back if j == 0 else dn[...] + back

    for j in range(3):
        tasks[Kind.fwd, j] = functools.partial(forward_third, j)
        tasks[Kind.grad, j] = functools.partial(grad_third, j)
        tasks[Kind.back, j] = functools.partial(back_third, j)

    def norm_down(upstream, norm, inv, gain):
        scaled = upstream * gain
        mean = jnp.mean(scaled, axis=-1, keepdims=True)
        along = jnp.mean(scaled * norm, axis=-1, keepdims=True)
        return inv * (scaled - mean - norm * along)

    part = ns.part
    def fold(v):
        return sum(v[k : k + 8] for k in range(0, 32, 8))

    @task(Kind.norm2b)
    def _():
        part[...] = jnp.zeros(part.shape, F32)

        @pl.loop(0, blocks)
        def _(i):
            rows = rows_of(i)
            up, norm = dn[rows], ns.norm2[rows]
            part[1] += fold(up * norm)
            d_resid = cot[rows].astype(F32) + norm_down(up, norm, ns.inv2[rows], gains[1:2])
            dn[rows] = d_resid
            n1[rows] = d_resid.astype(HALF)

    @task(Kind.datt)
    def _():
        @pl.loop(0, width // 256)
        def _(i):
            rows = pl.ds(pl.multiple_of(i * 256, 256), 256)
            n2[:, rows] = dot(n1[:tokens], wo_all[rows, :], NT).astype(HALF)

    @task(Kind.grad, 3)
    def _():
        @pl.loop(0, width // 256)
        def _(i):
            cols = pl.ds(pl.multiple_of(i * 256, 256), 256)
            ns.grads[1, cols, :width] = dot(ns.att[:, cols], n1[:tokens], TN)

        sum_task(3, 0)()

    n1_own, n1_all = ns.n1_t.at[:, :tokens], ns.n1_t

    def grad_joined(h):
        cols = slice(h * per, (h + 1) * per)
        v_cols = slice(width + h * per, width + (h + 1) * per)
        weight_grad(4 + h, 0, n1_own, dq.at[:, cols], per)
        weight_grad(4 + h, per, n1_all, dkv.at[:, cols], per)
        weight_grad(4 + h, 2 * per, n1_all, dkv.at[:, v_cols], per)
        sum_task(4 + h, 0)()

    rim_out = ns.rim_out
    dq, dkv = ns.dq, ns.dkv

    def attend_back(b, i):
        cols = pl.ds(pl.multiple_of(i * PAIR, PAIR), PAIR)
        rows = slice(b * length, (b + 1) * length)
        qs = stack_heads(q[rows, cols])
        ups = stack_heads(n2[rows, cols])
        scores = dot(kx[b, :, cols], qs, NT) * scale + ns.bias[...]
        probs = jnp.exp(scores - ns.stat[b * pairs + i])
        d_probs = dot(vx[b, :, cols], ups, NT)
        centred = d_probs - jnp.sum(probs * d_probs, axis=0, keepdims=True)
        d_scores = (probs * centred * scale).astype(HALF)
        d_q = pick_heads(dot(d_scores, kx[b, :, cols], TN))
        dq[rows, cols] = unturn(d_q).astype(HALF)
        d_k = dot(d_scores, qs, NN)
        d_v = dot(probs.astype(HALF), ups, NN)
        v_cols = pl.ds(pl.multiple_of(width + i * PAIR, PAIR), PAIR)
        for k in range(2):
            part_rows = slice(k * tokens + b * length, k * tokens + (b + 1) * length)
            piece = slice(k * length, (k + 1) * length)
            dkv[part_rows, cols] = unturn(d_k[piece], k).astype(HALF)
            dkv[part_rows, v_cols] = d_v[piece].astype(HALF)

    for j in range(6):
        tasks[Kind.attb, j] = some_pairs(attend_back, j % 2 * 3 + j // 2)

    for h in range(3):
        tasks[Kind.grad, 4 + h] = functools.partial(grad_joined, h)

    @task(Kind.backq)
    def _():
        e[:, :width] = dot(dq[...], wj_all[:, :width], NT)

    @task(Kind.backkv)
    def _():
        e[:, :width] = e[:, :width] + dot(dkv[:tokens], wj_all[:, width:], NT)

    rims = halo(1, rim_in.at[0], rim_out.at[0], rim_in.at[1], rim_out.at[1])

    @task(Kind.backh)
    def _():
        total = jnp.zeros((1, width), F32)
        for b in range(2):
            first = tokens + b * length
            back = dot(dkv[first : first + length], wj_all[:, width:], NT)
            for side in range(2):
                piece = back[side * half : (side + 1) * half]
                rim_out[side, b] = piece.astype(HALF)
                norm = centre(xh[side, b].astype(F32))[0]
                total = total + jnp.sum(piece * norm, axis=0, keepdims=True)
        part[0, 0:1] = part[0, 0:1] + total

    @task(Kind.rim)
    def _():
        exchange_start(rims)

    @task(Kind.rimw)
    def _():
        exchange_wait(rims)

    gain_sum, gain_in = ns.gain_sum, ns.gain_in
    gain_sems = (ns.n_send, ns.n_recv)

    def gain_push(t):
        peer = at.peers[GAIN_PATH[t]]
        copies[Kind.n] = push(gain_sum.at[t], gain_in.at[t], gain_sems, (t,), peer)

    @task(Kind.n, 0)
    def _():
        @pl.loop(0, blocks)
        def _(i):
            rows = rows_of(i)
            part[0] += fold(e[rows, :width] * ns.norm1[rows])

        gain_sum[0] = jnp.zeros(gain_sum.shape[1:], F32)
        for k in range(2):
            gain_sum[0, k : k + 1] = jnp.sum(part[k], axis=0, keepdims=True)
        gain_push(0)

    @task(Kind.norm1b)
    def _():
        for b in range(2):
            for side in range(2):
                first = b * length + side * half
                for k in range(0, half, 32):
                    rows = slice(first + k, first + k + 32)
                    up = e[rows, :width] + rim_in[side, b, k : k + 32].astype(F32)
                    d_source = norm_down(up, ns.norm1[rows], ns.inv1[rows], gains[0:1])
                    ns.grad[rows] = (dn[rows] + d_source).astype(HALF)

    def gain_task(t):
        def run():
            copies.pop(Kind.n).wait()
            gain_sum[t] = gain_sum[t - 1] + gain_in[t - 1]
            if t < 5:
                gain_push(t)
                return
            shift = ((32 - (at.dp * 8 + seq)) * ROWS) % width
            own = pltpu.roll(gain_sum[5], shift, 1)
            ns.o_g1[...] = own[0:1, :ROWS]
            ns.o_g2[...] = own[1:2, :ROWS]

        return run

    for t in range(1, 6):
        tasks[Kind.n, t] = gain_task(t)

    @task(Kind.final)
    def _():
        @pl.loop(0, width // 256)
        def _(i):
            cols = pl.ds(pl.multiple_of(i * 256, 256), 256)
            value = resid[:, cols]
            for j in range(3):
                value = value + dot(de[j, :, 2 * third :], wf_all[j, cols, 2 * third :], NT)
            ns.out[:, cols] = value.astype(HALF)

    steps = [run for _, run in sorted(tasks.items(), key=lambda item: item[0])]
    assert sorted(ORDER) == list(range(len(steps)))
    for number in ORDER:
        steps[number]()


def fused_layer(x, cot, wj, wo, we, wc, g1, g2, freq):
    tokens, width = x.shape
    ff = wc.shape[1]
    length = tokens // 2
    half = WINDOW // 2
    span = length + 2 * half
    pairs = width // PAIR
    lead = (2, 2, 2, 2, 2, ROWS)
    ins = dict(x=x, cot=cot, wj=wj, wo=wo, we=we, wc=wc, g1=g1, g2=g2, freq=freq)
    outs = dict(
        out=((tokens, width), HALF),
        grad=((tokens, width), HALF),
        o_e=((ROWS, 2 * ff), F32),
        o_c=((ROWS, ff), F32),
        o_o=((ROWS, width), F32),
        o_j=((ROWS, 3 * width), F32),
        o_g1=((1, ROWS), F32),
        o_g2=((1, ROWS), F32),
    )
    held = dict(bn=((2, 2, 2, 2, 2, 8, 128), F32))
    for name in ("bk", "bv", "bq", "bo"):
        held[name] = (lead + (width,), HALF)
    for j in range(3):
        held["bf%d" % j] = (lead + (ff,), HALF)
    held.update(
        wj_all=((width, 3 * width), HALF),
        wo_all=((width, width), HALF),
        wf_all=((3, width, ff), HALF),
        gains=((8, width), F32),
        cos=((2, length, PAIR), F32),
        sin=((2, length, PAIR), F32),
        xh=((2, 2, half, width), HALF),
        low=((length, PAIR), HALF),
        high=((length, PAIR), HALF),
        bias=((span, 2 * length), F32),
        norm1=((tokens, width), F32),
        inv1=((tokens, 1), F32),
        n1=((2 * tokens, width), HALF),
        n1_t=((width, 2 * tokens), HALF),
        cot_t=((width, tokens), HALF),
        q=((tokens, width), HALF),
        kx=((2, span, width), HALF),
        vx=((2, span, width), HALF),
        stat=((2 * pairs, 1, 2 * length), F32),
        att=((tokens, width), HALF),
        resid=((tokens, width), F32),
        norm2=((tokens, width), F32),
        inv2=((tokens, 1), F32),
        n2=((tokens, width), HALF),
        n2_t=((width, tokens), HALF),
        e=((tokens, ff), F32),
        de=((3, tokens, ff), HALF),
        dn=((tokens, width), F32),
        part=((2, 8, width), F32),
        dq=((tokens, width), HALF),
        dkv=((2 * tokens, 2 * width), HALF),
        rim_out=((2, 2, half, width), HALF),
        rim_in=((2, 2, half, width), HALF),
        gain_sum=((6, 8, width), F32),
        gain_in=((5, 8, width), F32),
        grads=((2, width, ff), F32),
        s3=((2, 2, ROWS, ff), F32),
        s4=((2, ROWS, ff), F32),
    )
    for i in range(7):
        size = ff if i < 3 else width
        held["r0_%d" % i] = ((2, 8 * ROWS, size), F32)
        held["r1_%d" % i] = ((2, 2, 2, ROWS, size), HALF)
        held["r2_%d" % i] = ((2, 2, ROWS, size), HALF)
        held["r3_%d" % i] = ((2, ROWS, size), F32)
        held["r4_%d" % i] = ((ROWS, size), F32)
    sems = {}
    for side in ("send", "recv"):
        sems["g_" + side] = (8, 5)
        sems["h_" + side] = (2, 2)
        sems["s_" + side] = (7, 6)
        sems["n_" + side] = (5,)
    vmem = pl.BlockSpec(memory_space=pltpu.VMEM)
    names = tuple(ins) + tuple(outs) + tuple(held) + tuple(sems)
    return pl.pallas_call(
        functools.partial(layer_kernel, names),
        out_shape=tuple(jax.ShapeDtypeStruct(*v) for v in outs.values()),
        in_specs=[vmem] * len(ins),
        out_specs=(vmem,) * len(outs),
        scratch_shapes=[pltpu.VMEM(*v) for v in held.values()]
        + [pltpu.SemaphoreType.DMA(v) for v in sems.values()],
        compiler_params=pltpu.CompilerParams(
            collective_id=0, has_side_effects=True, vmem_limit_bytes=VMEM_LIMIT
        ),
    )(*ins.values())


VMEM_LIMIT = 63 * MIB


def hand_on(arrays):
    vmem = pl.BlockSpec(memory_space=pltpu.VMEM)
    count = len(arrays)

    def kernel(*refs):
        for source, target in zip(refs[:count], refs[count:]):
            target[...] = source[...]

    return pl.pallas_call(
        kernel,
        out_shape=tuple(jax.ShapeDtypeStruct(a.shape, a.dtype) for a in arrays),
        in_specs=[vmem] * count,
        out_specs=(vmem,) * count,
    )(*arrays)


def fast_layer(
    layer_input, cotangent, w_joined, w_output, w_expand, w_contract, gain_one, gain_two
):
    width = layer_input.shape[-1]
    tokens = layer_input.shape[0] * layer_input.shape[1] * layer_input.shape[2]
    half_dim = HEAD_DIM // 2
    freqs = np.float32(ROPE_BASE) ** (-np.arange(half_dim, dtype=np.float32) * 2.0 / HEAD_DIM)
    freq = np.tile(freqs.astype(np.float32), PAIR // half_dim)[None, :]
    outs = fused_layer(
        layer_input.reshape(tokens, width),
        cotangent.reshape(tokens, width),
        w_joined,
        w_output,
        w_expand,
        w_contract.T,
        gain_one[None, :],
        gain_two[None, :],
        freq,
    )
    out, grad, o_e, o_c, o_o, o_j, o_g1, o_g2 = hand_on(outs)
    return (
        out.reshape(layer_input.shape),
        grad.reshape(layer_input.shape),
        o_j,
        o_o,
        o_e,
        o_c.T,
        o_g1[0],
        o_g2[0],
    )


def solution(mesh):
    fits = mesh.shape["dp"] == 4 and mesh.shape["seq"] == 8
    body = fast_layer if fits else plain_layer
    placed = (
        P(None, "dp", "seq", None),
        P(None, "dp", "seq", None),
        P(("dp", "seq"), None),
        P(("dp", "seq"), None),
        P(("dp", "seq"), None),
        P(None, ("dp", "seq")),
        P(("dp", "seq")),
        P(("dp", "seq")),
    )
    return jax.shard_map(
        body,
        mesh=mesh,
        in_specs=placed,
        out_specs=(
            P(None, "dp", "seq", None),
            P(None, "dp", "seq", None),
            P(("dp", "seq"), None),
            P(("dp", "seq"), None),
            P(("dp", "seq"), None),
            P(None, ("dp", "seq")),
            P(("dp", "seq")),
            P(("dp", "seq")),
        ),
        check_vma=False,
    )
```

```python
import enum
import functools
import types

import jax
import jax.numpy as jnp
from jax import lax
import numpy as np
from jax.experimental import pallas as pl
from jax.experimental.pallas import tpu as pltpu
from jax.sharding import PartitionSpec as P

HEADS = 12
HEAD_DIM = 64
WINDOW = 128


NORM_EPS = 1e-05
ROPE_BASE = 10000.0
MASK_FILL = -1e30
SQRT_HALF = 0.7071067811865476
INV_ROOT_TAU = 0.3989422804014327


LANES = 128


def pair_sum(value, outer):
    outer_size = lax.axis_size(outer)
    pairs = outer_size // 2
    core = lax.axis_index(outer) % 2
    blocks = value.reshape(pairs, 2, value.shape[0] // outer_size, value.shape[1])
    other = lax.dynamic_index_in_dim(blocks, 1 - core, axis=1, keepdims=False)
    own = lax.dynamic_index_in_dim(blocks, core, axis=1, keepdims=False)
    swap = [(i, i ^ 1) for i in range(outer_size)]
    return own + lax.ppermute(other, outer, swap)


def line_sum(value, outer):
    outer_size = lax.axis_size(outer)
    if outer_size == 4:
        line = lax.axis_index(outer) // 2
        other = lax.dynamic_index_in_dim(value, 1 - line, axis=0, keepdims=False)
        own = lax.dynamic_index_in_dim(value, line, axis=0, keepdims=False)
        swap = [(i, i ^ 2) for i in range(outer_size)]
        arrived = lax.ppermute(other.astype(jnp.bfloat16), outer, swap)
        value = own + arrived.astype(jnp.float32)
    else:
        groups = [list(range(c, outer_size, 2)) for c in range(2)]
        arrived = lax.all_to_all(
            value.astype(jnp.bfloat16), outer, 0, 0, axis_index_groups=groups
        )
        value = jnp.sum(arrived.astype(jnp.float32), axis=0)
    return value


def ring_sum(value, inner):
    inner_size = lax.axis_size(inner)
    blocks = value.reshape(inner_size, value.shape[0] // inner_size, value.shape[1])
    return jnp.sum(lax.all_to_all(blocks, inner, 0, 0), axis=0)


def norm_apply(values, gain):
    center = jnp.mean(values, axis=-1, keepdims=True)
    shifted = values - center
    inv_std = lax.rsqrt(jnp.mean(shifted * shifted, axis=-1, keepdims=True) + NORM_EPS)
    normed = shifted * inv_std
    return (normed * gain.astype(jnp.float32), normed, inv_std)


def norm_back(upstream, normed, inv_std, gain):
    scaled = upstream * gain.astype(jnp.float32)
    inner = (
        scaled
        - jnp.mean(scaled, axis=-1, keepdims=True)
        - normed * jnp.mean(scaled * normed, axis=-1, keepdims=True)
    )
    return (inv_std * inner, jnp.sum(upstream * normed, axis=(0, 1)))


def gelu_slope(values):
    cumul = 0.5 * (1.0 + jax.scipy.special.erf(values * SQRT_HALF))
    return cumul + values * jnp.exp(-0.5 * values * values) * INV_ROOT_TAU


def rope_tables(positions, head_dim):
    half_dim = head_dim // 2
    freqs = ROPE_BASE ** (-jnp.arange(half_dim).astype(jnp.float32) * 2.0 / head_dim)
    angles = positions.astype(jnp.float32)[:, None] * freqs[None, :]
    return (jnp.cos(angles)[:, None, :], jnp.sin(angles)[:, None, :])


def rotate(values, cosine, sine):
    half_dim = values.shape[-1] // 2
    first = values[..., :half_dim]
    second = values[..., half_dim:]
    return jnp.concatenate(
        [first * cosine - second * sine, second * cosine + first * sine], axis=-1
    )


def unrotate(values, cosine, sine):
    half_dim = values.shape[-1] // 2
    first = values[..., :half_dim]
    second = values[..., half_dim:]
    return jnp.concatenate(
        [first * cosine + second * sine, second * cosine - first * sine], axis=-1
    )


def plain_layer(
    layer_input, cotangent, w_joined, w_output, w_expand, w_contract, gain_one, gain_two
):
    micro, local_batch, group, width = layer_input.shape
    heads = HEADS
    head_dim = HEAD_DIM
    half = WINDOW // 2
    ffn = w_contract.shape[0]
    batch = micro * local_batch
    scale = head_dim ** (-0.5)
    axes = ("dp", "seq")
    seq_count = lax.axis_size("seq")
    up = [(i, i + 1) for i in range(seq_count - 1)]
    down = [(j, i) for i, j in up]
    group_start = lax.axis_index("seq") * group
    cosine, sine = rope_tables(group_start + jnp.arange(group, dtype=jnp.int32), head_dim)
    query_pos = group_start + jnp.arange(group, dtype=jnp.int32)[:, None]
    key_pos = group_start - half + jnp.arange(group + 2 * half, dtype=jnp.int32)[None, :]
    allowed = (
        (jnp.abs(query_pos - key_pos) <= half) & (key_pos >= 0) & (key_pos < group * seq_count)
    )
    gains = jnp.pad(jnp.stack([gain_one, gain_two], axis=1), ((0, 0), (0, LANES - 2)))
    pack_one = jnp.concatenate([w_joined, gains], axis=1)
    pack_two = jnp.concatenate([w_expand, w_contract.T, w_output], axis=1)
    full_one = lax.all_gather(pack_one, axes, axis=0, tiled=True)
    full_two = lax.all_gather(pack_two, axes, axis=0, tiled=True)
    full_joined = full_one[:, : 3 * width]
    full_gain_one = full_one[:, 3 * width]
    full_gain_two = full_one[:, 3 * width + 1]
    full_expand = full_two[:, : 2 * ffn]
    full_contract = full_two[:, 2 * ffn : 3 * ffn]
    full_output = full_two[:, 3 * ffn :]

    source32 = layer_input.reshape(batch, group, width).astype(jnp.float32)
    upstream_half = cotangent.reshape(batch, group, width)
    normed_f, norm_one, inv_one = norm_apply(source32, full_gain_one)
    normed_one = normed_f.astype(jnp.bfloat16)
    joined = jnp.einsum(
        "bcd,de->bce", normed_one, full_joined, preferred_element_type=jnp.float32
    )
    shape_heads = (batch, group, heads, head_dim)
    k_rot = rotate(joined[..., width : 2 * width].reshape(shape_heads), cosine, sine).astype(
        jnp.bfloat16
    )
    v_half = joined[..., 2 * width :].astype(jnp.bfloat16)
    key_value = jnp.stack([k_rot.reshape(batch, group, width), v_half])
    before = lax.ppermute(key_value[:, :, group - half :], "seq", up)
    after = lax.ppermute(key_value[:, :, :half], "seq", down)
    q_rot = rotate(joined[..., :width].reshape(shape_heads), cosine, sine).astype(jnp.bfloat16)
    extended = jnp.concatenate([before, key_value, after], axis=2)
    ext_shape = (batch, group + 2 * half, heads, head_dim)
    key_rows = extended[0].reshape(ext_shape)
    value_rows = extended[1].reshape(ext_shape)
    scores = (
        jnp.einsum("bqhd,bkhd->bhqk", q_rot, key_rows, preferred_element_type=jnp.float32)
        * scale
    )
    scores = jnp.where(allowed[None, None], scores, MASK_FILL)
    row_max = jnp.max(scores, axis=-1, keepdims=True)
    log_total = row_max + jnp.log(jnp.sum(jnp.exp(scores - row_max), axis=-1, keepdims=True))
    probs = jnp.exp(scores - log_total)
    probs_half = probs.astype(jnp.bfloat16)
    attended = jnp.einsum(
        "bhqk,bkhd->bqhd", probs_half, value_rows, preferred_element_type=jnp.float32
    )
    attended = attended.astype(jnp.bfloat16).reshape(batch, group, width)
    resid = source32 + jnp.einsum(
        "bcd,de->bce", attended, full_output, preferred_element_type=jnp.float32
    )
    normed_g, norm_two, inv_two = norm_apply(resid, full_gain_two)
    normed_two = normed_g.astype(jnp.bfloat16)
    expanded = jnp.einsum(
        "bcd,de->bce", normed_two, full_expand, preferred_element_type=jnp.float32
    )
    pre_act = expanded[..., :ffn]
    gate_part = expanded[..., ffn:]
    activated = jax.nn.gelu(pre_act, approximate=False)
    mixed = (activated * gate_part).astype(jnp.bfloat16)
    contract_acc = jnp.einsum(
        "bcd,bcf->df", upstream_half, mixed, preferred_element_type=jnp.float32
    )
    d_mixed = jnp.einsum(
        "bcd,df->bcf", upstream_half, full_contract, preferred_element_type=jnp.float32
    )
    d_expanded = jnp.concatenate(
        [d_mixed * gate_part * gelu_slope(pre_act), d_mixed * activated], axis=-1
    ).astype(jnp.bfloat16)
    expand_acc = jnp.einsum(
        "bcd,bce->de", normed_two, d_expanded, preferred_element_type=jnp.float32
    )
    ffn_grads, d_expanded = lax.optimization_barrier(
        (jnp.concatenate([expand_acc, contract_acc], axis=1), d_expanded)
    )
    ffn_pair = pair_sum(ffn_grads, "dp")
    d_normed_two = jnp.einsum(
        "bce,de->bcd", d_expanded, full_expand, preferred_element_type=jnp.float32
    )
    d_resid_n, gain_two_part = norm_back(d_normed_two, norm_two, inv_two, full_gain_two)
    d_resid = upstream_half.astype(jnp.float32) + d_resid_n
    d_resid_half = d_resid.astype(jnp.bfloat16)
    ffn_pair, d_resid_half = lax.optimization_barrier((ffn_pair, d_resid_half))
    ffn_line = line_sum(ffn_pair, "dp")
    d_attended = jnp.einsum(
        "bce,de->bcd", d_resid_half, full_output, preferred_element_type=jnp.float32
    )
    d_attended = d_attended.astype(jnp.bfloat16).reshape(shape_heads)
    d_probs = jnp.einsum(
        "bqhd,bkhd->bhqk", d_attended, value_rows, preferred_element_type=jnp.float32
    )
    centred = d_probs - jnp.sum(probs * d_probs, axis=-1, keepdims=True)
    d_scores = (probs * centred * scale).astype(jnp.bfloat16)
    d_key_ext = jnp.einsum(
        "bhqk,bqhd->bkhd", d_scores, q_rot, preferred_element_type=jnp.float32
    )
    d_value_ext = jnp.einsum(
        "bhqk,bqhd->bkhd", probs_half, d_attended, preferred_element_type=jnp.float32
    )
    ext_grads = jnp.stack(
        [
            d_key_ext.reshape(batch, group + 2 * half, width),
            d_value_ext.reshape(batch, group + 2 * half, width),
        ]
    )
    rims = ext_grads.astype(jnp.bfloat16)
    ffn_line, rims = lax.optimization_barrier((ffn_line, rims))
    ffn_sum = ring_sum(ffn_line, "seq")
    from_left = lax.ppermute(rims[:, :, group + half :], "seq", up).astype(jnp.float32)
    from_right = lax.ppermute(rims[:, :, :half], "seq", down).astype(jnp.float32)
    d_query = jnp.einsum(
        "bhqk,bkhd->bqhd", d_scores, key_rows, preferred_element_type=jnp.float32
    )
    output_acc = jnp.einsum(
        "bcd,bce->de", attended, d_resid_half, preferred_element_type=jnp.float32
    )
    final = resid + jnp.einsum(
        "bcf,df->bcd", mixed, full_contract, preferred_element_type=jnp.float32
    )
    own_grads = ext_grads[:, :, half : half + group]
    own_grads = own_grads + jnp.pad(
        from_left, ((0, 0), (0, 0), (0, group - half), (0, 0))
    ) + jnp.pad(from_right, ((0, 0), (0, 0), (group - half, 0), (0, 0)))
    d_key = unrotate(own_grads[0].reshape(shape_heads), cosine, sine).reshape(
        batch, group, width
    )
    d_query_flat = unrotate(d_query, cosine, sine).reshape(batch, group, width)
    d_joined = jnp.concatenate([d_query_flat, d_key, own_grads[1]], axis=-1).astype(
        jnp.bfloat16
    )
    d_normed_one = jnp.einsum(
        "bce,de->bcd", d_joined, full_joined, preferred_element_type=jnp.float32
    )
    d_source, gain_one_part = norm_back(d_normed_one, norm_one, inv_one, full_gain_one)
    input_grad = (d_resid + d_source).astype(jnp.bfloat16)
    joined_acc = jnp.einsum(
        "bcd,bce->de", normed_one, d_joined, preferred_element_type=jnp.float32
    )
    gain_parts = jnp.pad(
        jnp.stack([gain_one_part, gain_two_part], axis=1), ((0, 0), (0, LANES - 2))
    )
    last_grads = jnp.concatenate([joined_acc, output_acc, gain_parts], axis=1)
    last_sum = ring_sum(line_sum(pair_sum(last_grads, "dp"), "dp"), "seq")
    return (
        final.astype(jnp.bfloat16).reshape(layer_input.shape),
        input_grad.reshape(layer_input.shape),
        last_sum[:, : 3 * width],
        last_sum[:, 3 * width : 4 * width],
        ffn_sum[:, : 2 * ffn],
        ffn_sum[:, 2 * ffn :].T,
        last_sum[:, 4 * width],
        last_sum[:, 4 * width + 1],
    )


MESH = pl.DeviceIdType.MESH
ROWS = 24
MIB = 2**20
F32 = jnp.float32
HALF = jnp.bfloat16
PAIR = 128


def place(steep=False):
    dp, seq = lax.axis_index("dp"), lax.axis_index("seq")
    y, core = dp // 2, dp % 2
    z, x = seq // 2, seq % 2
    zh, zl = z // 2, z % 2
    turn = 1 if steep else core
    peers = dict(
        pair=(dp + 1 - 2 * core, seq),
        r=(dp + 2 * turn * (1 - 2 * y), seq + (1 - turn) * (1 - 2 * x)),
        p=(dp + 2 * (1 - turn) * (1 - 2 * y), seq + turn * (1 - 2 * x)),
        zl=(dp, seq + 2 - 4 * zl),
        zh=(dp, seq + 4 - 8 * zh),
        left=(dp, (seq + 7) % 8),
        right=(dp, (seq + 1) % 8),
    )
    r = x * (1 - turn) + y * turn
    p = y * (1 - turn) + x * turn
    return types.SimpleNamespace(dp=dp, seq=seq, core=core, turn=turn, zh=zh, zl=zl, r=r, p=p, peers=peers)


def meet(at):
    barrier = pltpu.get_barrier_semaphore()
    for peer in at.peers.values():
        pl.semaphore_signal(barrier, inc=1, device_id=peer, device_id_type=MESH)
    pl.semaphore_wait(barrier, len(at.peers))


def remote(src, dst, sems, where, peer):
    send, recv = sems
    return pltpu.make_async_remote_copy(
        src_ref=src,
        dst_ref=dst,
        send_sem=send.at[where],
        recv_sem=recv.at[where],
        device_id=peer,
        device_id_type=MESH,
    )


def push(*args):
    copy = remote(*args)
    copy.start()
    return copy


def gather_spot(at, path, stage=0):
    return (at.core,) + tuple(getattr(at, name) for name in reversed(path[stage:]))


def gather_send(at, path, buf, sems, group, stage):
    part = buf.at[gather_spot(at, path, stage)]
    name = path[stage] if stage < 4 else "pair"
    return push(part, part, sems, (group, stage), at.peers[name])


def plane_index(path, steep, core, y, z, x):
    r, p = (y, x) if steep or core else (x, y)
    place = dict(r=r, p=p, zh=z // 2, zl=z % 2)
    return (core,) + tuple(place[name] for name in reversed(path))


def relay(path, steep, buf, store):
    for core in range(2):
        for y in range(2):
            for z in range(4):
                blocks = [buf[plane_index(path, steep, core, y, z, x)].astype(F32) for x in range(2)]
                store(y * 384 + core * 192 + z * 48, jnp.concatenate(blocks, axis=0).astype(HALF))


def relay_gains(path, steep, buf, gains):
    width = gains.shape[1]
    total = jnp.zeros((8, width), F32)
    row, lane = (lax.broadcasted_iota(jnp.int32, (8, 128), k) for k in range(2))
    valid = (row < 2) & (lane < ROWS)
    for core in range(2):
        for y in range(2):
            for z in range(4):
                for x in range(2):
                    block = jnp.where(valid, buf[plane_index(path, steep, core, y, z, x)], 0.0)
                    wide = jnp.concatenate([block, jnp.zeros((8, width - 128), F32)], axis=1)
                    shift = ROWS * (y * 16 + core * 8 + z * 2 + x)
                    total = total + (pltpu.roll(wide, shift, 1) if shift else wide)
    gains[...] = total


def block_row(at, p, z, r):
    y = p * (1 - at.turn) + r * at.turn
    x = r * (1 - at.turn) + p * at.turn
    return y, pl.multiple_of(z * 48 + x * ROWS, 8)


def sum_stage(at, stage, grads, bufs, sems, index, width, emit):
    r0, r1, r2, r3, r4, s1, s2, s3, s4 = bufs
    core, r, p, zh, zl = at.core, at.r, at.p, at.zh, at.zl
    peers = at.peers
    w = slice(0, width)

    def kept(pp, z):
        y, row = block_row(at, pp, z, r)
        return y, pl.ds(row, ROWS)

    if stage == 0:
        copies = []
        for y in range(2):
            rows = pl.ds(pl.multiple_of(y * 384 + (1 - core) * 192, 192), 192)
            copies.append(push(grads.at[rows, w], r0.at[y], sems, (index, y), peers["pair"]))
        return copies
    if stage == 1:

        @pl.loop(0, 8)
        def _(i):
            pp, z = i // 4, i % 4
            y, row = block_row(at, pp, z, 1 - r)
            base = pl.multiple_of(y * 384 + core * 192 + row, 8)
            s1[pp, z // 2, z % 2, :, w] = (grads[pl.ds(base, ROWS), w] + r0[y, pl.ds(row, ROWS)]).astype(HALF)
            y, rows = kept(pp, z)
            base = pl.multiple_of(y * 384 + core * 192 + rows.start, 8)
            r0[y, rows] = grads[pl.ds(base, ROWS), w] + r0[y, rows]

        return [push(s1.at[:, :, :, :, w], r1, sems, (index, 2), peers["r"])]
    if stage == 2:

        @pl.loop(0, 4)
        def _(z):
            zh, zl = z // 2, z % 2
            s2[zh, zl, :, w] = (r0[kept(1 - p, z)] + r1[1 - p, zh, zl].astype(F32)).astype(HALF)
            r0[kept(p, z)] = r0[kept(p, z)] + r1[p, zh, zl].astype(F32)

        return [push(s2.at[:, :, :, w], r2, sems, (index, 3), peers["p"])]
    if stage == 3:
        for h in range(2):
            far, near = 2 * h + 1 - zl, 2 * h + zl
            s3[h, :, w] = r0[kept(p, far)] + r2[h, 1 - zl].astype(F32)
            r0[kept(p, near)] = r0[kept(p, near)] + r2[h, zl].astype(F32)
        return [push(s3.at[:, :, w], r3, sems, (index, 4), peers["zl"])]
    if stage == 4:
        s4[:, w] = r0[kept(p, 2 * (1 - zh) + zl)] + r3[1 - zh]
        return [push(s4.at[:, w], r4, sems, (index, 5), peers["zh"])]
    emit((r0[kept(p, 2 * zh + zl)] + r3[zh]) + r4[...])
    return []


GAIN_PATH = ("pair", "r", "p", "zl", "zh")


def dot(a, b, dims):
    return lax.dot_general(a, b, (dims, ((), ())), preferred_element_type=F32)


NN, NT, TN = ((1,), (0,)), ((1,), (1,)), ((0,), (0,))


def swap_halves(v):
    lane = lax.broadcasted_iota(jnp.int32, v.shape, 1) % HEAD_DIM
    return jnp.where(
        lane < HEAD_DIM // 2,
        pltpu.roll(v, PAIR - HEAD_DIM // 2, 1),
        pltpu.roll(v, HEAD_DIM // 2, 1),
    )


class Kind(enum.IntEnum):
    g = 0
    s = 1
    pre = 2
    n1 = 3
    n1h = 4
    halo = 5
    halow = 6
    proj = 7
    att = 8
    oproj = 9
    norm2 = 10
    fwd = 11
    grad = 12
    back = 13
    norm2b = 14
    datt = 15
    attb = 16
    backq = 17
    backkv = 18
    backh = 19
    rim = 20
    rimw = 21
    n = 22
    norm1b = 23
    final = 24
    projh = 25


PATHS = (("zh", "zl", "p", "r"), ("p", "r", "zh", "zl"))
GATHER = ((0, 0), (0, 0), (1, 0), (0, 0), (1, 1), (0, 0), (0, 0), (1, 0))
SUM_STEEP = (0, 0, 0, 0, 0, 0, 0)
ORDER = (
    0, 6, 86, 83, 1, 12, 7, 18, 2, 13, 24, 8, 87, 3, 19, 30, 25, 36, 14, 9, 4, 20, 31, 42,
    5, 26, 84, 85, 37, 15, 32, 10, 43, 21, 11, 88, 27, 38, 16, 44, 33, 17, 90, 133, 22, 39,
    23, 89, 28, 91, 45, 92, 93, 29, 94, 95, 34, 96, 97, 98, 35, 40, 99, 102, 109, 41, 100,
    103, 110, 48, 46, 53, 47, 101, 104, 49, 111, 112, 105, 113, 114, 54, 58, 115, 50, 63,
    106, 116, 55, 117, 107, 118, 119, 51, 59, 68, 108, 122, 64, 73, 120, 56, 121, 60, 125,
    132, 52, 126, 69, 78, 65, 127, 57, 74, 128, 61, 70, 129, 66, 79, 123, 130, 75, 62, 71,
    80, 67, 124, 131, 76, 72, 81, 77, 82,
)


def layer_kernel(names, *refs):
    ns = types.SimpleNamespace(**dict(zip(names, refs)))
    at = place()
    seq = at.seq
    x, cot, gains = ns.x, ns.cot, ns.gains
    tokens, width = x.shape
    third = ns.de.shape[2] // 3
    ff = 3 * third
    length = tokens // 2
    half = WINDOW // 2
    scale = HEAD_DIM ** (-0.5)
    cos, sin, low, high = ns.cos, ns.sin, ns.low, ns.high
    n1, n2, q, kx, vx = ns.n1, ns.n2, ns.q, ns.kx, ns.vx
    blocks = tokens // 32
    span = length + 2 * half
    pairs = width // PAIR

    def rows_of(i, n=32):
        return pl.ds(pl.multiple_of(i * n, n), n)

    wj, wo, we, wc = ns.wj, ns.wo, ns.we, ns.wc
    views = (at, place(True))
    group_at = [views[steep] for steep, _ in GATHER]
    paths = [PATHS[way] for _, way in GATHER]
    spots = [gather_spot(*pair) for pair in zip(group_at, paths)]
    bn = ns.bn
    for k, ref in enumerate((ns.g1, ns.g2)):
        bn[spots[0] + (slice(k, k + 1), slice(0, ROWS))] = ref[...].astype(F32)
    ns.bk[spots[1]] = wj[:, width : 2 * width]
    ns.bv[spots[2]] = wj[:, 2 * width :]
    ns.bq[spots[3]] = wj[:, :width]
    ns.bo[spots[4]] = wo[...]
    for j in range(3):
        buf, spot = getattr(ns, "bf%d" % j), spots[5 + j]
        buf[spot + (slice(None), slice(0, third))] = we[:, j * third : (j + 1) * third]
        buf[spot + (slice(None), slice(third, 2 * third))] = we[
            :, ff + j * third : ff + (j + 1) * third
        ]
        buf[spot + (slice(None), slice(2 * third, ff))] = wc[:, j * third : (j + 1) * third]

    xh, rim_in = ns.xh, ns.rim_in

    @pl.when(seq == 0)
    def _():
        xh[0] = jnp.zeros(xh.shape[1:], HALF)
        rim_in[0] = jnp.zeros(rim_in.shape[1:], HALF)

    @pl.when(seq == 7)
    def _():
        xh[1] = jnp.zeros(xh.shape[1:], HALF)
        rim_in[1] = jnp.zeros(rim_in.shape[1:], HALF)

    meet(at)

    wj_all, wo_all, wf_all = ns.wj_all, ns.wo_all, ns.wf_all

    def into(ref, offset):
        def store(row, value):
            ref[row : row + 48, offset : offset + value.shape[1]] = value

        return store

    groups = [
        (bn, None),
        (ns.bk, into(wj_all, width)),
        (ns.bv, into(wj_all, 2 * width)),
        (ns.bq, into(wj_all, 0)),
        (ns.bo, into(wo_all, 0)),
    ] + [(buf, into(wf_all.at[j], 0)) for j, buf in enumerate((ns.bf0, ns.bf1, ns.bf2))]
    copies = {}
    tasks = {}

    def task(*name):
        def note(f):
            tasks[name] = f

        return note

    def gather_task(i, stage):
        def run():
            buf, store = groups[i]
            if stage:
                copies.pop(i).wait()
            if stage < 5:
                sems = (ns.g_send, ns.g_recv)
                copies[i] = gather_send(group_at[i], paths[i], buf, sems, i, stage)
            elif store is None:
                relay_gains(paths[i], GATHER[i][0], buf, gains)
            else:
                relay(paths[i], GATHER[i][0], buf, store)

        return run

    for i in range(len(groups)):
        for stage in range(6):
            tasks[Kind.g, i, stage] = gather_task(i, stage)

    def centre(values):
        mean = jnp.mean(values, axis=-1, keepdims=True)
        shifted = values - mean
        inv = lax.rsqrt(jnp.mean(shifted * shifted, axis=-1, keepdims=True) + NORM_EPS)
        return shifted * inv, inv

    @task(Kind.pre)
    def _():
        lane = lax.broadcasted_iota(jnp.int32, (length, PAIR), 1)
        row = lax.broadcasted_iota(jnp.int32, (length, PAIR), 0)
        sign = jnp.where(lane % HEAD_DIM < HEAD_DIM // 2, -1.0, 1.0)
        beside = jnp.where(row < half, row - half, row + half)
        for k, offset in enumerate((row, beside)):
            angle = (offset + seq * length).astype(F32) * ns.freq[...]
            cos[k] = jnp.cos(angle)
            sin[k] = jnp.sin(angle) * sign
        low[...] = jnp.where(lane < HEAD_DIM, 1.0, 0.0).astype(HALF)
        high[...] = jnp.where(lane < HEAD_DIM, 0.0, 1.0).astype(HALF)
        key = lax.broadcasted_iota(jnp.int32, (span, 2 * length), 0)
        key = jnp.where(key < length, key, jnp.where(key < length + half, key - span + half, key - half))
        query = lax.broadcasted_iota(jnp.int32, (span, 2 * length), 1) % length
        key_pos = key + seq * length
        allowed = (jnp.abs(key - query) <= half) & (key_pos >= 0) & (key_pos < 8 * length)
        ns.bias[...] = jnp.where(allowed, 0.0, MASK_FILL)

        @pl.loop(0, blocks)
        def _(i):
            rows = rows_of(i)
            norm, inv = centre(x[rows].astype(F32))
            ns.norm1[rows] = norm
            ns.inv1[rows] = inv

        for c in range(0, width, 256):
            ns.cot_t[c : c + 256] = jnp.transpose(cot[:, c : c + 256].astype(F32)).astype(HALF)

    @task(Kind.n1)
    def _():
        for c in range(0, width, 256):
            value = ns.norm1[:, c : c + 256] * gains[0:1, c : c + 256]
            n1[:tokens, c : c + 256] = value.astype(HALF)
            ns.n1_t[c : c + 256, :tokens] = jnp.transpose(value).astype(HALF)

    @task(Kind.n1h)
    def _():
        for b in range(2):
            for side in range(2):
                rows = slice(tokens + b * length + side * half, tokens + b * length + (side + 1) * half)
                n1[rows] = (centre(xh[side, b].astype(F32))[0] * gains[0:1]).astype(HALF)
        for c in range(0, width, 256):
            value = n1[tokens:, c : c + 256].astype(F32)
            ns.n1_t[c : c + 256, tokens:] = jnp.transpose(value).astype(HALF)

    halo_sems = (ns.h_send, ns.h_recv)

    def halo(i, from_left, to_left, from_right, to_right):
        def left():
            return remote(to_left, from_right, halo_sems, (i, 0), at.peers["left"])

        def right():
            return remote(to_right, from_left, halo_sems, (i, 1), at.peers["right"])

        return left, right

    x_rows = x.reshape(2, length, width)
    x_halo = halo(0, xh.at[0], x_rows.at[:, :half], xh.at[1], x_rows.at[:, half:])

    def exchange_start(sides):
        pl.when(seq > 0)(lambda: sides[0]().start())
        pl.when(seq < 7)(lambda: sides[1]().start())

    def exchange_wait(sides):
        left, right = sides

        @pl.when(seq > 0)
        def _():
            left().wait_send()
            right().wait_recv()

        @pl.when(seq < 7)
        def _():
            right().wait_send()
            left().wait_recv()

    def project(offset, first, store):
        @pl.loop(0, width // 256)
        def _(i):
            base = pl.multiple_of(i * 256, 256)
            value = dot(n1[first : first + tokens], wj_all[:, pl.ds(offset + base, 256)], NN)
            for b in range(2):
                for c in range(2):
                    store(
                        b + first // length,
                        pl.ds(base + c * PAIR, PAIR),
                        value[b * length : (b + 1) * length, c * PAIR : (c + 1) * PAIR],
                    )

    def turn(v, k=0):
        return v * cos[k] + swap_halves(v) * sin[k]

    def unturn(v, k=0):
        return v * cos[k] - swap_halves(v) * sin[k]

    def store_k(b, cols, v):
        k = b // 2
        kx[b % 2, k * length : (k + 1) * length, cols] = turn(v, k).astype(HALF)

    def store_v(b, cols, v):
        k = b // 2
        vx[b % 2, k * length : (k + 1) * length, cols] = v.astype(HALF)

    def store_q(b, cols, v):
        q[b * length : (b + 1) * length, cols] = turn(v).astype(HALF)

    @task(Kind.halo)
    def _():
        exchange_start(x_halo)

    @task(Kind.halow)
    def _():
        exchange_wait(x_halo)

    @task(Kind.proj, 0)
    def _():
        project(width, 0, store_k)

    @task(Kind.proj, 2)
    def _():
        project(2 * width, 0, store_v)

    @task(Kind.proj, 1)
    def _():
        project(0, 0, store_q)

    @task(Kind.projh)
    def _():
        project(width, tokens, store_k)
        project(2 * width, tokens, store_v)

    def stack_heads(v):
        return jnp.concatenate([v * low[...], v * high[...]], axis=0)

    lower = lax.broadcasted_iota(jnp.int32, (length, PAIR), 1) < HEAD_DIM

    def pick_heads(v):
        return jnp.where(lower, v[:length], v[length:])

    def attend(b, i):
        cols = pl.ds(pl.multiple_of(i * PAIR, PAIR), PAIR)
        rows = slice(b * length, (b + 1) * length)
        qs = stack_heads(q[rows, cols])
        scores = dot(kx[b, :, cols], qs, NT) * scale + ns.bias[...]
        top = jnp.max(scores, axis=0, keepdims=True)
        raised = jnp.exp(scores - top)
        total = jnp.sum(raised, axis=0, keepdims=True)
        probs = raised * (1.0 / total)
        ns.stat[b * pairs + i] = top + jnp.log(total)
        ns.att[rows, cols] = pick_heads(dot(probs.astype(HALF), vx[b, :, cols], TN)).astype(HALF)

    def some_pairs(f, j):
        few = pairs // 3
        return lambda: pl.loop(j % 3 * few, (j % 3 + 1) * few)(functools.partial(f, j // 3))

    for j in range(6):
        tasks[Kind.att, j] = some_pairs(attend, j)

    resid = ns.resid

    @task(Kind.oproj)
    def _():
        @pl.loop(0, width // 256)
        def _(i):
            cols = pl.ds(pl.multiple_of(i * 256, 256), 256)
            resid[:, cols] = x[:, cols].astype(F32) + dot(ns.att[...], wo_all[:, cols], NN)

    @task(Kind.norm2)
    def _():
        @pl.loop(0, blocks)
        def _(i):
            rows = rows_of(i)
            norm, inv = centre(resid[rows])
            ns.norm2[rows] = norm
            ns.inv2[rows] = inv
            n2[rows] = (norm * gains[1:2]).astype(HALF)

        for c in range(0, width, 256):
            ns.n2_t[c : c + 256] = jnp.transpose(n2[:, c : c + 256].astype(F32)).astype(HALF)

    per = width // 3

    def run_sum(index, stage):
        size = ff if index < 3 else width

        def emit(value):
            if index < 3:
                j = index * third
                ns.o_e[:, j : j + third] = value[:, :third]
                ns.o_e[:, ff + j : ff + j + third] = value[:, third : 2 * third]
                ns.o_c[:, j : j + third] = value[:, 2 * third :]
            elif index == 3:
                ns.o_o[...] = value
            else:
                for k in range(3):
                    j = k * width + (index - 4) * per
                    ns.o_j[:, j : j + per] = value[:, k * per : (k + 1) * per]

        bufs = [getattr(ns, "r%d_%d" % (k, index)) for k in range(5)]
        bufs += [ns.bf0.at[0, index % 2], ns.bf1.at[0, index % 2, 0]]
        bufs += [getattr(ns, "s%d" % k).at[index % 2] for k in range(3, 5)]
        return sum_stage(
            views[SUM_STEEP[index]],
            stage,
            ns.grads.at[index % 2],
            bufs,
            (ns.s_send, ns.s_recv),
            index,
            size,
            emit,
        )

    def sum_task(i, stage):
        def run():
            for copy in copies.pop((Kind.s, i), ()):
                copy.wait()
            copies[Kind.s, i] = run_sum(i, stage)

        return run

    for i in range(7):
        for stage in range(1, 6):
            tasks[Kind.s, i, stage] = sum_task(i, stage)

    def weight_grad(index, offset, left, right, columns):
        step = min(columns, 384)

        @pl.loop(0, columns // step)
        def _(i):
            base = pl.multiple_of(i * step, step)
            ns.grads[index % 2, :, pl.ds(offset + base, step)] = dot(
                left[...], right[:, pl.ds(base, step)], NN
            )

    e, de, dn = ns.e, ns.de, ns.dn

    def forward_third(j):
        w = wf_all.at[j]
        for c in range(0, 2 * third, third):
            e[:, c : c + third] = dot(n2[...], w[:, c : c + third], NN)
        e[:, 2 * third :] = dot(cot[...], w[:, 2 * third :], NN)

        @pl.loop(0, blocks)
        def _(i):
            rows = rows_of(i)
            pre, gate, d_mixed = (e[rows, c * third : (c + 1) * third] for c in range(3))
            cumul = 0.5 * (1.0 + lax.erf(pre * SQRT_HALF))
            active = pre * cumul
            slope = cumul + pre * jnp.exp(-0.5 * pre * pre) * INV_ROOT_TAU
            de[j, rows, :third] = (d_mixed * gate * slope).astype(HALF)
            de[j, rows, third : 2 * third] = (d_mixed * active).astype(HALF)
            de[j, rows, 2 * third :] = (active * gate).astype(HALF)

    def grad_third(j):
        weight_grad(j, 0, ns.n2_t, de.at[j], 2 * third)
        weight_grad(j, 2 * third, ns.cot_t, de.at[j, :, 2 * third :], third)
        sum_task(j, 0)()

    def back_third(j):
        back = dot(de[j, :, : 2 * third], wf_all[j, :, : 2 * third], NT)
        dn[...] = back if j == 0 else dn[...] + back

    for j in range(3):
        tasks[Kind.fwd, j] = functools.partial(forward_third, j)
        tasks[Kind.grad, j] = functools.partial(grad_third, j)
        tasks[Kind.back, j] = functools.partial(back_third, j)

    def norm_down(upstream, norm, inv, gain):
        scaled = upstream * gain
        mean = jnp.mean(scaled, axis=-1, keepdims=True)
        along = jnp.mean(scaled * norm, axis=-1, keepdims=True)
        return inv * (scaled - mean - norm * along)

    part = ns.part
    def fold(v):
        return sum(v[k : k + 8] for k in range(0, 32, 8))

    @task(Kind.norm2b)
    def _():
        part[...] = jnp.zeros(part.shape, F32)

        @pl.loop(0, blocks)
        def _(i):
            rows = rows_of(i)
            up, norm = dn[rows], ns.norm2[rows]
            part[1] += fold(up * norm)
            d_resid = cot[rows].astype(F32) + norm_down(up, norm, ns.inv2[rows], gains[1:2])
            dn[rows] = d_resid
            n1[rows] = d_resid.astype(HALF)

    @task(Kind.datt)
    def _():
        @pl.loop(0, width // 256)
        def _(i):
            rows = pl.ds(pl.multiple_of(i * 256, 256), 256)
            n2[:, rows] = dot(n1[:tokens], wo_all[rows, :], NT).astype(HALF)

    @task(Kind.grad, 3)
    def _():
        @pl.loop(0, width // 256)
        def _(i):
            cols = pl.ds(pl.multiple_of(i * 256, 256), 256)
            ns.grads[1, cols, :width] = dot(ns.att[:, cols], n1[:tokens], TN)

        sum_task(3, 0)()

    n1_own, n1_all = ns.n1_t.at[:, :tokens], ns.n1_t

    def grad_joined(h):
        cols = slice(h * per, (h + 1) * per)
        v_cols = slice(width + h * per, width + (h + 1) * per)
        weight_grad(4 + h, 0, n1_own, dq.at[:, cols], per)
        weight_grad(4 + h, per, n1_all, dkv.at[:, cols], per)
        weight_grad(4 + h, 2 * per, n1_all, dkv.at[:, v_cols], per)
        sum_task(4 + h, 0)()

    rim_out = ns.rim_out
    dq, dkv = ns.dq, ns.dkv

    def attend_back(b, i):
        cols = pl.ds(pl.multiple_of(i * PAIR, PAIR), PAIR)
        rows = slice(b * length, (b + 1) * length)
        qs = stack_heads(q[rows, cols])
        ups = stack_heads(n2[rows, cols])
        scores = dot(kx[b, :, cols], qs, NT) * scale + ns.bias[...]
        probs = jnp.exp(scores - ns.stat[b * pairs + i])
        d_probs = dot(vx[b, :, cols], ups, NT)
        centred = d_probs - jnp.sum(probs * d_probs, axis=0, keepdims=True)
        d_scores = (probs * centred * scale).astype(HALF)
        d_q = pick_heads(dot(d_scores, kx[b, :, cols], TN))
        dq[rows, cols] = unturn(d_q).astype(HALF)
        d_k = dot(d_scores, qs, NN)
        d_v = dot(probs.astype(HALF), ups, NN)
        v_cols = pl.ds(pl.multiple_of(width + i * PAIR, PAIR), PAIR)
        for k in range(2):
            part_rows = slice(k * tokens + b * length, k * tokens + (b + 1) * length)
            piece = slice(k * length, (k + 1) * length)
            dkv[part_rows, cols] = unturn(d_k[piece], k).astype(HALF)
            dkv[part_rows, v_cols] = d_v[piece].astype(HALF)

    for j in range(6):
        tasks[Kind.attb, j] = some_pairs(attend_back, j % 2 * 3 + j // 2)

    for h in range(3):
        tasks[Kind.grad, 4 + h] = functools.partial(grad_joined, h)

    @task(Kind.backq)
    def _():
        e[:, :width] = dot(dq[...], wj_all[:, :width], NT)

    @task(Kind.backkv)
    def _():
        e[:, :width] = e[:, :width] + dot(dkv[:tokens], wj_all[:, width:], NT)

    rims = halo(1, rim_in.at[0], rim_out.at[0], rim_in.at[1], rim_out.at[1])

    @task(Kind.backh)
    def _():
        total = jnp.zeros((1, width), F32)
        for b in range(2):
            first = tokens + b * length
            back = dot(dkv[first : first + length], wj_all[:, width:], NT)
            for side in range(2):
                piece = back[side * half : (side + 1) * half]
                rim_out[side, b] = piece.astype(HALF)
                norm = centre(xh[side, b].astype(F32))[0]
                total = total + jnp.sum(piece * norm, axis=0, keepdims=True)
        part[0, 0:1] = part[0, 0:1] + total

    @task(Kind.rim)
    def _():
        exchange_start(rims)

    @task(Kind.rimw)
    def _():
        exchange_wait(rims)

    gain_sum, gain_in = ns.gain_sum, ns.gain_in
    gain_sems = (ns.n_send, ns.n_recv)

    def gain_push(t):
        peer = at.peers[GAIN_PATH[t]]
        copies[Kind.n] = push(gain_sum.at[t], gain_in.at[t], gain_sems, (t,), peer)

    @task(Kind.n, 0)
    def _():
        @pl.loop(0, blocks)
        def _(i):
            rows = rows_of(i)
            part[0] += fold(e[rows, :width] * ns.norm1[rows])

        gain_sum[0] = jnp.zeros(gain_sum.shape[1:], F32)
        for k in range(2):
            gain_sum[0, k : k + 1] = jnp.sum(part[k], axis=0, keepdims=True)
        gain_push(0)

    @task(Kind.norm1b)
    def _():
        for b in range(2):
            for side in range(2):
                first = b * length + side * half
                for k in range(0, half, 32):
                    rows = slice(first + k, first + k + 32)
                    up = e[rows, :width] + rim_in[side, b, k : k + 32].astype(F32)
                    d_source = norm_down(up, ns.norm1[rows], ns.inv1[rows], gains[0:1])
                    ns.grad[rows] = (dn[rows] + d_source).astype(HALF)

    def gain_task(t):
        def run():
            copies.pop(Kind.n).wait()
            gain_sum[t] = gain_sum[t - 1] + gain_in[t - 1]
            if t < 5:
                gain_push(t)
                return
            shift = ((32 - (at.dp * 8 + seq)) * ROWS) % width
            own = pltpu.roll(gain_sum[5], shift, 1)
            ns.o_g1[...] = own[0:1, :ROWS]
            ns.o_g2[...] = own[1:2, :ROWS]

        return run

    for t in range(1, 6):
        tasks[Kind.n, t] = gain_task(t)

    @task(Kind.final)
    def _():
        @pl.loop(0, width // 256)
        def _(i):
            cols = pl.ds(pl.multiple_of(i * 256, 256), 256)
            value = resid[:, cols]
            for j in range(3):
                value = value + dot(de[j, :, 2 * third :], wf_all[j, cols, 2 * third :], NT)
            ns.out[:, cols] = value.astype(HALF)

    steps = [run for _, run in sorted(tasks.items(), key=lambda item: item[0])]
    assert sorted(ORDER) == list(range(len(steps)))
    for number in ORDER:
        steps[number]()


def fused_layer(x, cot, wj, wo, we, wc, g1, g2, freq):
    tokens, width = x.shape
    ff = wc.shape[1]
    length = tokens // 2
    half = WINDOW // 2
    span = length + 2 * half
    pairs = width // PAIR
    lead = (2, 2, 2, 2, 2, ROWS)
    ins = dict(x=x, cot=cot, wj=wj, wo=wo, we=we, wc=wc, g1=g1, g2=g2, freq=freq)
    outs = dict(
        out=((tokens, width), HALF),
        grad=((tokens, width), HALF),
        o_e=((ROWS, 2 * ff), F32),
        o_c=((ROWS, ff), F32),
        o_o=((ROWS, width), F32),
        o_j=((ROWS, 3 * width), F32),
        o_g1=((1, ROWS), F32),
        o_g2=((1, ROWS), F32),
    )
    held = dict(bn=((2, 2, 2, 2, 2, 8, 128), F32))
    for name in ("bk", "bv", "bq", "bo"):
        held[name] = (lead + (width,), HALF)
    for j in range(3):
        held["bf%d" % j] = (lead + (ff,), HALF)
    held.update(
        wj_all=((width, 3 * width), HALF),
        wo_all=((width, width), HALF),
        wf_all=((3, width, ff), HALF),
        gains=((8, width), F32),
        cos=((2, length, PAIR), F32),
        sin=((2, length, PAIR), F32),
        xh=((2, 2, half, width), HALF),
        low=((length, PAIR), HALF),
        high=((length, PAIR), HALF),
        bias=((span, 2 * length), F32),
        norm1=((tokens, width), F32),
        inv1=((tokens, 1), F32),
        n1=((2 * tokens, width), HALF),
        n1_t=((width, 2 * tokens), HALF),
        cot_t=((width, tokens), HALF),
        q=((tokens, width), HALF),
        kx=((2, span, width), HALF),
        vx=((2, span, width), HALF),
        stat=((2 * pairs, 1, 2 * length), F32),
        att=((tokens, width), HALF),
        resid=((tokens, width), F32),
        norm2=((tokens, width), F32),
        inv2=((tokens, 1), F32),
        n2=((tokens, width), HALF),
        n2_t=((width, tokens), HALF),
        e=((tokens, ff), F32),
        de=((3, tokens, ff), HALF),
        dn=((tokens, width), F32),
        part=((2, 8, width), F32),
        dq=((tokens, width), HALF),
        dkv=((2 * tokens, 2 * width), HALF),
        rim_out=((2, 2, half, width), HALF),
        rim_in=((2, 2, half, width), HALF),
        gain_sum=((6, 8, width), F32),
        gain_in=((5, 8, width), F32),
        grads=((2, width, ff), F32),
        s3=((2, 2, ROWS, ff), F32),
        s4=((2, ROWS, ff), F32),
    )
    for i in range(7):
        size = ff if i < 3 else width
        held["r0_%d" % i] = ((2, 8 * ROWS, size), F32)
        held["r1_%d" % i] = ((2, 2, 2, ROWS, size), HALF)
        held["r2_%d" % i] = ((2, 2, ROWS, size), HALF)
        held["r3_%d" % i] = ((2, ROWS, size), F32)
        held["r4_%d" % i] = ((ROWS, size), F32)
    sems = {}
    for side in ("send", "recv"):
        sems["g_" + side] = (8, 5)
        sems["h_" + side] = (2, 2)
        sems["s_" + side] = (7, 6)
        sems["n_" + side] = (5,)
    vmem = pl.BlockSpec(memory_space=pltpu.VMEM)
    names = tuple(ins) + tuple(outs) + tuple(held) + tuple(sems)
    return pl.pallas_call(
        functools.partial(layer_kernel, names),
        out_shape=tuple(jax.ShapeDtypeStruct(*v) for v in outs.values()),
        in_specs=[vmem] * len(ins),
        out_specs=(vmem,) * len(outs),
        scratch_shapes=[pltpu.VMEM(*v) for v in held.values()]
        + [pltpu.SemaphoreType.DMA(v) for v in sems.values()],
        compiler_params=pltpu.CompilerParams(
            collective_id=0, has_side_effects=True, vmem_limit_bytes=VMEM_LIMIT
        ),
    )(*ins.values())


VMEM_LIMIT = 63 * MIB


def hand_on(arrays):
    vmem = pl.BlockSpec(memory_space=pltpu.VMEM)
    count = len(arrays)

    def kernel(*refs):
        for source, target in zip(refs[:count], refs[count:]):
            target[...] = source[...]

    return pl.pallas_call(
        kernel,
        out_shape=tuple(jax.ShapeDtypeStruct(a.shape, a.dtype) for a in arrays),
        in_specs=[vmem] * count,
        out_specs=(vmem,) * count,
    )(*arrays)


def fast_layer(
    layer_input, cotangent, w_joined, w_output, w_expand, w_contract, gain_one, gain_two
):
    width = layer_input.shape[-1]
    tokens = layer_input.shape[0] * layer_input.shape[1] * layer_input.shape[2]
    half_dim = HEAD_DIM // 2
    freqs = np.float32(ROPE_BASE) ** (-np.arange(half_dim, dtype=np.float32) * 2.0 / HEAD_DIM)
    freq = np.tile(freqs.astype(np.float32), PAIR // half_dim)[None, :]
    outs = fused_layer(
        layer_input.reshape(tokens, width),
        cotangent.reshape(tokens, width),
        w_joined,
        w_output,
        w_expand,
        w_contract.T,
        gain_one[None, :],
        gain_two[None, :],
        freq,
    )
    out, grad, o_e, o_c, o_o, o_j, o_g1, o_g2 = hand_on(outs)
    return (
        out.reshape(layer_input.shape),
        grad.reshape(layer_input.shape),
        o_j,
        o_o,
        o_e,
        o_c.T,
        o_g1[0],
        o_g2[0],
    )


def solution(mesh):
    fits = mesh.shape["dp"] == 4 and mesh.shape["seq"] == 8
    body = fast_layer if fits else plain_layer
    placed = (
        P(None, "dp", "seq", None),
        P(None, "dp", "seq", None),
        P(("dp", "seq"), None),
        P(("dp", "seq"), None),
        P(("dp", "seq"), None),
        P(None, ("dp", "seq")),
        P(("dp", "seq")),
        P(("dp", "seq")),
    )
    return jax.shard_map(
        body,
        mesh=mesh,
        in_specs=placed,
        out_specs=(
            P(None, "dp", "seq", None),
            P(None, "dp", "seq", None),
            P(("dp", "seq"), None),
            P(("dp", "seq"), None),
            P(("dp", "seq"), None),
            P(None, ("dp", "seq")),
            P(("dp", "seq")),
            P(("dp", "seq")),
        ),
        check_vma=False,
    )
```

```python
import enum
import functools
import types

import jax
import jax.numpy as jnp
from jax import lax
import numpy as np
from jax.experimental import pallas as pl
from jax.experimental.pallas import tpu as pltpu
from jax.sharding import PartitionSpec as P

HEADS = 12
HEAD_DIM = 64
WINDOW = 128


NORM_EPS = 1e-05
ROPE_BASE = 10000.0
MASK_FILL = -1e30
SQRT_HALF = 0.7071067811865476
INV_ROOT_TAU = 0.3989422804014327


LANES = 128


def pair_sum(value, outer):
    outer_size = lax.axis_size(outer)
    pairs = outer_size // 2
    core = lax.axis_index(outer) % 2
    blocks = value.reshape(pairs, 2, value.shape[0] // outer_size, value.shape[1])
    other = lax.dynamic_index_in_dim(blocks, 1 - core, axis=1, keepdims=False)
    own = lax.dynamic_index_in_dim(blocks, core, axis=1, keepdims=False)
    swap = [(i, i ^ 1) for i in range(outer_size)]
    return own + lax.ppermute(other, outer, swap)


def line_sum(value, outer):
    outer_size = lax.axis_size(outer)
    if outer_size == 4:
        line = lax.axis_index(outer) // 2
        other = lax.dynamic_index_in_dim(value, 1 - line, axis=0, keepdims=False)
        own = lax.dynamic_index_in_dim(value, line, axis=0, keepdims=False)
        swap = [(i, i ^ 2) for i in range(outer_size)]
        arrived = lax.ppermute(other.astype(jnp.bfloat16), outer, swap)
        value = own + arrived.astype(jnp.float32)
    else:
        groups = [list(range(c, outer_size, 2)) for c in range(2)]
        arrived = lax.all_to_all(
            value.astype(jnp.bfloat16), outer, 0, 0, axis_index_groups=groups
        )
        value = jnp.sum(arrived.astype(jnp.float32), axis=0)
    return value


def ring_sum(value, inner):
    inner_size = lax.axis_size(inner)
    blocks = value.reshape(inner_size, value.shape[0] // inner_size, value.shape[1])
    return jnp.sum(lax.all_to_all(blocks, inner, 0, 0), axis=0)


def norm_apply(values, gain):
    center = jnp.mean(values, axis=-1, keepdims=True)
    shifted = values - center
    inv_std = lax.rsqrt(jnp.mean(shifted * shifted, axis=-1, keepdims=True) + NORM_EPS)
    normed = shifted * inv_std
    return (normed * gain.astype(jnp.float32), normed, inv_std)


def norm_back(upstream, normed, inv_std, gain):
    scaled = upstream * gain.astype(jnp.float32)
    inner = (
        scaled
        - jnp.mean(scaled, axis=-1, keepdims=True)
        - normed * jnp.mean(scaled * normed, axis=-1, keepdims=True)
    )
    return (inv_std * inner, jnp.sum(upstream * normed, axis=(0, 1)))


def gelu_slope(values):
    cumul = 0.5 * (1.0 + jax.scipy.special.erf(values * SQRT_HALF))
    return cumul + values * jnp.exp(-0.5 * values * values) * INV_ROOT_TAU


def rope_tables(positions, head_dim):
    half_dim = head_dim // 2
    freqs = ROPE_BASE ** (-jnp.arange(half_dim).astype(jnp.float32) * 2.0 / head_dim)
    angles = positions.astype(jnp.float32)[:, None] * freqs[None, :]
    return (jnp.cos(angles)[:, None, :], jnp.sin(angles)[:, None, :])


def rotate(values, cosine, sine):
    half_dim = values.shape[-1] // 2
    first = values[..., :half_dim]
    second = values[..., half_dim:]
    return jnp.concatenate(
        [first * cosine - second * sine, second * cosine + first * sine], axis=-1
    )


def unrotate(values, cosine, sine):
    half_dim = values.shape[-1] // 2
    first = values[..., :half_dim]
    second = values[..., half_dim:]
    return jnp.concatenate(
        [first * cosine + second * sine, second * cosine - first * sine], axis=-1
    )


def plain_layer(
    layer_input, cotangent, w_joined, w_output, w_expand, w_contract, gain_one, gain_two
):
    micro, local_batch, group, width = layer_input.shape
    heads = HEADS
    head_dim = HEAD_DIM
    half = WINDOW // 2
    ffn = w_contract.shape[0]
    batch = micro * local_batch
    scale = head_dim ** (-0.5)
    axes = ("dp", "seq")
    seq_count = lax.axis_size("seq")
    up = [(i, i + 1) for i in range(seq_count - 1)]
    down = [(j, i) for i, j in up]
    group_start = lax.axis_index("seq") * group
    cosine, sine = rope_tables(group_start + jnp.arange(group, dtype=jnp.int32), head_dim)
    query_pos = group_start + jnp.arange(group, dtype=jnp.int32)[:, None]
    key_pos = group_start - half + jnp.arange(group + 2 * half, dtype=jnp.int32)[None, :]
    allowed = (
        (jnp.abs(query_pos - key_pos) <= half) & (key_pos >= 0) & (key_pos < group * seq_count)
    )
    gains = jnp.pad(jnp.stack([gain_one, gain_two], axis=1), ((0, 0), (0, LANES - 2)))
    pack_one = jnp.concatenate([w_joined, gains], axis=1)
    pack_two = jnp.concatenate([w_expand, w_contract.T, w_output], axis=1)
    full_one = lax.all_gather(pack_one, axes, axis=0, tiled=True)
    full_two = lax.all_gather(pack_two, axes, axis=0, tiled=True)
    full_joined = full_one[:, : 3 * width]
    full_gain_one = full_one[:, 3 * width]
    full_gain_two = full_one[:, 3 * width + 1]
    full_expand = full_two[:, : 2 * ffn]
    full_contract = full_two[:, 2 * ffn : 3 * ffn]
    full_output = full_two[:, 3 * ffn :]

    source32 = layer_input.reshape(batch, group, width).astype(jnp.float32)
    upstream_half = cotangent.reshape(batch, group, width)
    normed_f, norm_one, inv_one = norm_apply(source32, full_gain_one)
    normed_one = normed_f.astype(jnp.bfloat16)
    joined = jnp.einsum(
        "bcd,de->bce", normed_one, full_joined, preferred_element_type=jnp.float32
    )
    shape_heads = (batch, group, heads, head_dim)
    k_rot = rotate(joined[..., width : 2 * width].reshape(shape_heads), cosine, sine).astype(
        jnp.bfloat16
    )
    v_half = joined[..., 2 * width :].astype(jnp.bfloat16)
    key_value = jnp.stack([k_rot.reshape(batch, group, width), v_half])
    before = lax.ppermute(key_value[:, :, group - half :], "seq", up)
    after = lax.ppermute(key_value[:, :, :half], "seq", down)
    q_rot = rotate(joined[..., :width].reshape(shape_heads), cosine, sine).astype(jnp.bfloat16)
    extended = jnp.concatenate([before, key_value, after], axis=2)
    ext_shape = (batch, group + 2 * half, heads, head_dim)
    key_rows = extended[0].reshape(ext_shape)
    value_rows = extended[1].reshape(ext_shape)
    scores = (
        jnp.einsum("bqhd,bkhd->bhqk", q_rot, key_rows, preferred_element_type=jnp.float32)
        * scale
    )
    scores = jnp.where(allowed[None, None], scores, MASK_FILL)
    row_max = jnp.max(scores, axis=-1, keepdims=True)
    log_total = row_max + jnp.log(jnp.sum(jnp.exp(scores - row_max), axis=-1, keepdims=True))
    probs = jnp.exp(scores - log_total)
    probs_half = probs.astype(jnp.bfloat16)
    attended = jnp.einsum(
        "bhqk,bkhd->bqhd", probs_half, value_rows, preferred_element_type=jnp.float32
    )
    attended = attended.astype(jnp.bfloat16).reshape(batch, group, width)
    resid = source32 + jnp.einsum(
        "bcd,de->bce", attended, full_output, preferred_element_type=jnp.float32
    )
    normed_g, norm_two, inv_two = norm_apply(resid, full_gain_two)
    normed_two = normed_g.astype(jnp.bfloat16)
    expanded = jnp.einsum(
        "bcd,de->bce", normed_two, full_expand, preferred_element_type=jnp.float32
    )
    pre_act = expanded[..., :ffn]
    gate_part = expanded[..., ffn:]
    activated = jax.nn.gelu(pre_act, approximate=False)
    mixed = (activated * gate_part).astype(jnp.bfloat16)
    contract_acc = jnp.einsum(
        "bcd,bcf->df", upstream_half, mixed, preferred_element_type=jnp.float32
    )
    d_mixed = jnp.einsum(
        "bcd,df->bcf", upstream_half, full_contract, preferred_element_type=jnp.float32
    )
    d_expanded = jnp.concatenate(
        [d_mixed * gate_part * gelu_slope(pre_act), d_mixed * activated], axis=-1
    ).astype(jnp.bfloat16)
    expand_acc = jnp.einsum(
        "bcd,bce->de", normed_two, d_expanded, preferred_element_type=jnp.float32
    )
    ffn_grads, d_expanded = lax.optimization_barrier(
        (jnp.concatenate([expand_acc, contract_acc], axis=1), d_expanded)
    )
    ffn_pair = pair_sum(ffn_grads, "dp")
    d_normed_two = jnp.einsum(
        "bce,de->bcd", d_expanded, full_expand, preferred_element_type=jnp.float32
    )
    d_resid_n, gain_two_part = norm_back(d_normed_two, norm_two, inv_two, full_gain_two)
    d_resid = upstream_half.astype(jnp.float32) + d_resid_n
    d_resid_half = d_resid.astype(jnp.bfloat16)
    ffn_pair, d_resid_half = lax.optimization_barrier((ffn_pair, d_resid_half))
    ffn_line = line_sum(ffn_pair, "dp")
    d_attended = jnp.einsum(
        "bce,de->bcd", d_resid_half, full_output, preferred_element_type=jnp.float32
    )
    d_attended = d_attended.astype(jnp.bfloat16).reshape(shape_heads)
    d_probs = jnp.einsum(
        "bqhd,bkhd->bhqk", d_attended, value_rows, preferred_element_type=jnp.float32
    )
    centred = d_probs - jnp.sum(probs * d_probs, axis=-1, keepdims=True)
    d_scores = (probs * centred * scale).astype(jnp.bfloat16)
    d_key_ext = jnp.einsum(
        "bhqk,bqhd->bkhd", d_scores, q_rot, preferred_element_type=jnp.float32
    )
    d_value_ext = jnp.einsum(
        "bhqk,bqhd->bkhd", probs_half, d_attended, preferred_element_type=jnp.float32
    )
    ext_grads = jnp.stack(
        [
            d_key_ext.reshape(batch, group + 2 * half, width),
            d_value_ext.reshape(batch, group + 2 * half, width),
        ]
    )
    rims = ext_grads.astype(jnp.bfloat16)
    ffn_line, rims = lax.optimization_barrier((ffn_line, rims))
    ffn_sum = ring_sum(ffn_line, "seq")
    from_left = lax.ppermute(rims[:, :, group + half :], "seq", up).astype(jnp.float32)
    from_right = lax.ppermute(rims[:, :, :half], "seq", down).astype(jnp.float32)
    d_query = jnp.einsum(
        "bhqk,bkhd->bqhd", d_scores, key_rows, preferred_element_type=jnp.float32
    )
    output_acc = jnp.einsum(
        "bcd,bce->de", attended, d_resid_half, preferred_element_type=jnp.float32
    )
    final = resid + jnp.einsum(
        "bcf,df->bcd", mixed, full_contract, preferred_element_type=jnp.float32
    )
    own_grads = ext_grads[:, :, half : half + group]
    own_grads = own_grads + jnp.pad(
        from_left, ((0, 0), (0, 0), (0, group - half), (0, 0))
    ) + jnp.pad(from_right, ((0, 0), (0, 0), (group - half, 0), (0, 0)))
    d_key = unrotate(own_grads[0].reshape(shape_heads), cosine, sine).reshape(
        batch, group, width
    )
    d_query_flat = unrotate(d_query, cosine, sine).reshape(batch, group, width)
    d_joined = jnp.concatenate([d_query_flat, d_key, own_grads[1]], axis=-1).astype(
        jnp.bfloat16
    )
    d_normed_one = jnp.einsum(
        "bce,de->bcd", d_joined, full_joined, preferred_element_type=jnp.float32
    )
    d_source, gain_one_part = norm_back(d_normed_one, norm_one, inv_one, full_gain_one)
    input_grad = (d_resid + d_source).astype(jnp.bfloat16)
    joined_acc = jnp.einsum(
        "bcd,bce->de", normed_one, d_joined, preferred_element_type=jnp.float32
    )
    gain_parts = jnp.pad(
        jnp.stack([gain_one_part, gain_two_part], axis=1), ((0, 0), (0, LANES - 2))
    )
    last_grads = jnp.concatenate([joined_acc, output_acc, gain_parts], axis=1)
    last_sum = ring_sum(line_sum(pair_sum(last_grads, "dp"), "dp"), "seq")
    return (
        final.astype(jnp.bfloat16).reshape(layer_input.shape),
        input_grad.reshape(layer_input.shape),
        last_sum[:, : 3 * width],
        last_sum[:, 3 * width : 4 * width],
        ffn_sum[:, : 2 * ffn],
        ffn_sum[:, 2 * ffn :].T,
        last_sum[:, 4 * width],
        last_sum[:, 4 * width + 1],
    )


MESH = pl.DeviceIdType.MESH
ROWS = 24
MIB = 2**20
F32 = jnp.float32
HALF = jnp.bfloat16
PAIR = 128


def place(steep=False):
    dp, seq = lax.axis_index("dp"), lax.axis_index("seq")
    y, core = dp // 2, dp % 2
    z, x = seq // 2, seq % 2
    zh, zl = z // 2, z % 2
    turn = 1 if steep else core
    peers = dict(
        pair=(dp + 1 - 2 * core, seq),
        r=(dp + 2 * turn * (1 - 2 * y), seq + (1 - turn) * (1 - 2 * x)),
        p=(dp + 2 * (1 - turn) * (1 - 2 * y), seq + turn * (1 - 2 * x)),
        zl=(dp, seq + 2 - 4 * zl),
        zh=(dp, seq + 4 - 8 * zh),
        left=(dp, (seq + 7) % 8),
        right=(dp, (seq + 1) % 8),
    )
    r = x * (1 - turn) + y * turn
    p = y * (1 - turn) + x * turn
    return types.SimpleNamespace(dp=dp, seq=seq, core=core, turn=turn, zh=zh, zl=zl, r=r, p=p, peers=peers)


def meet(at):
    barrier = pltpu.get_barrier_semaphore()
    for peer in at.peers.values():
        pl.semaphore_signal(barrier, inc=1, device_id=peer, device_id_type=MESH)
    pl.semaphore_wait(barrier, len(at.peers))


def remote(src, dst, sems, where, peer):
    send, recv = sems
    return pltpu.make_async_remote_copy(
        src_ref=src,
        dst_ref=dst,
        send_sem=send.at[where],
        recv_sem=recv.at[where],
        device_id=peer,
        device_id_type=MESH,
    )


def push(*args):
    copy = remote(*args)
    copy.start()
    return copy


def gather_spot(at, path, stage=0):
    return (at.core,) + tuple(getattr(at, name) for name in reversed(path[stage:]))


def gather_send(at, path, buf, sems, group, stage):
    part = buf.at[gather_spot(at, path, stage)]
    name = path[stage] if stage < 4 else "pair"
    return push(part, part, sems, (group, stage), at.peers[name])


def plane_index(path, steep, core, y, z, x):
    r, p = (y, x) if steep or core else (x, y)
    place = dict(r=r, p=p, zh=z // 2, zl=z % 2)
    return (core,) + tuple(place[name] for name in reversed(path))


def relay(path, steep, buf, store):
    for core in range(2):
        for y in range(2):
            for z in range(4):
                blocks = [buf[plane_index(path, steep, core, y, z, x)].astype(F32) for x in range(2)]
                store(y * 384 + core * 192 + z * 48, jnp.concatenate(blocks, axis=0).astype(HALF))


def relay_gains(path, steep, buf, gains):
    width = gains.shape[1]
    total = jnp.zeros((8, width), F32)
    row, lane = (lax.broadcasted_iota(jnp.int32, (8, 128), k) for k in range(2))
    valid = (row < 2) & (lane < ROWS)
    for core in range(2):
        for y in range(2):
            for z in range(4):
                for x in range(2):
                    block = jnp.where(valid, buf[plane_index(path, steep, core, y, z, x)], 0.0)
                    wide = jnp.concatenate([block, jnp.zeros((8, width - 128), F32)], axis=1)
                    shift = ROWS * (y * 16 + core * 8 + z * 2 + x)
                    total = total + (pltpu.roll(wide, shift, 1) if shift else wide)
    gains[...] = total


def block_row(at, p, z, r):
    y = p * (1 - at.turn) + r * at.turn
    x = r * (1 - at.turn) + p * at.turn
    return y, pl.multiple_of(z * 48 + x * ROWS, 8)


def sum_stage(at, stage, grads, bufs, sems, index, width, emit):
    r0, r1, r2, r3, r4, s1, s2, s3, s4 = bufs
    core, r, p, zh, zl = at.core, at.r, at.p, at.zh, at.zl
    peers = at.peers
    w = slice(0, width)

    def kept(pp, z):
        y, row = block_row(at, pp, z, r)
        return y, pl.ds(row, ROWS)

    if stage == 0:
        copies = []
        for y in range(2):
            rows = pl.ds(pl.multiple_of(y * 384 + (1 - core) * 192, 192), 192)
            copies.append(push(grads.at[rows, w], r0.at[y], sems, (index, y), peers["pair"]))
        return copies
    if stage == 1:

        @pl.loop(0, 8)
        def _(i):
            pp, z = i // 4, i % 4
            y, row = block_row(at, pp, z, 1 - r)
            base = pl.multiple_of(y * 384 + core * 192 + row, 8)
            s1[pp, z // 2, z % 2, :, w] = (grads[pl.ds(base, ROWS), w] + r0[y, pl.ds(row, ROWS)]).astype(HALF)
            y, rows = kept(pp, z)
            base = pl.multiple_of(y * 384 + core * 192 + rows.start, 8)
            r0[y, rows] = grads[pl.ds(base, ROWS), w] + r0[y, rows]

        return [push(s1.at[:, :, :, :, w], r1, sems, (index, 2), peers["r"])]
    if stage == 2:

        @pl.loop(0, 4)
        def _(z):
            zh, zl = z // 2, z % 2
            s2[zh, zl, :, w] = (r0[kept(1 - p, z)] + r1[1 - p, zh, zl].astype(F32)).astype(HALF)
            r0[kept(p, z)] = r0[kept(p, z)] + r1[p, zh, zl].astype(F32)

        return [push(s2.at[:, :, :, w], r2, sems, (index, 3), peers["p"])]
    if stage == 3:
        for h in range(2):
            far, near = 2 * h + 1 - zl, 2 * h + zl
            s3[h, :, w] = r0[kept(p, far)] + r2[h, 1 - zl].astype(F32)
            r0[kept(p, near)] = r0[kept(p, near)] + r2[h, zl].astype(F32)
        return [push(s3.at[:, :, w], r3, sems, (index, 4), peers["zl"])]
    if stage == 4:
        s4[:, w] = r0[kept(p, 2 * (1 - zh) + zl)] + r3[1 - zh]
        return [push(s4.at[:, w], r4, sems, (index, 5), peers["zh"])]
    emit((r0[kept(p, 2 * zh + zl)] + r3[zh]) + r4[...])
    return []


GAIN_PATH = ("pair", "r", "p", "zl", "zh")


def dot(a, b, dims):
    return lax.dot_general(a, b, (dims, ((), ())), preferred_element_type=F32)


NN, NT, TN = ((1,), (0,)), ((1,), (1,)), ((0,), (0,))


def swap_halves(v):
    lane = lax.broadcasted_iota(jnp.int32, v.shape, 1) % HEAD_DIM
    return jnp.where(
        lane < HEAD_DIM // 2,
        pltpu.roll(v, PAIR - HEAD_DIM // 2, 1),
        pltpu.roll(v, HEAD_DIM // 2, 1),
    )


class Kind(enum.IntEnum):
    g = 0
    s = 1
    pre = 2
    n1 = 3
    n1h = 4
    halo = 5
    halow = 6
    proj = 7
    att = 8
    oproj = 9
    norm2 = 10
    fwd = 11
    grad = 12
    back = 13
    norm2b = 14
    datt = 15
    attb = 16
    backq = 17
    backkv = 18
    backh = 19
    rim = 20
    rimw = 21
    n = 22
    norm1b = 23
    final = 24
    projh = 25


PATHS = (("zh", "zl", "p", "r"), ("p", "r", "zh", "zl"))
GATHER = ((0, 0), (0, 0), (0, 0), (0, 0), (0, 1), (0, 0), (0, 0), (0, 0))
SUM_STEEP = (0, 0, 0, 0, 0, 0, 0)
ORDER = (
    0, 6, 86, 83, 1, 12, 7, 18, 2, 13, 24, 8, 87, 3, 19, 30, 25, 36, 14, 9, 4, 20, 26, 5,
    31, 42, 84, 85, 15, 37, 10, 21, 11, 88, 32, 27, 16, 43, 38, 17, 90, 22, 133, 33, 23, 89,
    91, 28, 39, 92, 93, 44, 29, 94, 95, 34, 96, 97, 98, 35, 99, 40, 102, 45, 109, 41, 100,
    103, 48, 110, 46, 53, 47, 101, 49, 104, 111, 112, 105, 113, 114, 54, 58, 115, 50, 63,
    106, 116, 55, 117, 107, 118, 119, 51, 59, 68, 108, 122, 64, 73, 120, 56, 121, 60, 125,
    132, 52, 126, 69, 78, 65, 127, 57, 74, 123, 128, 61, 70, 129, 66, 79, 130, 75, 62, 71,
    124, 131, 67, 80, 76, 72, 81, 77, 82,
)


def layer_kernel(names, *refs):
    ns = types.SimpleNamespace(**dict(zip(names, refs)))
    at = place()
    seq = at.seq
    x, cot, gains = ns.x, ns.cot, ns.gains
    tokens, width = x.shape
    third = ns.de.shape[2] // 3
    ff = 3 * third
    length = tokens // 2
    half = WINDOW // 2
    scale = HEAD_DIM ** (-0.5)
    cos, sin, low, high = ns.cos, ns.sin, ns.low, ns.high
    n1, n2, q, kx, vx = ns.n1, ns.n2, ns.q, ns.kx, ns.vx
    blocks = tokens // 32
    span = length + 2 * half
    pairs = width // PAIR

    def rows_of(i, n=32):
        return pl.ds(pl.multiple_of(i * n, n), n)

    wj, wo, we, wc = ns.wj, ns.wo, ns.we, ns.wc
    views = (at, place(True))
    group_at = [views[steep] for steep, _ in GATHER]
    paths = [PATHS[way] for _, way in GATHER]
    spots = [gather_spot(*pair) for pair in zip(group_at, paths)]
    bn = ns.bn
    for k, ref in enumerate((ns.g1, ns.g2)):
        bn[spots[0] + (slice(k, k + 1), slice(0, ROWS))] = ref[...].astype(F32)
    ns.bk[spots[1]] = wj[:, width : 2 * width]
    ns.bv[spots[2]] = wj[:, 2 * width :]
    ns.bq[spots[3]] = wj[:, :width]
    ns.bo[spots[4]] = wo[...]
    for j in range(3):
        buf, spot = getattr(ns, "bf%d" % j), spots[5 + j]
        buf[spot + (slice(None), slice(0, third))] = we[:, j * third : (j + 1) * third]
        buf[spot + (slice(None), slice(third, 2 * third))] = we[
            :, ff + j * third : ff + (j + 1) * third
        ]
        buf[spot + (slice(None), slice(2 * third, ff))] = wc[:, j * third : (j + 1) * third]

    xh, rim_in = ns.xh, ns.rim_in

    @pl.when(seq == 0)
    def _():
        xh[0] = jnp.zeros(xh.shape[1:], HALF)
        rim_in[0] = jnp.zeros(rim_in.shape[1:], HALF)

    @pl.when(seq == 7)
    def _():
        xh[1] = jnp.zeros(xh.shape[1:], HALF)
        rim_in[1] = jnp.zeros(rim_in.shape[1:], HALF)

    meet(at)

    wj_all, wo_all, wf_all = ns.wj_all, ns.wo_all, ns.wf_all

    def into(ref, offset):
        def store(row, value):
            ref[row : row + 48, offset : offset + value.shape[1]] = value

        return store

    groups = [
        (bn, None),
        (ns.bk, into(wj_all, width)),
        (ns.bv, into(wj_all, 2 * width)),
        (ns.bq, into(wj_all, 0)),
        (ns.bo, into(wo_all, 0)),
    ] + [(buf, into(wf_all.at[j], 0)) for j, buf in enumerate((ns.bf0, ns.bf1, ns.bf2))]
    copies = {}
    tasks = {}

    def task(*name):
        def note(f):
            tasks[name] = f

        return note

    def gather_task(i, stage):
        def run():
            buf, store = groups[i]
            if stage:
                copies.pop(i).wait()
            if stage < 5:
                sems = (ns.g_send, ns.g_recv)
                copies[i] = gather_send(group_at[i], paths[i], buf, sems, i, stage)
            elif store is None:
                relay_gains(paths[i], GATHER[i][0], buf, gains)
            else:
                relay(paths[i], GATHER[i][0], buf, store)

        return run

    for i in range(len(groups)):
        for stage in range(6):
            tasks[Kind.g, i, stage] = gather_task(i, stage)

    def centre(values):
        mean = jnp.mean(values, axis=-1, keepdims=True)
        shifted = values - mean
        inv = lax.rsqrt(jnp.mean(shifted * shifted, axis=-1, keepdims=True) + NORM_EPS)
        return shifted * inv, inv

    @task(Kind.pre)
    def _():
        lane = lax.broadcasted_iota(jnp.int32, (length, PAIR), 1)
        row = lax.broadcasted_iota(jnp.int32, (length, PAIR), 0)
        sign = jnp.where(lane % HEAD_DIM < HEAD_DIM // 2, -1.0, 1.0)
        beside = jnp.where(row < half, row - half, row + half)
        for k, offset in enumerate((row, beside)):
            angle = (offset + seq * length).astype(F32) * ns.freq[...]
            cos[k] = jnp.cos(angle)
            sin[k] = jnp.sin(angle) * sign
        low[...] = jnp.where(lane < HEAD_DIM, 1.0, 0.0).astype(HALF)
        high[...] = jnp.where(lane < HEAD_DIM, 0.0, 1.0).astype(HALF)
        key = lax.broadcasted_iota(jnp.int32, (span, 2 * length), 0)
        key = jnp.where(key < length, key, jnp.where(key < length + half, key - span + half, key - half))
        query = lax.broadcasted_iota(jnp.int32, (span, 2 * length), 1) % length
        key_pos = key + seq * length
        allowed = (jnp.abs(key - query) <= half) & (key_pos >= 0) & (key_pos < 8 * length)
        ns.bias[...] = jnp.where(allowed, 0.0, MASK_FILL)

        @pl.loop(0, blocks)
        def _(i):
            rows = rows_of(i)
            norm, inv = centre(x[rows].astype(F32))
            ns.norm1[rows] = norm
            ns.inv1[rows] = inv

        for c in range(0, width, 256):
            ns.cot_t[c : c + 256] = jnp.transpose(cot[:, c : c + 256].astype(F32)).astype(HALF)

    @task(Kind.n1)
    def _():
        for c in range(0, width, 256):
            value = ns.norm1[:, c : c + 256] * gains[0:1, c : c + 256]
            n1[:tokens, c : c + 256] = value.astype(HALF)
            ns.n1_t[c : c + 256, :tokens] = jnp.transpose(value).astype(HALF)

    @task(Kind.n1h)
    def _():
        for b in range(2):
            for side in range(2):
                rows = slice(tokens + b * length + side * half, tokens + b * length + (side + 1) * half)
                n1[rows] = (centre(xh[side, b].astype(F32))[0] * gains[0:1]).astype(HALF)
        for c in range(0, width, 256):
            value = n1[tokens:, c : c + 256].astype(F32)
            ns.n1_t[c : c + 256, tokens:] = jnp.transpose(value).astype(HALF)

    halo_sems = (ns.h_send, ns.h_recv)

    def halo(i, from_left, to_left, from_right, to_right):
        def left():
            return remote(to_left, from_right, halo_sems, (i, 0), at.peers["left"])

        def right():
            return remote(to_right, from_left, halo_sems, (i, 1), at.peers["right"])

        return left, right

    x_rows = x.reshape(2, length, width)
    x_halo = halo(0, xh.at[0], x_rows.at[:, :half], xh.at[1], x_rows.at[:, half:])

    def exchange_start(sides):
        pl.when(seq > 0)(lambda: sides[0]().start())
        pl.when(seq < 7)(lambda: sides[1]().start())

    def exchange_wait(sides):
        left, right = sides

        @pl.when(seq > 0)
        def _():
            left().wait_send()
            right().wait_recv()

        @pl.when(seq < 7)
        def _():
            right().wait_send()
            left().wait_recv()

    def project(offset, first, store):
        @pl.loop(0, width // 256)
        def _(i):
            base = pl.multiple_of(i * 256, 256)
            value = dot(n1[first : first + tokens], wj_all[:, pl.ds(offset + base, 256)], NN)
            for b in range(2):
                for c in range(2):
                    store(
                        b + first // length,
                        pl.ds(base + c * PAIR, PAIR),
                        value[b * length : (b + 1) * length, c * PAIR : (c + 1) * PAIR],
                    )

    def turn(v, k=0):
        return v * cos[k] + swap_halves(v) * sin[k]

    def unturn(v, k=0):
        return v * cos[k] - swap_halves(v) * sin[k]

    def store_k(b, cols, v):
        k = b // 2
        kx[b % 2, k * length : (k + 1) * length, cols] = turn(v, k).astype(HALF)

    def store_v(b, cols, v):
        k = b // 2
        vx[b % 2, k * length : (k + 1) * length, cols] = v.astype(HALF)

    def store_q(b, cols, v):
        q[b * length : (b + 1) * length, cols] = turn(v).astype(HALF)

    @task(Kind.halo)
    def _():
        exchange_start(x_halo)

    @task(Kind.halow)
    def _():
        exchange_wait(x_halo)

    @task(Kind.proj, 0)
    def _():
        project(width, 0, store_k)

    @task(Kind.proj, 2)
    def _():
        project(2 * width, 0, store_v)

    @task(Kind.proj, 1)
    def _():
        project(0, 0, store_q)

    @task(Kind.projh)
    def _():
        project(width, tokens, store_k)
        project(2 * width, tokens, store_v)

    def stack_heads(v):
        return jnp.concatenate([v * low[...], v * high[...]], axis=0)

    lower = lax.broadcasted_iota(jnp.int32, (length, PAIR), 1) < HEAD_DIM

    def pick_heads(v):
        return jnp.where(lower, v[:length], v[length:])

    def attend(b, i):
        cols = pl.ds(pl.multiple_of(i * PAIR, PAIR), PAIR)
        rows = slice(b * length, (b + 1) * length)
        qs = stack_heads(q[rows, cols])
        scores = dot(kx[b, :, cols], qs, NT) * scale + ns.bias[...]
        top = jnp.max(scores, axis=0, keepdims=True)
        raised = jnp.exp(scores - top)
        total = jnp.sum(raised, axis=0, keepdims=True)
        probs = raised * (1.0 / total)
        ns.stat[b * pairs + i] = top + jnp.log(total)
        ns.att[rows, cols] = pick_heads(dot(probs.astype(HALF), vx[b, :, cols], TN)).astype(HALF)

    def some_pairs(f, j):
        few = pairs // 3
        return lambda: pl.loop(j % 3 * few, (j % 3 + 1) * few)(functools.partial(f, j // 3))

    for j in range(6):
        tasks[Kind.att, j] = some_pairs(attend, j)

    resid = ns.resid

    @task(Kind.oproj)
    def _():
        @pl.loop(0, width // 256)
        def _(i):
            cols = pl.ds(pl.multiple_of(i * 256, 256), 256)
            resid[:, cols] = x[:, cols].astype(F32) + dot(ns.att[...], wo_all[:, cols], NN)

    @task(Kind.norm2)
    def _():
        @pl.loop(0, blocks)
        def _(i):
            rows = rows_of(i)
            norm, inv = centre(resid[rows])
            ns.norm2[rows] = norm
            ns.inv2[rows] = inv
            n2[rows] = (norm * gains[1:2]).astype(HALF)

        for c in range(0, width, 256):
            ns.n2_t[c : c + 256] = jnp.transpose(n2[:, c : c + 256].astype(F32)).astype(HALF)

    per = width // 3

    def run_sum(index, stage):
        size = ff if index < 3 else width

        def emit(value):
            if index < 3:
                j = index * third
                ns.o_e[:, j : j + third] = value[:, :third]
                ns.o_e[:, ff + j : ff + j + third] = value[:, third : 2 * third]
                ns.o_c[:, j : j + third] = value[:, 2 * third :]
            elif index == 3:
                ns.o_o[...] = value
            else:
                for k in range(3):
                    j = k * width + (index - 4) * per
                    ns.o_j[:, j : j + per] = value[:, k * per : (k + 1) * per]

        bufs = [getattr(ns, "r%d_%d" % (k, index)) for k in range(5)]
        bufs += [ns.bf0.at[0, index % 2], ns.bf1.at[0, index % 2, 0]]
        bufs += [getattr(ns, "s%d" % k).at[index % 2] for k in range(3, 5)]
        return sum_stage(
            views[SUM_STEEP[index]],
            stage,
            ns.grads.at[index % 2],
            bufs,
            (ns.s_send, ns.s_recv),
            index,
            size,
            emit,
        )

    def sum_task(i, stage):
        def run():
            for copy in copies.pop((Kind.s, i), ()):
                copy.wait()
            copies[Kind.s, i] = run_sum(i, stage)

        return run

    for i in range(7):
        for stage in range(1, 6):
            tasks[Kind.s, i, stage] = sum_task(i, stage)

    def weight_grad(index, offset, left, right, columns):
        step = min(columns, 384)

        @pl.loop(0, columns // step)
        def _(i):
            base = pl.multiple_of(i * step, step)
            ns.grads[index % 2, :, pl.ds(offset + base, step)] = dot(
                left[...], right[:, pl.ds(base, step)], NN
            )

    e, de, dn = ns.e, ns.de, ns.dn

    def forward_third(j):
        w = wf_all.at[j]
        for c in range(0, 2 * third, third):
            e[:, c : c + third] = dot(n2[...], w[:, c : c + third], NN)
        e[:, 2 * third :] = dot(cot[...], w[:, 2 * third :], NN)

        @pl.loop(0, blocks)
        def _(i):
            rows = rows_of(i)
            pre, gate, d_mixed = (e[rows, c * third : (c + 1) * third] for c in range(3))
            cumul = 0.5 * (1.0 + lax.erf(pre * SQRT_HALF))
            active = pre * cumul
            slope = cumul + pre * jnp.exp(-0.5 * pre * pre) * INV_ROOT_TAU
            de[j, rows, :third] = (d_mixed * gate * slope).astype(HALF)
            de[j, rows, third : 2 * third] = (d_mixed * active).astype(HALF)
            de[j, rows, 2 * third :] = (active * gate).astype(HALF)

    def grad_third(j):
        weight_grad(j, 0, ns.n2_t, de.at[j], 2 * third)
        weight_grad(j, 2 * third, ns.cot_t, de.at[j, :, 2 * third :], third)
        sum_task(j, 0)()

    def back_third(j):
        back = dot(de[j, :, : 2 * third], wf_all[j, :, : 2 * third], NT)
        dn[...] = back if j == 0 else dn[...] + back

    for j in range(3):
        tasks[Kind.fwd, j] = functools.partial(forward_third, j)
        tasks[Kind.grad, j] = functools.partial(grad_third, j)
        tasks[Kind.back, j] = functools.partial(back_third, j)

    def norm_down(upstream, norm, inv, gain):
        scaled = upstream * gain
        mean = jnp.mean(scaled, axis=-1, keepdims=True)
        along = jnp.mean(scaled * norm, axis=-1, keepdims=True)
        return inv * (scaled - mean - norm * along)

    part = ns.part
    def fold(v):
        return sum(v[k : k + 8] for k in range(0, 32, 8))

    @task(Kind.norm2b)
    def _():
        part[...] = jnp.zeros(part.shape, F32)

        @pl.loop(0, blocks)
        def _(i):
            rows = rows_of(i)
            up, norm = dn[rows], ns.norm2[rows]
            part[1] += fold(up * norm)
            d_resid = cot[rows].astype(F32) + norm_down(up, norm, ns.inv2[rows], gains[1:2])
            dn[rows] = d_resid
            n1[rows] = d_resid.astype(HALF)

    @task(Kind.datt)
    def _():
        @pl.loop(0, width // 256)
        def _(i):
            rows = pl.ds(pl.multiple_of(i * 256, 256), 256)
            n2[:, rows] = dot(n1[:tokens], wo_all[rows, :], NT).astype(HALF)

    @task(Kind.grad, 3)
    def _():
        @pl.loop(0, width // 256)
        def _(i):
            cols = pl.ds(pl.multiple_of(i * 256, 256), 256)
            ns.grads[1, cols, :width] = dot(ns.att[:, cols], n1[:tokens], TN)

        sum_task(3, 0)()

    n1_own, n1_all = ns.n1_t.at[:, :tokens], ns.n1_t

    def grad_joined(h):
        cols = slice(h * per, (h + 1) * per)
        v_cols = slice(width + h * per, width + (h + 1) * per)
        weight_grad(4 + h, 0, n1_own, dq.at[:, cols], per)
        weight_grad(4 + h, per, n1_all, dkv.at[:, cols], per)
        weight_grad(4 + h, 2 * per, n1_all, dkv.at[:, v_cols], per)
        sum_task(4 + h, 0)()

    rim_out = ns.rim_out
    dq, dkv = ns.dq, ns.dkv

    def attend_back(b, i):
        cols = pl.ds(pl.multiple_of(i * PAIR, PAIR), PAIR)
        rows = slice(b * length, (b + 1) * length)
        qs = stack_heads(q[rows, cols])
        ups = stack_heads(n2[rows, cols])
        scores = dot(kx[b, :, cols], qs, NT) * scale + ns.bias[...]
        probs = jnp.exp(scores - ns.stat[b * pairs + i])
        d_probs = dot(vx[b, :, cols], ups, NT)
        centred = d_probs - jnp.sum(probs * d_probs, axis=0, keepdims=True)
        d_scores = (probs * centred * scale).astype(HALF)
        d_q = pick_heads(dot(d_scores, kx[b, :, cols], TN))
        dq[rows, cols] = unturn(d_q).astype(HALF)
        d_k = dot(d_scores, qs, NN)
        d_v = dot(probs.astype(HALF), ups, NN)
        v_cols = pl.ds(pl.multiple_of(width + i * PAIR, PAIR), PAIR)
        for k in range(2):
            part_rows = slice(k * tokens + b * length, k * tokens + (b + 1) * length)
            piece = slice(k * length, (k + 1) * length)
            dkv[part_rows, cols] = unturn(d_k[piece], k).astype(HALF)
            dkv[part_rows, v_cols] = d_v[piece].astype(HALF)

    for j in range(6):
        tasks[Kind.attb, j] = some_pairs(attend_back, j % 2 * 3 + j // 2)

    for h in range(3):
        tasks[Kind.grad, 4 + h] = functools.partial(grad_joined, h)

    @task(Kind.backq)
    def _():
        e[:, :width] = dot(dq[...], wj_all[:, :width], NT)

    @task(Kind.backkv)
    def _():
        e[:, :width] = e[:, :width] + dot(dkv[:tokens], wj_all[:, width:], NT)

    rims = halo(1, rim_in.at[0], rim_out.at[0], rim_in.at[1], rim_out.at[1])

    @task(Kind.backh)
    def _():
        total = jnp.zeros((1, width), F32)
        for b in range(2):
            first = tokens + b * length
            back = dot(dkv[first : first + length], wj_all[:, width:], NT)
            for side in range(2):
                piece = back[side * half : (side + 1) * half]
                rim_out[side, b] = piece.astype(HALF)
                norm = centre(xh[side, b].astype(F32))[0]
                total = total + jnp.sum(piece * norm, axis=0, keepdims=True)
        part[0, 0:1] = part[0, 0:1] + total

    @task(Kind.rim)
    def _():
        exchange_start(rims)

    @task(Kind.rimw)
    def _():
        exchange_wait(rims)

    gain_sum, gain_in = ns.gain_sum, ns.gain_in
    gain_sems = (ns.n_send, ns.n_recv)

    def gain_push(t):
        peer = at.peers[GAIN_PATH[t]]
        copies[Kind.n] = push(gain_sum.at[t], gain_in.at[t], gain_sems, (t,), peer)

    @task(Kind.n, 0)
    def _():
        @pl.loop(0, blocks)
        def _(i):
            rows = rows_of(i)
            part[0] += fold(e[rows, :width] * ns.norm1[rows])

        gain_sum[0] = jnp.zeros(gain_sum.shape[1:], F32)
        for k in range(2):
            gain_sum[0, k : k + 1] = jnp.sum(part[k], axis=0, keepdims=True)
        gain_push(0)

    @task(Kind.norm1b)
    def _():
        for b in range(2):
            for side in range(2):
                first = b * length + side * half
                for k in range(0, half, 32):
                    rows = slice(first + k, first + k + 32)
                    up = e[rows, :width] + rim_in[side, b, k : k + 32].astype(F32)
                    d_source = norm_down(up, ns.norm1[rows], ns.inv1[rows], gains[0:1])
                    ns.grad[rows] = (dn[rows] + d_source).astype(HALF)

    def gain_task(t):
        def run():
            copies.pop(Kind.n).wait()
            gain_sum[t] = gain_sum[t - 1] + gain_in[t - 1]
            if t < 5:
                gain_push(t)
                return
            shift = ((32 - (at.dp * 8 + seq)) * ROWS) % width
            own = pltpu.roll(gain_sum[5], shift, 1)
            ns.o_g1[...] = own[0:1, :ROWS]
            ns.o_g2[...] = own[1:2, :ROWS]

        return run

    for t in range(1, 6):
        tasks[Kind.n, t] = gain_task(t)

    @task(Kind.final)
    def _():
        @pl.loop(0, width // 256)
        def _(i):
            cols = pl.ds(pl.multiple_of(i * 256, 256), 256)
            value = resid[:, cols]
            for j in range(3):
                value = value + dot(de[j, :, 2 * third :], wf_all[j, cols, 2 * third :], NT)
            ns.out[:, cols] = value.astype(HALF)

    steps = [run for _, run in sorted(tasks.items(), key=lambda item: item[0])]
    assert sorted(ORDER) == list(range(len(steps)))
    for number in ORDER:
        steps[number]()


def fused_layer(x, cot, wj, wo, we, wc, g1, g2, freq):
    tokens, width = x.shape
    ff = wc.shape[1]
    length = tokens // 2
    half = WINDOW // 2
    span = length + 2 * half
    pairs = width // PAIR
    lead = (2, 2, 2, 2, 2, ROWS)
    ins = dict(x=x, cot=cot, wj=wj, wo=wo, we=we, wc=wc, g1=g1, g2=g2, freq=freq)
    outs = dict(
        out=((tokens, width), HALF),
        grad=((tokens, width), HALF),
        o_e=((ROWS, 2 * ff), F32),
        o_c=((ROWS, ff), F32),
        o_o=((ROWS, width), F32),
        o_j=((ROWS, 3 * width), F32),
        o_g1=((1, ROWS), F32),
        o_g2=((1, ROWS), F32),
    )
    held = dict(bn=((2, 2, 2, 2, 2, 8, 128), F32))
    for name in ("bk", "bv", "bq", "bo"):
        held[name] = (lead + (width,), HALF)
    for j in range(3):
        held["bf%d" % j] = (lead + (ff,), HALF)
    held.update(
        wj_all=((width, 3 * width), HALF),
        wo_all=((width, width), HALF),
        wf_all=((3, width, ff), HALF),
        gains=((8, width), F32),
        cos=((2, length, PAIR), F32),
        sin=((2, length, PAIR), F32),
        xh=((2, 2, half, width), HALF),
        low=((length, PAIR), HALF),
        high=((length, PAIR), HALF),
        bias=((span, 2 * length), F32),
        norm1=((tokens, width), F32),
        inv1=((tokens, 1), F32),
        n1=((2 * tokens, width), HALF),
        n1_t=((width, 2 * tokens), HALF),
        cot_t=((width, tokens), HALF),
        q=((tokens, width), HALF),
        kx=((2, span, width), HALF),
        vx=((2, span, width), HALF),
        stat=((2 * pairs, 1, 2 * length), F32),
        att=((tokens, width), HALF),
        resid=((tokens, width), F32),
        norm2=((tokens, width), F32),
        inv2=((tokens, 1), F32),
        n2=((tokens, width), HALF),
        n2_t=((width, tokens), HALF),
        e=((tokens, ff), F32),
        de=((3, tokens, ff), HALF),
        dn=((tokens, width), F32),
        part=((2, 8, width), F32),
        dq=((tokens, width), HALF),
        dkv=((2 * tokens, 2 * width), HALF),
        rim_out=((2, 2, half, width), HALF),
        rim_in=((2, 2, half, width), HALF),
        gain_sum=((6, 8, width), F32),
        gain_in=((5, 8, width), F32),
        grads=((2, width, ff), F32),
        s3=((2, 2, ROWS, ff), F32),
        s4=((2, ROWS, ff), F32),
    )
    for i in range(7):
        size = ff if i < 3 else width
        held["r0_%d" % i] = ((2, 8 * ROWS, size), F32)
        held["r1_%d" % i] = ((2, 2, 2, ROWS, size), HALF)
        held["r2_%d" % i] = ((2, 2, ROWS, size), HALF)
        held["r3_%d" % i] = ((2, ROWS, size), F32)
        held["r4_%d" % i] = ((ROWS, size), F32)
    sems = {}
    for side in ("send", "recv"):
        sems["g_" + side] = (8, 5)
        sems["h_" + side] = (2, 2)
        sems["s_" + side] = (7, 6)
        sems["n_" + side] = (5,)
    vmem = pl.BlockSpec(memory_space=pltpu.VMEM)
    names = tuple(ins) + tuple(outs) + tuple(held) + tuple(sems)
    return pl.pallas_call(
        functools.partial(layer_kernel, names),
        out_shape=tuple(jax.ShapeDtypeStruct(*v) for v in outs.values()),
        in_specs=[vmem] * len(ins),
        out_specs=(vmem,) * len(outs),
        scratch_shapes=[pltpu.VMEM(*v) for v in held.values()]
        + [pltpu.SemaphoreType.DMA(v) for v in sems.values()],
        compiler_params=pltpu.CompilerParams(
            collective_id=0, has_side_effects=True, vmem_limit_bytes=VMEM_LIMIT
        ),
    )(*ins.values())


VMEM_LIMIT = 63 * MIB


def hand_on(arrays):
    vmem = pl.BlockSpec(memory_space=pltpu.VMEM)
    count = len(arrays)

    def kernel(*refs):
        for source, target in zip(refs[:count], refs[count:]):
            target[...] = source[...]

    return pl.pallas_call(
        kernel,
        out_shape=tuple(jax.ShapeDtypeStruct(a.shape, a.dtype) for a in arrays),
        in_specs=[vmem] * count,
        out_specs=(vmem,) * count,
    )(*arrays)


def fast_layer(
    layer_input, cotangent, w_joined, w_output, w_expand, w_contract, gain_one, gain_two
):
    width = layer_input.shape[-1]
    tokens = layer_input.shape[0] * layer_input.shape[1] * layer_input.shape[2]
    half_dim = HEAD_DIM // 2
    freqs = np.float32(ROPE_BASE) ** (-np.arange(half_dim, dtype=np.float32) * 2.0 / HEAD_DIM)
    freq = np.tile(freqs.astype(np.float32), PAIR // half_dim)[None, :]
    outs = fused_layer(
        layer_input.reshape(tokens, width),
        cotangent.reshape(tokens, width),
        w_joined,
        w_output,
        w_expand,
        w_contract.T,
        gain_one[None, :],
        gain_two[None, :],
        freq,
    )
    out, grad, o_e, o_c, o_o, o_j, o_g1, o_g2 = hand_on(outs)
    return (
        out.reshape(layer_input.shape),
        grad.reshape(layer_input.shape),
        o_j,
        o_o,
        o_e,
        o_c.T,
        o_g1[0],
        o_g2[0],
    )


def solution(mesh):
    fits = mesh.shape["dp"] == 4 and mesh.shape["seq"] == 8
    body = fast_layer if fits else plain_layer
    placed = (
        P(None, "dp", "seq", None),
        P(None, "dp", "seq", None),
        P(("dp", "seq"), None),
        P(("dp", "seq"), None),
        P(("dp", "seq"), None),
        P(None, ("dp", "seq")),
        P(("dp", "seq")),
        P(("dp", "seq")),
    )
    return jax.shard_map(
        body,
        mesh=mesh,
        in_specs=placed,
        out_specs=(
            P(None, "dp", "seq", None),
            P(None, "dp", "seq", None),
            P(("dp", "seq"), None),
            P(("dp", "seq"), None),
            P(("dp", "seq"), None),
            P(None, ("dp", "seq")),
            P(("dp", "seq")),
            P(("dp", "seq")),
        ),
        check_vma=False,
    )
```
